32 devices in a mesh: seq: 8 (over z, core), tp: 4 (over y, x).
Axes of the slice: x: 2, y: 2, z: 4, core: 2. Of those that a mesh axis runs over, the one named last changes fastest.
Arguments:
- layer_input: bfloat16 [6144, 2048], P(('seq', 'tp')), may hold values from -6 to 6
- cotangent: bfloat16 [6144, 2048], P(('seq', 'tp')), may hold values from -6 to 6
- query_key_value_weight: bfloat16 [3, 2048, 2048], P(None, 'seq', 'tp'), may hold values from -0.125 to 0.125
- output_weight: bfloat16 [2048, 2048], P('tp', 'seq'), may hold values from -0.125 to 0.125
- gate_up_weight: bfloat16 [2, 2048, 8192], P(None, 'seq', 'tp'), may hold values from -0.125 to 0.125
- down_weight: bfloat16 [8192, 2048], P('tp', 'seq'), may hold values from -0.0625 to 0.0625
- input_first_factor: bfloat16 [5, 2048, 128], P(None, 'seq'), may hold values from -0.125 to 0.125
- output_first_factor: bfloat16 [2048, 128], P('tp', 'seq'), may hold values from -0.125 to 0.125
- down_first_factor: bfloat16 [8192, 128], P('tp', 'seq'), may hold values from -0.0625 to 0.0625
- query_key_value_second: bfloat16 [3, 128, 2048], P(None, 'seq', 'tp'), may hold values from -0.375 to 0.375
- gate_up_second_factor: bfloat16 [2, 128, 8192], P(None, 'seq', 'tp'), may hold values from -0.375 to 0.375
- output_down_second_factor: bfloat16 [2, 128, 2048], P(None, 'seq'), may hold values from -0.375 to 0.375
- norm_gain_table: float32 [4, 2048], replicated, may hold values from 0.5 to 2
- sequence_adapter: int32 [3], replicated, may hold values from 0 to 7
- block_sequence: int32 [48], replicated, may hold values from 0 to 2, as said below
- block_position: int32 [48], replicated, may hold values from 0 to 15
Outputs:
- output: float32 [6144, 2048], P(('seq', 'tp'))
- input_grad: float32 [6144, 2048], P(('seq', 'tp'))
- grad_a_in: float32 [5, 2048, 128], P(None, 'seq')
- grad_a_o: float32 [2048, 128], P('tp', 'seq')
- grad_a_down: float32 [8192, 128], P('tp', 'seq')
- grad_b_qkv: float32 [3, 128, 2048], P(None, 'seq', 'tp')
- grad_b_gu: float32 [2, 128, 8192], P(None, 'seq', 'tp')
- grad_b_out: float32 [2, 128, 2048], P(None, 'seq')
The draws below stay inside these ranges and needn't reach their ends.
Inputs may be any that keep to these rules, and one draw needn't show every extreme that they name: block_sequence and block_position together name each of the 3 sequences' 8 + 8 places exactly once; places below 8 are the prompt's blocks in order, the others its continuations.
All inputs are finite; a program needn't handle non-finite values.
Results may differ from the reference program's by a relative error of at most 0.028.
Values may be sent and summed in bfloat16 or wider, within the bound.
No kernel may reach another device: no remote copies, remote signals or barrier semaphores. Data moves between devices by JAX's collectives and lax.ppermute only.
A program may use at most 256 MiB of HBM per device.

```python
import jax
import jax.numpy as jnp
from jax import lax

MODEL_DIMENSION = 2048
HEADS = 16
HEAD_DIM = 128
FEEDFORWARD_UNITS = 8192
ADAPTER_CHOICES = 8
ADAPTER_RANK = 16
BLK = 128
PROMPT_BLOCKS = 8
CONTS = 8
NBLK = 48
SEQS = 3
TOKENS = 6144


def layout_codes(key):
    return jax.random.permutation(jax.random.fold_in(key, 11), NBLK)


def draw_block_sequence(key, part):
    return (layout_codes(key) // (PROMPT_BLOCKS + CONTS)).astype(jnp.int32)


def draw_block_position(key, part):
    return (layout_codes(key) % (PROMPT_BLOCKS + CONTS)).astype(jnp.int32)


def block_levels(own_key, extent, shards, least, top_value):
    gain, own = 1.0, jax.random.fold_in(own_key, 6)
    for axis_at, blocks in shards:
        steps = jnp.exp(jax.random.uniform(jax.random.fold_in(own, axis_at), (blocks,), jnp.float32, least / len(shards), top_value / len(shards)))
        gain = gain * jnp.repeat(steps, extent[axis_at] // blocks).reshape([-1 if axis == axis_at else 1 for axis in range(len(extent))])
    return gain


def normal_values(rng, dims, scale, reach, pieces=(), kind=jnp.bfloat16):
    gain = block_levels(rng, dims, pieces, -0.22, 0.18) if pieces else 1.0
    array = jax.random.normal(rng, dims, jnp.float32) * scale * gain
    return jnp.minimum(jnp.maximum(array, -reach), reach).astype(kind)


def setup_inputs(seed: int = 0) -> dict:
    keys = jax.random.split(jax.random.key(seed), 17)
    layer_input = normal_values(keys[0], (TOKENS, MODEL_DIMENSION), 1.0, 6.0, ((0, 32),))
    cotangent = normal_values(keys[1], (TOKENS, MODEL_DIMENSION), 1.0, 6.0, ((0, 32),))
    query_key_value_weight = normal_values(keys[2], (3, MODEL_DIMENSION, MODEL_DIMENSION), MODEL_DIMENSION ** -0.5, 0.125, ((1, 8), (2, 4)))
    output_weight = normal_values(keys[3], (MODEL_DIMENSION, MODEL_DIMENSION), MODEL_DIMENSION ** -0.5, 0.125, ((0, 4), (1, 8)))
    gate_up_weight = normal_values(keys[4], (2, MODEL_DIMENSION, FEEDFORWARD_UNITS), MODEL_DIMENSION ** -0.5, 0.125, ((1, 8), (2, 4)))
    down_weight = normal_values(keys[5], (FEEDFORWARD_UNITS, MODEL_DIMENSION), FEEDFORWARD_UNITS ** -0.5, 0.0625, ((0, 4), (1, 8)))
    input_first_factor = normal_values(keys[6], (5, MODEL_DIMENSION, ADAPTER_CHOICES * ADAPTER_RANK), MODEL_DIMENSION ** -0.5, 0.125, ((1, 8),))
    output_first_factor = normal_values(keys[7], (MODEL_DIMENSION, ADAPTER_CHOICES * ADAPTER_RANK), MODEL_DIMENSION ** -0.5, 0.125, ((0, 4), (1, 8)))
    down_first_factor = normal_values(keys[8], (FEEDFORWARD_UNITS, ADAPTER_CHOICES * ADAPTER_RANK), FEEDFORWARD_UNITS ** -0.5, 0.0625, ((0, 4), (1, 8)))
    query_key_value_second = normal_values(keys[9], (3, ADAPTER_CHOICES * ADAPTER_RANK, MODEL_DIMENSION), (16 * ADAPTER_RANK) ** -0.5, 0.375, ((1, 8), (2, 4)))
    gate_up_second_factor = normal_values(keys[10], (2, ADAPTER_CHOICES * ADAPTER_RANK, FEEDFORWARD_UNITS), (16 * ADAPTER_RANK) ** -0.5, 0.375, ((1, 8), (2, 4)))
    output_down_second_factor = normal_values(keys[11], (2, ADAPTER_CHOICES * ADAPTER_RANK, MODEL_DIMENSION), (16 * ADAPTER_RANK) ** -0.5, 0.375, ((1, 8),))
    norm_gain_table = jnp.clip(jax.random.uniform(keys[12], (4, MODEL_DIMENSION), jnp.float32, 0.5, 2.0), 0.5, 2.0)
    sequence_adapter = jax.random.randint(keys[13], (SEQS,), 0, ADAPTER_CHOICES).astype(jnp.int32)
    block_sequence = draw_block_sequence(jax.random.fold_in(keys[16], 71), 0)
    block_position = draw_block_position(jax.random.fold_in(keys[16], 71), 0)
    return {"layer_input": layer_input, "cotangent": cotangent, "query_key_value_weight": query_key_value_weight, "output_weight": output_weight, "gate_up_weight": gate_up_weight, "down_weight": down_weight, "input_first_factor": input_first_factor, "output_first_factor": output_first_factor, "down_first_factor": down_first_factor, "query_key_value_second": query_key_value_second, "gate_up_second_factor": gate_up_second_factor, "output_down_second_factor": output_down_second_factor, "norm_gain_table": norm_gain_table, "sequence_adapter": sequence_adapter, "block_sequence": block_sequence, "block_position": block_position}


EPS = 1e-06
THETA = 500000.0
adapter_scale = 2.0
NEG = -1e+30
HIGH = lax.Precision.HIGHEST

@jax.custom_vjp
def low(v):
    return lax.optimization_barrier(v.astype(jnp.bfloat16)).astype(jnp.float32)

@jax.custom_vjp
def lowrank_pullback(v):
    return v

def low_keep(v):
    return (low(v), None)

def low_pass(kept, grad):
    return (grad,)

def back_keep(v):
    return (v, None)

def back_low(kept, grad):
    return (low(grad),)
low.defvjp(low_keep, low_pass)
lowrank_pullback.defvjp(back_keep, back_low)

def widened_rows(tensor):
    return tensor.astype(jnp.float32)

def precise_product(left, right):
    return jnp.dot(left, right, precision=HIGH, preferred_element_type=jnp.float32)

def rms_norm(values_in, gain_row):
    return values_in * lax.rsqrt(lax.optimization_barrier(jnp.mean(values_in * values_in, axis=-1, keepdims=True)) + EPS) * gain_row

def rotary(vals_in, cosine, sine_table):
    half_dim = vals_in.shape[-1] // 2
    first_half = vals_in[..., :half_dim]
    second_half = vals_in[..., half_dim:]
    return jnp.concatenate([first_half * cosine - second_half * sine_table, second_half * cosine + first_half * sine_table], axis=-1)

def adapter_addend(source_rows, adapter_first, adapter_second, adapter_selector):
    return adapter_scale * precise_product(precise_product(source_rows, adapter_first) * adapter_selector, adapter_second)

def attend(seq_queries, seq_keys, seq_values):
    length = seq_queries.shape[0]
    block_of = jnp.arange(length, dtype=jnp.int32) // BLK
    token_of = jnp.arange(length, dtype=jnp.int32) % BLK
    prompt_seen = (block_of[None, :] < PROMPT_BLOCKS) & (block_of[None, :] < block_of[:, None])
    own_block = (block_of[None, :] == block_of[:, None]) & (token_of[None, :] <= token_of[:, None])
    visible = prompt_seen | own_block
    scores = jnp.einsum('qhd,khd->hqk', seq_queries, seq_keys, precision=HIGH) * HEAD_DIM ** (-0.5)
    scores = jnp.where(visible[None], lowrank_pullback(scores), NEG)
    probs_tile = low(jax.nn.softmax(scores, axis=-1))
    return jnp.einsum('hqk,khd->qhd', probs_tile, seq_values, precision=HIGH)

def forward(input_rows, adapter_table, frozen, layout):
    input_first_factor, output_first_factor, down_first_factor, query_key_value_second, gate_up_second_factor, output_down_second_factor = adapter_table
    query_key_value_weight, output_weight, gate_up_weight, down_weight, norm_gain_table = frozen
    adapter_selector, cosine, sine_table, seq_order, inverse = layout
    tokens = input_rows.shape[0]
    head_shape = (tokens, HEADS, HEAD_DIM)
    normed_query = lowrank_pullback(precise_product(input_rows, query_key_value_weight[0]) + adapter_addend(input_rows, input_first_factor[0], query_key_value_second[0], adapter_selector))
    normed_key = lowrank_pullback(precise_product(input_rows, query_key_value_weight[1]) + adapter_addend(input_rows, input_first_factor[1], query_key_value_second[1], adapter_selector))
    projected_value = precise_product(input_rows, query_key_value_weight[2]) + adapter_addend(input_rows, input_first_factor[2], query_key_value_second[2], adapter_selector)
    queries = low(lowrank_pullback(rotary(rms_norm(normed_query, norm_gain_table[0]).reshape(head_shape), cosine, sine_table)))
    key_rows = low(lowrank_pullback(rotary(rms_norm(normed_key, norm_gain_table[1]).reshape(head_shape), cosine, sine_table)))
    value_rows = low(lowrank_pullback(projected_value)).reshape(head_shape)
    block_shape = (NBLK, BLK, HEADS, HEAD_DIM)
    seq_shape = (SEQS, (PROMPT_BLOCKS + CONTS) * BLK, HEADS, HEAD_DIM)
    arranged = tuple((tensor.reshape(block_shape)[seq_order].reshape(seq_shape) for tensor in (queries, key_rows, value_rows)))

    def per_seq(running, packed):
        return (running, jax.checkpoint(attend)(packed[0], packed[1], packed[2]))
    unused_carry, attended = lax.scan(per_seq, jnp.zeros((), jnp.float32), arranged)
    attended = attended.reshape(block_shape)[inverse].reshape(tokens, HEADS * HEAD_DIM)
    head_outputs = low(lowrank_pullback(attended))
    attention_output = lowrank_pullback(precise_product(head_outputs, output_weight) + adapter_addend(head_outputs, output_first_factor, output_down_second_factor[0], adapter_selector))
    hidden = input_rows + rms_norm(attention_output, norm_gain_table[2])
    hidden_lowrank = low(hidden)
    gate_activation = lowrank_pullback(precise_product(hidden_lowrank, gate_up_weight[0]) + adapter_addend(hidden_lowrank, input_first_factor[3], gate_up_second_factor[0], adapter_selector))
    up_activation = lowrank_pullback(precise_product(hidden_lowrank, gate_up_weight[1]) + adapter_addend(hidden_lowrank, input_first_factor[4], gate_up_second_factor[1], adapter_selector))
    gated_activation = low(jax.nn.silu(gate_activation) * up_activation)
    feedforward_output = lowrank_pullback(precise_product(gated_activation, down_weight) + adapter_addend(gated_activation, down_first_factor, output_down_second_factor[1], adapter_selector))
    return hidden + rms_norm(feedforward_output, norm_gain_table[3])

def reference(layer_input, cotangent, query_key_value_weight, output_weight, gate_up_weight, down_weight, input_first_factor, output_first_factor, down_first_factor, query_key_value_second, gate_up_second_factor, output_down_second_factor, norm_gain_table, sequence_adapter, block_sequence, block_position):
    adapter_slots = input_first_factor.shape[2]
    row_seq = jnp.repeat(block_sequence, BLK)
    row_pos = jnp.repeat(block_position, BLK)
    row_token = jnp.tile(jnp.arange(BLK, dtype=jnp.int32), NBLK)
    row_adapter = sequence_adapter[row_seq]
    adapter_selector = (jnp.arange(adapter_slots, dtype=jnp.int32)[None, :] // ADAPTER_RANK == row_adapter[:, None]).astype(jnp.float32)
    position = jnp.where(row_pos < PROMPT_BLOCKS, row_pos * BLK, PROMPT_BLOCKS * BLK) + row_token
    frequency = THETA ** (-(jnp.arange(HEAD_DIM // 2, dtype=jnp.float32) * 2.0) / HEAD_DIM)
    angles = position.astype(jnp.float32)[:, None] * frequency[None, :]
    cosine = jnp.cos(angles)[:, None, :]
    sine_table = jnp.sin(angles)[:, None, :]
    seq_order = jnp.argsort(block_sequence * (PROMPT_BLOCKS + CONTS) + block_position).astype(jnp.int32)
    inverse = jnp.argsort(seq_order).astype(jnp.int32)
    layout = (adapter_selector, cosine, sine_table, seq_order, inverse)
    frozen = (widened_rows(query_key_value_weight), widened_rows(output_weight), widened_rows(gate_up_weight), widened_rows(down_weight), widened_rows(norm_gain_table))
    adapter_table = (widened_rows(input_first_factor), widened_rows(output_first_factor), widened_rows(down_first_factor), widened_rows(query_key_value_second), widened_rows(gate_up_second_factor), widened_rows(output_down_second_factor))

    def layer(input_rows, adapter_set):
        return forward(input_rows, adapter_set, frozen, layout)
    output, pull_back = jax.vjp(layer, widened_rows(layer_input), adapter_table)
    input_grad, adapter_grads = pull_back(widened_rows(cotangent))
    return (output, input_grad, adapter_grads[0], adapter_grads[1], adapter_grads[2], adapter_grads[3], adapter_grads[4], adapter_grads[5])
```

```python
import functools

import jax
import jax.numpy as jnp
from jax import lax
from jax.experimental import pallas as pl
from jax.experimental.pallas import tpu as pltpu
from jax.sharding import PartitionSpec as P

HEAD_DIM = 128
ADAPTER_RANK = 16
BLK = 128
PROMPT_BLOCKS = 8
EPS = 1e-06
THETA = 500000.0
NEG = -1e30
LOG2E = 1.4426950408889634
F32 = jnp.float32
BF16 = jnp.bfloat16


def mm(a, b):
    return jnp.dot(a, b, preferred_element_type=F32)


def mm_nt(a, b):
    return lax.dot_general(a, b, (((1,), (1,)), ((), ())), preferred_element_type=F32)


def mm_tn(a, b):
    return lax.dot_general(a, b, (((0,), (0,)), ((), ())), preferred_element_type=F32)


def bits_of(count):
    n = count.bit_length() - 1
    assert 1 << n == count
    return n


def flip(value, axis, count, bit):
    return lax.ppermute(value, axis, [(i, i ^ (1 << bit)) for i in range(count)])


def gather_order(value, axis, count, order):
    rank = lax.axis_index(axis)
    have = []
    current = value
    for bit in order:
        other = flip(current, axis, count, bit)
        mine_low = ((rank >> bit) & 1) == 0
        at = len([b for b in have if b > bit])
        low = jnp.where(mine_low, current, other)
        high = jnp.where(mine_low, other, current)
        current = jnp.stack([low, high], axis=at)
        have = sorted(have + [bit], reverse=True)
    return current.reshape((count,) + value.shape)


def gather_rows(value, axis, count):
    order = list(range(bits_of(count)))
    half = value.shape[0] // 2
    first = gather_order(value[:half], axis, count, order)
    second = gather_order(value[half:], axis, count, order[::-1])
    return jnp.concatenate([first, second], axis=1).reshape(-1, value.shape[1])


def scatter_order(value, axis, count, order):
    n = bits_of(count)
    rank = lax.axis_index(axis)
    current = value.reshape((2,) * n + value.shape[1:])
    have = list(range(n - 1, -1, -1))
    for bit in order:
        at = have.index(bit)
        mine = (rank >> bit) & 1
        keep = lax.dynamic_index_in_dim(current, mine, at, keepdims=False)
        give = lax.dynamic_index_in_dim(current, 1 - mine, at, keepdims=False)
        got = flip(give.astype(BF16), axis, count, bit)
        current = keep.astype(F32) + got.astype(F32)
        have.remove(bit)
    return current


def scatter_rows(value, axis, count):
    order = list(range(bits_of(count)))
    rows, width = value.shape
    blocks = value.reshape(count, rows // count, width)
    half = rows // count // 2
    first = scatter_order(blocks[:, :half], axis, count, order[::-1])
    second = scatter_order(blocks[:, half:], axis, count, order)
    return jnp.concatenate([first, second], axis=0)


def sum_all(value, axis, count):
    for bit in range(bits_of(count)):
        value = value + flip(value, axis, count, bit)
    return value


def fill(sources, sem):
    copies = [pltpu.make_async_copy(src, dst, sem.at[i]) for i, (src, dst) in enumerate(sources)]
    for copy in copies:
        copy.start()
    for copy in copies:
        copy.wait()


def gather_prompt(prompt_at, source, target, count):
    def step(i, carry):
        start = pl.multiple_of(prompt_at[i] * BLK, BLK)
        target[pl.ds(pl.multiple_of(i * BLK, BLK), BLK), :] = source[pl.ds(start, BLK), :]
        return carry

    lax.fori_loop(0, count, step, 0)


def masked_scores(keys, own_keys, queries, place, scale):
    prompt = mm_nt(keys, queries) * scale
    block = lax.broadcasted_iota(jnp.int32, prompt.shape, 0) // BLK
    prompt = jnp.where(block < place, prompt, NEG)
    own = mm_nt(own_keys, queries) * scale
    causal = lax.broadcasted_iota(jnp.int32, own.shape, 0) <= lax.broadcasted_iota(
        jnp.int32, own.shape, 1
    )
    own = jnp.where(causal, own, NEG)
    top = jnp.maximum(jnp.max(prompt, axis=0, keepdims=True), jnp.max(own, axis=0, keepdims=True))
    prompt = jnp.exp2(prompt - top)
    own = jnp.exp2(own - top)
    total = jnp.sum(prompt, axis=0, keepdims=True) + jnp.sum(own, axis=0, keepdims=True)
    return prompt, own, 1.0 / total


def attend_kernel(
    slots, group, rows, prompt_count, q_seq, q_place, prompt_at, *refs
):
    near = refs[:slots]
    far = refs[slots : slots * group]
    out = refs[slots * group]
    q_buf, k_buf, v_buf, kp, vp, sem = refs[slots * group + 1 :]
    plan = []
    for i, ref in enumerate(near):
        at = pl.ds(i * rows, rows)
        plan += [(ref.at[0], q_buf.at[at]), (ref.at[1], k_buf.at[at]), (ref.at[2], v_buf.at[at])]
    for i, ref in enumerate(far):
        at = pl.ds((slots + i) * rows, rows)
        plan += [(ref.at[0], k_buf.at[at]), (ref.at[1], v_buf.at[at])]
    fill(plan, sem)
    gather_prompt(prompt_at, k_buf, kp, prompt_count)
    gather_prompt(prompt_at, v_buf, vp, prompt_count)
    scale = HEAD_DIM ** (-0.5) * LOG2E
    span = PROMPT_BLOCKS * BLK

    def step(i, carry):
        at = pl.ds(pl.multiple_of(i * BLK, BLK), BLK)
        of_seq = pl.ds(pl.multiple_of(q_seq[i] * span, span), span)
        prompt, own, inverse = masked_scores(
            kp[of_seq, :], k_buf[at, :], q_buf[at, :], q_place[i], scale
        )
        result = mm_tn(vp[of_seq, :], prompt.astype(BF16)) + mm_tn(v_buf[at, :], own.astype(BF16))
        out[at, :] = (result * inverse).T.astype(BF16)
        return carry

    lax.fori_loop(0, slots * rows // BLK, step, 0)


def attend_back_kernel(
    slots, group, rows, prompt_count, q_seq, q_place, prompt_at, *refs
):
    near = refs[:slots]
    far = refs[slots : slots * group]
    grads = refs[slots * group : slots * group + slots]
    dq_out, dk_out, dv_out = refs[slots * group + slots : slots * group + slots + 3]
    q_buf, k_buf, v_buf, do_buf, kp, vp, dkp, dvp, sem = refs[slots * group + slots + 3 :]
    plan = []
    for i, ref in enumerate(near):
        at = pl.ds(i * rows, rows)
        plan += [(ref.at[0], q_buf.at[at]), (ref.at[1], k_buf.at[at]), (ref.at[2], v_buf.at[at])]
    for i, ref in enumerate(far):
        at = pl.ds((slots + i) * rows, rows)
        plan += [(ref.at[0], k_buf.at[at]), (ref.at[1], v_buf.at[at])]
    for i, ref in enumerate(grads):
        plan += [(ref, do_buf.at[pl.ds(i * rows, rows)])]
    fill(plan, sem)
    gather_prompt(prompt_at, k_buf, kp, prompt_count)
    gather_prompt(prompt_at, v_buf, vp, prompt_count)
    dkp[...] = jnp.zeros_like(dkp)
    dvp[...] = jnp.zeros_like(dvp)
    scale = HEAD_DIM ** (-0.5)
    span = PROMPT_BLOCKS * BLK
    own_rows = slots * rows
    zeros = jnp.zeros((BLK, HEAD_DIM), BF16)

    def clear(i, carry):
        at = pl.ds(pl.multiple_of(own_rows + i * BLK, BLK), BLK)
        dk_out[at, :] = zeros
        dv_out[at, :] = zeros
        return carry

    lax.fori_loop(0, (group - 1) * own_rows // BLK, clear, 0)

    def step(i, carry):
        at = pl.ds(pl.multiple_of(i * BLK, BLK), BLK)
        seq, place = q_seq[i], q_place[i]
        of_seq = pl.ds(pl.multiple_of(seq * span, span), span)
        queries, grad = q_buf[at, :], do_buf[at, :]
        prompt, own, inverse = masked_scores(
            kp[of_seq, :], k_buf[at, :], queries, place, scale * LOG2E
        )
        prompt, own = prompt * inverse, own * inverse
        d_prompt = mm_nt(vp[of_seq, :], grad)
        d_own = mm_nt(v_buf[at, :], grad)
        delta = jnp.sum(prompt * d_prompt, axis=0, keepdims=True) + jnp.sum(
            own * d_own, axis=0, keepdims=True
        )
        ds_prompt = (prompt * (d_prompt - delta)).astype(BF16)
        ds_own = (own * (d_own - delta)).astype(BF16)
        dq = mm_tn(ds_prompt, kp[of_seq, :]) + mm_tn(ds_own, k_buf[at, :])
        dq_out[at, :] = (dq * scale).astype(BF16)
        dvp[of_seq, :] += mm(prompt.astype(BF16), grad)
        dkp[of_seq, :] += mm(ds_prompt, queries) * scale
        dk_out[at, :] = (mm(ds_own, queries) * scale).astype(BF16)
        dv_out[at, :] = mm(own.astype(BF16), grad).astype(BF16)
        return carry

    lax.fori_loop(0, own_rows // BLK, step, 0)

    def spread(i, carry):
        to = pl.ds(pl.multiple_of(prompt_at[i] * BLK, BLK), BLK)
        at = pl.ds(pl.multiple_of(i * BLK, BLK), BLK)
        dk_out[to, :] = (dk_out[to, :].astype(F32) + dkp[at, :]).astype(BF16)
        dv_out[to, :] = (dv_out[to, :].astype(F32) + dvp[at, :]).astype(BF16)
        return carry

    lax.fori_loop(0, prompt_count, spread, 0)


ANY = pl.BlockSpec(memory_space=pl.ANY)
WHOLE = pl.BlockSpec(memory_space=pltpu.VMEM)


def attend(tables, near, far, rows, prompt_count):
    slots = len(near)
    group = 1 + len(far) // slots
    own, every = slots * rows, slots * group * rows
    pairs = own * (PROMPT_BLOCKS + 1) * BLK
    return pl.pallas_call(
        functools.partial(attend_kernel, slots, group, rows, prompt_count),
        out_shape=jax.ShapeDtypeStruct((own, HEAD_DIM), BF16),
        grid_spec=pltpu.PrefetchScalarGridSpec(
            num_scalar_prefetch=3,
            in_specs=[ANY] * (slots * group),
            out_specs=WHOLE,
            scratch_shapes=[
                pltpu.VMEM((own, HEAD_DIM), BF16),
                pltpu.VMEM((every, HEAD_DIM), BF16),
                pltpu.VMEM((every, HEAD_DIM), BF16),
                pltpu.VMEM((prompt_count * BLK, HEAD_DIM), BF16),
                pltpu.VMEM((prompt_count * BLK, HEAD_DIM), BF16),
                pltpu.SemaphoreType.DMA((3 * slots + 2 * slots * (group - 1),)),
            ],
        ),
        cost_estimate=pl.CostEstimate(
            flops=4 * pairs * HEAD_DIM, bytes_accessed=6 * every * HEAD_DIM, transcendentals=pairs
        ),
        name="attend",
    )(*tables, *near, *far)


def attend_back(tables, near, far, grads, rows, prompt_count):
    slots = len(near)
    group = 1 + len(far) // slots
    own, every = slots * rows, slots * group * rows
    pairs = own * (PROMPT_BLOCKS + 1) * BLK
    return pl.pallas_call(
        functools.partial(attend_back_kernel, slots, group, rows, prompt_count),
        out_shape=[
            jax.ShapeDtypeStruct((own, HEAD_DIM), BF16),
            jax.ShapeDtypeStruct((every, HEAD_DIM), BF16),
            jax.ShapeDtypeStruct((every, HEAD_DIM), BF16),
        ],
        grid_spec=pltpu.PrefetchScalarGridSpec(
            num_scalar_prefetch=3,
            in_specs=[ANY] * (slots * group + slots),
            out_specs=[WHOLE] * 3,
            scratch_shapes=[
                pltpu.VMEM((own, HEAD_DIM), BF16),
                pltpu.VMEM((every, HEAD_DIM), BF16),
                pltpu.VMEM((every, HEAD_DIM), BF16),
                pltpu.VMEM((own, HEAD_DIM), BF16),
                pltpu.VMEM((prompt_count * BLK, HEAD_DIM), BF16),
                pltpu.VMEM((prompt_count * BLK, HEAD_DIM), BF16),
                pltpu.VMEM((prompt_count * BLK, HEAD_DIM), F32),
                pltpu.VMEM((prompt_count * BLK, HEAD_DIM), F32),
                pltpu.SemaphoreType.DMA((4 * slots + 2 * slots * (group - 1),)),
            ],
        ),
        cost_estimate=pl.CostEstimate(
            flops=10 * pairs * HEAD_DIM, bytes_accessed=12 * every * HEAD_DIM, transcendentals=pairs
        ),
        name="attend_back",
    )(*tables, *near, *far, *grads)


def rotate(values, cosine, sine):
    half = HEAD_DIM // 2
    first, second = values[..., :half], values[..., half:]
    return jnp.concatenate(
        [first * cosine - second * sine, second * cosine + first * sine], axis=-1
    )


def local(
    layer_input,
    cotangent,
    query_key_value_weight,
    output_weight,
    gate_up_weight,
    down_weight,
    input_first_factor,
    output_first_factor,
    down_first_factor,
    query_key_value_second,
    gate_up_second_factor,
    output_down_second_factor,
    norm_gain_table,
    sequence_adapter,
    block_sequence,
    block_position,
):
    tp, tp_rank = lax.axis_size("tp"), lax.axis_index("tp")
    seqs, seq_rank = lax.axis_size("seq"), lax.axis_index("seq")
    own_rows, width = layer_input.shape
    rows = own_rows * tp
    my_blocks = rows // BLK
    cols = query_key_value_weight.shape[2]
    heads = cols // HEAD_DIM
    hidden_cols = gate_up_weight.shape[2]
    k_rows = query_key_value_weight.shape[1]
    slots_a = input_first_factor.shape[2]
    rank_cols = output_first_factor.shape[1]
    group = seqs // heads
    head_rank, group_rank = seq_rank // group, seq_rank % group
    n_seq = sequence_adapter.shape[0]

    gather = lambda value: lax.all_gather(value, "seq", axis=0, tiled=True)
    w_qkv = gather(query_key_value_weight.transpose(1, 0, 2).reshape(k_rows, 3 * cols))
    a_part = k_rows // tp
    b_part = width // tp
    a_mine = lax.dynamic_slice_in_dim(input_first_factor, tp_rank * a_part, a_part, 1)
    b_mine = lax.dynamic_slice_in_dim(output_down_second_factor, tp_rank * b_part, b_part, 2)
    pieces = [
        a_mine,
        b_mine,
        query_key_value_second,
        output_first_factor,
        down_first_factor,
        gate_up_second_factor,
    ]
    packed = jnp.concatenate([piece.reshape(-1, 128) for piece in pieces], axis=0)
    packed = lax.all_gather(packed, "seq", axis=0)
    split, at = [], 0
    for piece in pieces:
        size = piece.size // 128
        split.append(packed[:, at : at + size])
        at += size
    w_o = gather(output_weight.T)
    w_gu = gather(gate_up_weight.transpose(1, 0, 2).reshape(k_rows, 2 * hidden_cols))
    w_down = gather(down_weight.T)

    shared = jnp.concatenate(split[:2], axis=1)
    shared = gather_order(shared, "tp", tp, list(range(bits_of(tp))))
    a_size = a_mine.size // 128
    a_in = (
        shared[:, :, :a_size]
        .reshape(tp, seqs, 5, a_part, slots_a)
        .transpose(2, 1, 0, 3, 4)
        .reshape(5, width, slots_a)
    )
    b_od = (
        shared[:, :, a_size:]
        .reshape(tp, seqs, 2, rank_cols, b_part)
        .transpose(2, 1, 3, 0, 4)
        .reshape(2, slots_a, width)
    )
    b_qkv = split[2].reshape(seqs, 3, rank_cols, cols).transpose(1, 0, 2, 3).reshape(3, slots_a, cols)
    a_o = split[3].reshape(seqs, cols, rank_cols).transpose(1, 0, 2).reshape(cols, slots_a)
    a_down = (
        split[4].reshape(seqs, hidden_cols, rank_cols).transpose(1, 0, 2).reshape(hidden_cols, slots_a)
    )
    b_gu = (
        split[5]
        .reshape(seqs, 2, rank_cols, hidden_cols)
        .transpose(1, 0, 2, 3)
        .reshape(2, slots_a, hidden_cols)
    )

    block_ids = seq_rank * my_blocks + jnp.arange(my_blocks, dtype=jnp.int32)
    block_of_row = jnp.arange(rows, dtype=jnp.int32) // BLK
    offset = jnp.arange(rows, dtype=jnp.int32) % BLK
    seq_blocks = block_sequence[block_ids]
    place_blocks = block_position[block_ids]
    adapter_blocks = sequence_adapter[seq_blocks]
    pick = lambda per_block: jnp.repeat(per_block, BLK)
    adapter_rows = pick(adapter_blocks)
    place_rows = pick(place_blocks)
    select = (
        jnp.arange(slots_a, dtype=jnp.int32)[None, :] // ADAPTER_RANK == adapter_rows[:, None]
    ).astype(F32) * 2.0
    position = (
        jnp.where(place_rows < PROMPT_BLOCKS, place_rows * BLK, PROMPT_BLOCKS * BLK) + offset
    )
    frequency = THETA ** (-(jnp.arange(HEAD_DIM // 2, dtype=F32) * 2.0) / HEAD_DIM)
    angles = position.astype(F32)[:, None] * frequency[None, :]
    cosine = jnp.cos(angles)[:, None, :]
    sine = jnp.sin(angles)[:, None, :]

    owner = (
        ((head_rank - jnp.arange(heads)) % heads)[None, :] * group
        + ((group_rank + jnp.arange(group)) % group)[:, None]
    ).reshape(-1)
    held = (owner[:, None] * my_blocks + jnp.arange(my_blocks)[None, :]).reshape(-1)
    held_seq = block_sequence[held].astype(jnp.int32)
    held_place = block_position[held].astype(jnp.int32)
    prompt_count = n_seq * PROMPT_BLOCKS
    wanted = jnp.arange(prompt_count, dtype=jnp.int32)
    code = jnp.where(held_place < PROMPT_BLOCKS, held_seq * PROMPT_BLOCKS + held_place, -1)
    prompt_at = jnp.sum(
        jnp.where(
            code[None, :] == wanted[:, None], jnp.arange(held.shape[0], dtype=jnp.int32)[None, :], 0
        ),
        axis=1,
    ).astype(jnp.int32)
    own_blocks = heads * my_blocks
    tables = (held_seq[:own_blocks], held_place[:own_blocks], prompt_at)

    def head_shift(value, by):
        return lax.ppermute(
            value,
            "seq",
            [
                (h * group + j, ((h + by) % heads) * group + j)
                for h in range(heads)
                for j in range(group)
            ],
        )

    def group_shift(value, by):
        return lax.ppermute(
            value,
            "seq",
            [
                (h * group + j, h * group + (j + by) % group)
                for h in range(heads)
                for j in range(group)
            ],
        )

    def to_heads(value):
        out = []
        for k in range(heads):
            piece = lax.dynamic_index_in_dim(value, (head_rank + k) % heads, 0, keepdims=False)
            out.append(piece if k == 0 else head_shift(piece, k))
        return out

    def from_heads(parts):
        back = [part if k == 0 else head_shift(part, -k) for k, part in enumerate(parts)]
        twice = jnp.stack(back + back)
        return lax.dynamic_slice_in_dim(twice, (-head_rank) % heads, heads, 0)

    x = gather_rows(layer_input, "tp", tp)
    latents = []
    projected = mm(x, w_qkv)
    for i in range(3):
        latents.append((mm(x, a_in[i]) * select).astype(BF16))
    z_q, z_k, z_v = [
        projected[:, i * cols : (i + 1) * cols] + mm(latents[i], b_qkv[i]) for i in range(3)
    ]
    gain_q = lax.dynamic_slice_in_dim(norm_gain_table[0], tp_rank * cols, cols)
    gain_k = lax.dynamic_slice_in_dim(norm_gain_table[1], tp_rank * cols, cols)
    squares = jnp.stack([jnp.sum(z_q * z_q, axis=1), jnp.sum(z_k * z_k, axis=1)])
    squares = sum_all(squares, "tp", tp)
    inv_q, inv_k = lax.rsqrt(squares / width + EPS)[:, :, None]
    shape3 = (rows, heads, HEAD_DIM)
    queries = rotate((z_q * inv_q * gain_q).reshape(shape3), cosine, sine).astype(BF16)
    keys = rotate((z_k * inv_k * gain_k).reshape(shape3), cosine, sine).astype(BF16)
    values = z_v.astype(BF16).reshape(shape3)
    qkv = jnp.stack([queries, keys, values]).transpose(2, 0, 1, 3)
    near = to_heads(qkv)
    far = []
    for j in range(1, group):
        far += [group_shift(part[1:], -j) for part in near]
    attended = attend(tables, near, far, rows, prompt_count)
    heads_out = (
        from_heads([attended[k * rows : (k + 1) * rows] for k in range(heads)])
        .transpose(1, 0, 2)
        .reshape(rows, cols)
    )

    o_latent = (mm(heads_out, a_o) * select).astype(BF16)
    partial = mm_nt(heads_out, w_o) + mm(o_latent, b_od[0])
    attn_out = scatter_rows(partial.astype(BF16), "tp", tp)
    x_own = layer_input.astype(F32)
    d_y = cotangent.astype(F32)
    scale_o = lax.rsqrt(jnp.mean(attn_out * attn_out, axis=1, keepdims=True) + EPS)
    hidden = x_own + attn_out * scale_o * norm_gain_table[2]
    h_low = gather_rows(hidden.astype(BF16), "tp", tp)

    g_latent = (mm(h_low, a_in[3]) * select).astype(BF16)
    u_latent = (mm(h_low, a_in[4]) * select).astype(BF16)
    gate = mm(h_low, w_gu[:, :hidden_cols]) + mm(g_latent, b_gu[0])
    up = mm(h_low, w_gu[:, hidden_cols:]) + mm(u_latent, b_gu[1])
    sigmoid = jax.nn.sigmoid(gate)
    silu = gate * sigmoid
    act = (silu * up).astype(BF16)
    d_latent = (mm(act, a_down) * select).astype(BF16)
    partial = mm_nt(act, w_down) + mm(d_latent, b_od[1])
    ff_out = scatter_rows(partial.astype(BF16), "tp", tp)
    scale_f = lax.rsqrt(jnp.mean(ff_out * ff_out, axis=1, keepdims=True) + EPS)
    output = hidden + ff_out * scale_f * norm_gain_table[3]

    def norm_back(values_in, inv, scaled):
        return inv * scaled - values_in * inv**3 * jnp.mean(scaled * values_in, axis=1, keepdims=True)

    d_ff = norm_back(ff_out, scale_f, d_y * norm_gain_table[3]).astype(BF16)
    d_ff = gather_rows(d_ff, "tp", tp)
    u_down = (mm_nt(d_ff, b_od[1]) * select).astype(BF16)
    d_act = mm(d_ff, w_down) + mm_nt(u_down, a_down)
    grad_a_down = mm_tn(act, u_down)
    grad_b_down = mm_tn(d_latent, d_ff)
    d_silu = sigmoid * (1.0 + gate * (1.0 - sigmoid))
    d_gate = (d_act * up * d_silu).astype(BF16)
    d_up = (d_act * silu).astype(BF16)
    u_gate = (mm_nt(d_gate, b_gu[0]) * select).astype(BF16)
    u_up = (mm_nt(d_up, b_gu[1]) * select).astype(BF16)
    partial = (
        mm_nt(d_gate, w_gu[:, :hidden_cols])
        + mm_nt(d_up, w_gu[:, hidden_cols:])
        + mm_nt(u_gate, a_in[3])
        + mm_nt(u_up, a_in[4])
    )
    d_hidden = d_y + scatter_rows(partial.astype(BF16), "tp", tp)
    grad_a_gate = mm_tn(h_low, u_gate)
    grad_a_up = mm_tn(h_low, u_up)
    grad_b_gate = mm_tn(g_latent, d_gate)
    grad_b_up = mm_tn(u_latent, d_up)

    d_attn = norm_back(attn_out, scale_o, d_hidden * norm_gain_table[2]).astype(BF16)
    d_attn = gather_rows(d_attn, "tp", tp)
    u_o = (mm_nt(d_attn, b_od[0]) * select).astype(BF16)
    d_heads = (mm(d_attn, w_o) + mm_nt(u_o, a_o)).astype(BF16)
    grad_a_o = mm_tn(heads_out, u_o)
    grad_b_o = mm_tn(o_latent, d_attn)
    grads = to_heads(d_heads.reshape(shape3).transpose(1, 0, 2))
    dq, dk, dv = attend_back(tables, near, far, grads, rows, prompt_count)
    kv_rows = heads * rows
    d_kv = jnp.stack([dk, dv]).reshape(2, group, kv_rows, HEAD_DIM)
    total = d_kv[:, 0].astype(F32)
    for j in range(1, group):
        total = total + group_shift(d_kv[:, j], j).astype(F32)
    d_qkv = jnp.concatenate([dq[None], total.astype(BF16)], axis=0)
    d_qkv = from_heads([d_qkv[:, k * rows : (k + 1) * rows] for k in range(heads)])
    d_qkv = d_qkv.transpose(1, 2, 0, 3)
    d_query, d_key = d_qkv[0].astype(F32), d_qkv[1].astype(F32)
    dz_v = d_qkv[2].reshape(rows, cols)
    scaled_q = rotate(d_query, cosine, -sine).reshape(rows, cols) * gain_q
    scaled_k = rotate(d_key, cosine, -sine).reshape(rows, cols) * gain_k
    parts = jnp.stack([jnp.sum(scaled_q * z_q, axis=1), jnp.sum(scaled_k * z_k, axis=1)])
    parts = sum_all(parts, "tp", tp) / width
    dz_q = (inv_q * scaled_q - z_q * inv_q**3 * parts[0][:, None]).astype(BF16)
    dz_k = (inv_k * scaled_k - z_k * inv_k**3 * parts[1][:, None]).astype(BF16)
    dz = [dz_q, dz_k, dz_v]
    us = [(mm_nt(dz[i], b_qkv[i]) * select).astype(BF16) for i in range(3)]
    partial = sum(mm_nt(dz[i], w_qkv[:, i * cols : (i + 1) * cols]) + mm_nt(us[i], a_in[i]) for i in range(3))
    input_grad = d_hidden + scatter_rows(partial.astype(BF16), "tp", tp)

    grad_a_in = jnp.stack([mm_tn(x, u) for u in us] + [grad_a_gate, grad_a_up])
    grad_b_qkv = jnp.stack([mm_tn(latents[i], dz[i]) for i in range(3)])
    grad_b_gu = jnp.stack([grad_b_gate, grad_b_up])
    grad_b_out = jnp.stack([grad_b_o, grad_b_down])

    def reduce_seq(value, dim):
        return lax.psum_scatter(
            value.astype(BF16), "seq", scatter_dimension=dim, tiled=True
        ).astype(F32)

    grad_a_in = reduce_seq(grad_a_in, 1)
    grad_a_o = reduce_seq(grad_a_o, 1)
    grad_a_down = reduce_seq(grad_a_down, 1)
    grad_b_qkv = reduce_seq(grad_b_qkv, 1)
    grad_b_gu = reduce_seq(grad_b_gu, 1)
    grad_b_out = reduce_seq(grad_b_out, 1)
    grad_a_in, grad_b_out = (
        lax.psum(grad_a_in.astype(BF16), "tp").astype(F32),
        lax.psum(grad_b_out.astype(BF16), "tp").astype(F32),
    )
    return (output, input_grad, grad_a_in, grad_a_o, grad_a_down, grad_b_qkv, grad_b_gu, grad_b_out)


def solution(mesh):
    return jax.shard_map(
        local,
        mesh=mesh,
        in_specs=(
            P(("seq", "tp"), None),
            P(("seq", "tp"), None),
            P(None, "seq", "tp"),
            P("tp", "seq"),
            P(None, "seq", "tp"),
            P("tp", "seq"),
            P(None, "seq", None),
            P("tp", "seq"),
            P("tp", "seq"),
            P(None, "seq", "tp"),
            P(None, "seq", "tp"),
            P(None, "seq", None),
            P(),
            P(),
            P(),
            P(),
        ),
        out_specs=(
            P(("seq", "tp"), None),
            P(("seq", "tp"), None),
            P(None, "seq", None),
            P("tp", "seq"),
            P("tp", "seq"),
            P(None, "seq", "tp"),
            P(None, "seq", "tp"),
            P(None, "seq", None),
        ),
        check_vma=False,
    )
```

```python
import functools

import jax
import jax.numpy as jnp
from jax import lax
from jax.experimental import pallas as pl
from jax.experimental.pallas import tpu as pltpu
from jax.sharding import PartitionSpec as P

HEAD_DIM = 128
ADAPTER_RANK = 16
BLK = 128
PROMPT_BLOCKS = 8
EPS = 1e-06
THETA = 500000.0
NEG = -1e30
LOG2E = 1.4426950408889634
F32 = jnp.float32
BF16 = jnp.bfloat16


def mm(a, b):
    return jnp.dot(a, b, preferred_element_type=F32)


def mm_nt(a, b):
    return lax.dot_general(a, b, (((1,), (1,)), ((), ())), preferred_element_type=F32)


def mm_tn(a, b):
    return lax.dot_general(a, b, (((0,), (0,)), ((), ())), preferred_element_type=F32)


def bits_of(count):
    n = count.bit_length() - 1
    assert 1 << n == count
    return n


def flip(value, axis, count, bit):
    return lax.ppermute(value, axis, [(i, i ^ (1 << bit)) for i in range(count)])


def gather_order(value, axis, count, order):
    rank = lax.axis_index(axis)
    have = []
    current = value
    for bit in order:
        other = flip(current, axis, count, bit)
        mine_low = ((rank >> bit) & 1) == 0
        at = len([b for b in have if b > bit])
        low = jnp.where(mine_low, current, other)
        high = jnp.where(mine_low, other, current)
        current = jnp.stack([low, high], axis=at)
        have = sorted(have + [bit], reverse=True)
    return current.reshape((count,) + value.shape)


def scatter_order(value, axis, count, order):
    n = bits_of(count)
    rank = lax.axis_index(axis)
    current = value.reshape((2,) * n + value.shape[1:])
    have = list(range(n - 1, -1, -1))
    for bit in order:
        at = have.index(bit)
        mine = (rank >> bit) & 1
        keep = lax.dynamic_index_in_dim(current, mine, at, keepdims=False)
        give = lax.dynamic_index_in_dim(current, 1 - mine, at, keepdims=False)
        got = flip(give.astype(BF16), axis, count, bit)
        current = keep.astype(F32) + got.astype(F32)
        have.remove(bit)
    return current


def part_orders(count):
    order = list(range(bits_of(count)))
    return (order, order[::-1])


def group_masks(count):
    groups = ([], [])
    for part, order in enumerate(part_orders(count)):
        for j in range(count):
            mask = sum(1 << bit for i, bit in enumerate(order) if (j >> i) & 1)
            groups[j >= count // 2].append((mask, part))
    return groups


def row_runs(count):
    return [run for masks in group_masks(count) for run in masks]


def gather_groups(parts, count, beside=None):
    near, far = [], []
    for value, order in zip(parts, part_orders(count)):
        for bit in order[:-1]:
            value = jnp.concatenate([value, flip(value, "tp", count, bit)], axis=0)
        near.append(value)
    if beside is not None:
        near[1], beside = lax.optimization_barrier((near[1], beside))
    for value, order in zip(near, part_orders(count)):
        far.append(flip(value, "tp", count, order[-1]))
    if beside is not None:
        return jnp.concatenate(near, axis=0), jnp.concatenate(far, axis=0), beside
    return jnp.concatenate(near, axis=0), jnp.concatenate(far, axis=0)


def scatter_groups(near, far, count):
    out = []
    size = near.shape[0] // 2
    for i, order in enumerate(part_orders(count)):
        got = flip(far[i], "tp", count, order[-1])
        total = near[i * size : (i + 1) * size].astype(F32) + got.astype(F32)
        for bit in order[-2::-1]:
            half = total.shape[0] // 2
            got = flip(total[half:].astype(BF16), "tp", count, bit)
            total = total[:half] + got.astype(F32)
        out.append(total)
    return out


def sum_rows(value, count):
    runs = row_runs(count)
    value = value.reshape(value.shape[0], len(runs), -1)
    total = value
    for mask in range(1, count):
        got = lax.ppermute(value, "tp", [(i, i ^ mask) for i in range(count)])
        order = [runs.index((other ^ mask, which)) for other, which in runs]
        total = total + jnp.concatenate([got[:, j : j + 1] for j in order], axis=1)
    return total.reshape(value.shape[0], -1)


def sum_all(value, axis, count):
    for bit in range(bits_of(count)):
        value = value + flip(value, axis, count, bit)
    return value


def copy_all(pairs, sem):
    copies = [pltpu.make_async_copy(src, dst, sem.at[i]) for i, (src, dst) in enumerate(pairs)]
    for copy in copies:
        copy.start()
    for copy in copies:
        copy.wait()


def gather_prompt(prompt_at, source, target, count):
    def step(i, carry):
        start = pl.multiple_of(prompt_at[i] * BLK, BLK)
        target[pl.ds(pl.multiple_of(i * BLK, BLK), BLK), :] = source[pl.ds(start, BLK), :]
        return carry

    lax.fori_loop(0, count, step, 0)


def masked_scores(keys, own_keys, queries, place, scale):
    prompt = mm_nt(keys, queries) * scale
    block = lax.broadcasted_iota(jnp.int32, prompt.shape, 0) // BLK
    prompt = jnp.where(block < place, prompt, NEG)
    own = mm_nt(own_keys, queries) * scale
    causal = lax.broadcasted_iota(jnp.int32, own.shape, 0) <= lax.broadcasted_iota(
        jnp.int32, own.shape, 1
    )
    own = jnp.where(causal, own, NEG)
    top = jnp.maximum(jnp.max(prompt, axis=0, keepdims=True), jnp.max(own, axis=0, keepdims=True))
    prompt = jnp.exp2(prompt - top)
    own = jnp.exp2(own - top)
    total = jnp.sum(prompt, axis=0, keepdims=True) + jnp.sum(own, axis=0, keepdims=True)
    return prompt, own, 1.0 / total


def load_plan(slots, group, rows, refs, q_buf, k_buf, v_buf):
    plan = []
    for i in range(slots):
        plan.append((refs[i], q_buf.at[pl.ds(i * rows, rows)]))
    for i in range(slots * group):
        at = pl.ds(i * rows, rows)
        ref = refs[slots + i]
        plan += [(ref.at[0], k_buf.at[at]), (ref.at[1], v_buf.at[at])]
    return plan


def attend_kernel(slots, group, rows, prompt_count, q_seq, q_place, prompt_at, *refs):
    n_in = slots + slots * group
    outs = refs[n_in : n_in + slots]
    q_buf, k_buf, v_buf, kp, vp, o_buf, sem = refs[n_in + slots :]
    copy_all(load_plan(slots, group, rows, refs, q_buf, k_buf, v_buf), sem)
    gather_prompt(prompt_at, k_buf, kp, prompt_count)
    gather_prompt(prompt_at, v_buf, vp, prompt_count)
    scale = HEAD_DIM ** (-0.5) * LOG2E
    span = PROMPT_BLOCKS * BLK

    def step(i, carry):
        at = pl.ds(pl.multiple_of(i * BLK, BLK), BLK)
        of_seq = pl.ds(pl.multiple_of(q_seq[i] * span, span), span)
        prompt, own, inverse = masked_scores(
            kp[of_seq, :], k_buf[at, :], q_buf[at, :], q_place[i], scale
        )
        result = mm_tn(vp[of_seq, :], prompt.astype(BF16)) + mm_tn(v_buf[at, :], own.astype(BF16))
        o_buf[at, :] = (result * inverse).T.astype(BF16)
        return carry

    lax.fori_loop(0, slots * rows // BLK, step, 0)
    copy_all([(o_buf.at[pl.ds(i * rows, rows)], outs[i]) for i in range(slots)], sem)


def attend_back_kernel(
    slots, group, rows, pieces, prompt_count, q_seq, q_place, prompt_at, piece_at, *refs
):
    n_in = slots + slots * group
    n_grad = slots * 2
    grads = refs[n_in : n_in + n_grad]
    outs = refs[n_in + n_grad : n_in + n_grad + slots]
    near_out = refs[n_in + n_grad + slots]
    rest = refs[n_in + n_grad + slots + 1 :]
    far_outs, rest = rest[: group - 1], rest[group - 1 :]
    q_buf, k_buf, v_buf, do_buf, kp, vp, dkp, dvp, dq_buf, dkv_buf, sem = rest
    plan = load_plan(slots, group, rows, refs, q_buf, k_buf, v_buf)
    size = rows // pieces
    for i in range(slots):
        for p in range(pieces):
            half, at = divmod(p, pieces // 2)
            to = pl.multiple_of(i * rows + piece_at[p] * size, 16)
            plan.append(
                (grads[i * 2 + half].at[pl.ds(at * size, size)], do_buf.at[pl.ds(to, size)])
            )
    copy_all(plan, sem)
    gather_prompt(prompt_at, k_buf, kp, prompt_count)
    gather_prompt(prompt_at, v_buf, vp, prompt_count)
    dkp[...] = jnp.zeros_like(dkp)
    dvp[...] = jnp.zeros_like(dvp)
    scale = HEAD_DIM ** (-0.5)
    span = PROMPT_BLOCKS * BLK
    own_rows = slots * rows
    zeros = jnp.zeros((BLK, HEAD_DIM), BF16)

    def rows_of(i):
        return pl.ds(pl.multiple_of(i * BLK, BLK), BLK)

    def clear(i, carry):
        for j in range(1, group):
            dkv_buf[j, 0, rows_of(i), :] = zeros
            dkv_buf[j, 1, rows_of(i), :] = zeros
        return carry

    lax.fori_loop(0, own_rows // BLK, clear, 0)

    def step(i, carry):
        at = rows_of(i)
        seq, place = q_seq[i], q_place[i]
        of_seq = pl.ds(pl.multiple_of(seq * span, span), span)
        queries, grad = q_buf[at, :], do_buf[at, :]
        prompt, own, inverse = masked_scores(
            kp[of_seq, :], k_buf[at, :], queries, place, scale * LOG2E
        )
        prompt, own = prompt * inverse, own * inverse
        d_prompt = mm_nt(vp[of_seq, :], grad)
        d_own = mm_nt(v_buf[at, :], grad)
        delta = jnp.sum(prompt * d_prompt, axis=0, keepdims=True) + jnp.sum(
            own * d_own, axis=0, keepdims=True
        )
        ds_prompt = (prompt * (d_prompt - delta)).astype(BF16)
        ds_own = (own * (d_own - delta)).astype(BF16)
        dq = mm_tn(ds_prompt, kp[of_seq, :]) + mm_tn(ds_own, k_buf[at, :])
        dq_buf[at, :] = (dq * scale).astype(BF16)
        dvp[of_seq, :] += mm(prompt.astype(BF16), grad)
        dkp[of_seq, :] += mm(ds_prompt, queries) * scale
        dkv_buf[0, 0, at, :] = (mm(ds_own, queries) * scale).astype(BF16)
        dkv_buf[0, 1, at, :] = mm(own.astype(BF16), grad).astype(BF16)
        return carry

    lax.fori_loop(0, own_rows // BLK, step, 0)
    blocks = own_rows // BLK

    def spread(i, carry):
        place = prompt_at[i]
        j, to = place // blocks, rows_of(place % blocks)
        dkv_buf[j, 0, to, :] = (dkv_buf[j, 0, to, :].astype(F32) + dkp[rows_of(i), :]).astype(BF16)
        dkv_buf[j, 1, to, :] = (dkv_buf[j, 1, to, :].astype(F32) + dvp[rows_of(i), :]).astype(BF16)
        return carry

    lax.fori_loop(0, prompt_count, spread, 0)
    plan = [(dq_buf.at[pl.ds(i * rows, rows)], outs[i]) for i in range(slots)]
    plan.append((dkv_buf.at[0], near_out))
    plan += [(dkv_buf.at[j], far_outs[j - 1]) for j in range(1, group)]
    copy_all(plan, sem)


ANY = pl.BlockSpec(memory_space=pl.ANY)


def attend(tables, queries, near, far, prompt_count):
    slots = len(near)
    rows = queries[0].shape[0]
    group = 1 + len(far) // slots
    own, every = slots * rows, slots * group * rows
    pairs = own * (PROMPT_BLOCKS + 1) * BLK
    wide = lambda count, kind=BF16: pltpu.VMEM((count, HEAD_DIM), kind)
    return pl.pallas_call(
        functools.partial(attend_kernel, slots, group, rows, prompt_count),
        out_shape=[jax.ShapeDtypeStruct((rows, HEAD_DIM), BF16)] * slots,
        grid_spec=pltpu.PrefetchScalarGridSpec(
            num_scalar_prefetch=3,
            in_specs=[ANY] * (slots + slots * group),
            out_specs=[ANY] * slots,
            scratch_shapes=[
                wide(own),
                wide(every),
                wide(every),
                wide(prompt_count * BLK),
                wide(prompt_count * BLK),
                wide(own),
                pltpu.SemaphoreType.DMA((slots + 2 * slots * group,)),
            ],
        ),
        cost_estimate=pl.CostEstimate(
            flops=4 * pairs * HEAD_DIM, bytes_accessed=6 * every * HEAD_DIM, transcendentals=pairs
        ),
        name="attend",
    )(*tables, *queries, *near, *far)


def attend_back(tables, piece_at, queries, near, far, grads, prompt_count):
    pieces = piece_at.shape[0]
    slots = len(near)
    rows = queries[0].shape[0]
    group = 1 + len(far) // slots
    own, every = slots * rows, slots * group * rows
    pairs = own * (PROMPT_BLOCKS + 1) * BLK
    wide = lambda count, kind=BF16: pltpu.VMEM((count, HEAD_DIM), kind)
    return pl.pallas_call(
        functools.partial(attend_back_kernel, slots, group, rows, pieces, prompt_count),
        out_shape=[jax.ShapeDtypeStruct((rows, HEAD_DIM), BF16)] * slots
        + [jax.ShapeDtypeStruct((2, own, HEAD_DIM), BF16)] * group,
        grid_spec=pltpu.PrefetchScalarGridSpec(
            num_scalar_prefetch=4,
            in_specs=[ANY] * (slots + slots * group + 2 * slots),
            out_specs=[ANY] * (slots + group),
            scratch_shapes=[
                wide(own),
                wide(every),
                wide(every),
                wide(own),
                wide(prompt_count * BLK),
                wide(prompt_count * BLK),
                wide(prompt_count * BLK, F32),
                wide(prompt_count * BLK, F32),
                wide(own),
                pltpu.VMEM((group, 2, own, HEAD_DIM), BF16),
                pltpu.SemaphoreType.DMA((slots + 2 * slots * group + slots * pieces,)),
            ],
        ),
        cost_estimate=pl.CostEstimate(
            flops=10 * pairs * HEAD_DIM, bytes_accessed=12 * every * HEAD_DIM, transcendentals=pairs
        ),
        name="attend_back",
    )(*tables, piece_at, *queries, *near, *far, *grads)


def turn(values, cosine, sine):
    return values * cosine + pltpu.roll(values, HEAD_DIM // 2, 1) * sine


def lanes(head, base=0):
    return pl.ds(pl.multiple_of(base + head * HEAD_DIM, HEAD_DIM), HEAD_DIM)


def piece_rows(index, size):
    return pl.ds(pl.multiple_of(index * size, 16), size)


def spread_kernel(slots, pieces, order, piece_at, z, inv, cs, gain, *outs):
    cols = slots * HEAD_DIM
    size = z.shape[0] // pieces

    def step(p, carry):
        at, to = piece_rows(p, size), piece_rows(piece_at[p], size)
        cosine, sine = cs[at, :HEAD_DIM], cs[at, HEAD_DIM:]
        for which in range(2):
            factor = inv[at, which : which + 1]
            for k in range(slots):
                head = order[k]
                scaled = z[at, lanes(head, which * cols)] * factor
                scaled = scaled * gain[which : which + 1, lanes(head)]
                turned = turn(scaled, cosine, sine).astype(BF16)
                if which == 0:
                    outs[k][to, :] = turned
                else:
                    outs[slots + k][0, to, :] = turned
        for k in range(slots):
            outs[slots + k][1, to, :] = z[at, lanes(order[k], 2 * cols)].astype(BF16)
        return carry

    lax.fori_loop(0, pieces, step, 0)


WHOLE = pl.BlockSpec(memory_space=pltpu.VMEM)
BIG = pltpu.CompilerParams(vmem_limit_bytes=56 * 1024 * 1024)


def spread_heads(order, piece_at, z, inv, cs, gain, slots):
    rows = z.shape[0]
    return pl.pallas_call(
        functools.partial(spread_kernel, slots, piece_at.shape[0]),
        out_shape=[jax.ShapeDtypeStruct((rows, HEAD_DIM), BF16)] * slots
        + [jax.ShapeDtypeStruct((2, rows, HEAD_DIM), BF16)] * slots,
        grid_spec=pltpu.PrefetchScalarGridSpec(
            num_scalar_prefetch=2, in_specs=[WHOLE] * 4, out_specs=[WHOLE] * (2 * slots)
        ),
        compiler_params=BIG,
        name="spread_heads",
    )(order, piece_at, z, inv, cs, gain)


def collect_kernel(slots, pieces, order, piece_at, *refs):
    outs = refs[slots:]
    size = refs[0].shape[0] // pieces
    for p in range(pieces):
        half, at = divmod(p, pieces // 2)
        for k in range(slots):
            outs[half][pl.ds(at * size, size), lanes(order[k])] = refs[k][
                piece_rows(piece_at[p], size), :
            ]


def collect_heads(order, piece_at, parts):
    slots = len(parts)
    rows = parts[0].shape[0]
    return pl.pallas_call(
        functools.partial(collect_kernel, slots, piece_at.shape[0]),
        out_shape=[jax.ShapeDtypeStruct((rows // 2, slots * HEAD_DIM), BF16)] * 2,
        grid_spec=pltpu.PrefetchScalarGridSpec(
            num_scalar_prefetch=2, in_specs=[WHOLE] * slots, out_specs=[WHOLE] * 2
        ),
        name="collect_heads",
    )(order, piece_at, *parts)


def unturn_kernel(slots, pieces, order, piece_at, *refs):
    dqs, dkvs, rest = refs[:slots], refs[slots : 2 * slots], refs[2 * slots :]
    z, cs, gain, scaled_out, part_out = rest
    cols = slots * HEAD_DIM
    size = z.shape[0] // pieces

    def step(p, carry):
        at, source = piece_rows(p, size), piece_rows(piece_at[p], size)
        cosine, sine = cs[at, :HEAD_DIM], cs[at, HEAD_DIM:]
        for which in range(2):
            total = jnp.zeros((size, HEAD_DIM), F32)
            for k in range(slots):
                head = order[k]
                grad = dqs[k][source, :] if which == 0 else dkvs[k][0, source, :]
                grad = turn(grad.astype(F32), cosine, -sine) * gain[which : which + 1, lanes(head)]
                scaled_out[at, lanes(head, which * cols)] = grad
                total = total + grad * z[at, lanes(head, which * cols)]
            part_out[at, which : which + 1] = jnp.sum(total, axis=1, keepdims=True)
        return carry

    lax.fori_loop(0, pieces, step, 0)


def unturn_heads(order, piece_at, dqs, dkvs, z, cs, gain):
    slots = len(dqs)
    rows = z.shape[0]
    cols = slots * HEAD_DIM
    return pl.pallas_call(
        functools.partial(unturn_kernel, slots, piece_at.shape[0]),
        out_shape=[
            jax.ShapeDtypeStruct((rows, 2 * cols), F32),
            jax.ShapeDtypeStruct((rows, 2), F32),
        ],
        grid_spec=pltpu.PrefetchScalarGridSpec(
            num_scalar_prefetch=2, in_specs=[WHOLE] * (2 * slots + 3), out_specs=[WHOLE] * 2
        ),
        compiler_params=BIG,
        name="unturn_heads",
    )(order, piece_at, *dqs, *dkvs, z, cs, gain)


def norm_back_kernel(slots, pieces, order, piece_at, *refs):
    dkvs, (scaled, z, coef, out) = refs[:slots], refs[slots:]
    cols = slots * HEAD_DIM
    size = z.shape[0] // pieces

    def step(p, carry):
        at, source = piece_rows(p, size), piece_rows(piece_at[p], size)
        for which in range(2):
            to = slice(which * cols, (which + 1) * cols)
            out[at, to] = (
                scaled[at, to] * coef[at, which : which + 1]
                - z[at, to] * coef[at, 2 + which : 3 + which]
            ).astype(BF16)
        for k in range(slots):
            out[at, lanes(order[k], 2 * cols)] = dkvs[k][1, source, :]
        return carry

    lax.fori_loop(0, pieces, step, 0)


def norm_back_heads(order, piece_at, dkvs, scaled, z, coef):
    slots = len(dkvs)
    return pl.pallas_call(
        functools.partial(norm_back_kernel, slots, piece_at.shape[0]),
        out_shape=jax.ShapeDtypeStruct(z.shape, BF16),
        grid_spec=pltpu.PrefetchScalarGridSpec(
            num_scalar_prefetch=2, in_specs=[WHOLE] * (slots + 3), out_specs=WHOLE
        ),
        compiler_params=BIG,
        name="norm_back_heads",
    )(order, piece_at, *dkvs, scaled, z, coef)


def fixed(*shape, at=None):
    place = at or (0,) * len(shape)
    return pl.BlockSpec(shape, lambda i: place)


def flat(value):
    return value.reshape(-1, value.shape[-1])


def qkv_kernel(x, latent, weight, second, z, squares):
    i = pl.program_id(0)
    result = mm(x[...], flat(weight[...])) + mm(latent[...], flat(second[...]))
    z[...] = result
    squares[0, :, :] = jnp.sum(result * result, axis=1, keepdims=True)


def qkv_product(x, latents, first, second, k_rows, cols):
    rows, width = x.shape
    shards, _, total = first.shape
    low = latents.shape[1] // 3
    return pl.pallas_call(
        qkv_kernel,
        grid=(3,),
        out_shape=[
            jax.ShapeDtypeStruct((rows, total), F32),
            jax.ShapeDtypeStruct((3, rows, 1), F32),
        ],
        in_specs=[
            fixed(rows, width),
            pl.BlockSpec((rows, low), lambda i: (0, i)),
            pl.BlockSpec((shards, k_rows, cols), lambda i: (0, 0, i)),
            pl.BlockSpec((low, cols), lambda i: (0, i)),
        ],
        out_specs=[
            pl.BlockSpec((rows, cols), lambda i: (0, i)),
            pl.BlockSpec((1, rows, 1), lambda i: (i, 0, 0)),
        ],
        compiler_params=BIG,
        cost_estimate=pl.CostEstimate(
            flops=2 * rows * width * total, bytes_accessed=2 * first.size, transcendentals=0
        ),
        name="qkv_product",
    )(x, latents, first, second)


def add_kernel(parts, a, weight, first, second, pick, *refs):
    outs, (latent_out, latent) = refs[:parts], refs[parts:]

    @pl.when(pl.program_id(0) == 0)
    def _():
        latent[...] = (mm(a[...], first[...]) * pick[...]).astype(BF16)
        latent_out[...] = latent[...]

    result = mm_nt(a[...], weight[...]) + mm(latent[...], second[...])
    size = result.shape[0] // parts
    for i in range(parts):
        outs[i][...] = result[i * size : (i + 1) * size].astype(BF16)


def add_product(a, weight, first, second, pick, parts, tile=512):
    rows, depth = a.shape
    width, low = weight.shape[0], first.shape[1]
    size = rows // parts
    return pl.pallas_call(
        functools.partial(add_kernel, parts),
        grid=(width // tile,),
        out_shape=[jax.ShapeDtypeStruct((size, width), BF16)] * parts
        + [jax.ShapeDtypeStruct((rows, low), BF16)],
        in_specs=[
            fixed(rows, depth),
            pl.BlockSpec((tile, depth), lambda i: (i, 0)),
            fixed(depth, low),
            pl.BlockSpec((low, tile), lambda i: (0, i)),
            fixed(rows, low),
        ],
        out_specs=[pl.BlockSpec((size, tile), lambda i: (0, i))] * parts + [fixed(rows, low)],
        scratch_shapes=[pltpu.VMEM((rows, low), BF16)],
        compiler_params=BIG,
        cost_estimate=pl.CostEstimate(
            flops=2 * rows * width * depth, bytes_accessed=2 * weight.size, transcendentals=0
        ),
        name="add_product",
    )(a, weight, first, second, pick)


def back_kernel(parts, a, weight, u, first, *outs):
    result = mm_nt(a[...], flat(weight[...])) + mm_nt(u[...], first[...])
    size = result.shape[0] // parts
    for i in range(parts):
        outs[i][...] = result[i * size : (i + 1) * size].astype(BF16)


def back_product(a, group, weight, k_rows, u, first, parts):
    rows, depth = a.shape
    rows //= 2
    shards = weight.shape[0]
    width, low = first.shape
    per = max(1, 512 // k_rows)
    size = rows // parts
    return pl.pallas_call(
        functools.partial(back_kernel, parts),
        grid=(shards // per,),
        out_shape=[jax.ShapeDtypeStruct((size, width), BF16)] * parts,
        in_specs=[
            fixed(rows, depth, at=(group, 0)),
            pl.BlockSpec((per, k_rows, depth), lambda i: (i, 0, 0)),
            fixed(rows, low, at=(group, 0)),
            pl.BlockSpec((per * k_rows, low), lambda i: (i, 0)),
        ],
        out_specs=[pl.BlockSpec((size, per * k_rows), lambda i: (0, i))] * parts,
        compiler_params=BIG,
        cost_estimate=pl.CostEstimate(
            flops=2 * rows * width * depth, bytes_accessed=2 * width * depth, transcendentals=0
        ),
        name="back_product",
    )(a, weight, u, first)


def gate_up_kernel(h, first, pick, w_g, w_u, b_g, b_u, gate_out, up_out, act, latent_out, latent):
    low = pick.shape[1]

    @pl.when(pl.program_id(0) == 0)
    def _():
        both = mm(h[...], first[...])
        latent[:, :low] = (both[:, :low] * pick[...]).astype(BF16)
        latent[:, low:] = (both[:, low:] * pick[...]).astype(BF16)
        latent_out[...] = latent[...]

    gate = mm(h[...], w_g[...]) + mm(latent[:, :low], b_g[...])
    up = mm(h[...], w_u[...]) + mm(latent[:, low:], b_u[...])
    gate_out[...] = gate
    up_out[...] = up
    act[...] = (gate / (1.0 + jnp.exp(-gate)) * up).astype(BF16)


def gate_up_product(h, w_gu, a_gu, b_gu, pick, tile=512):
    rows, width = h.shape
    units, low = w_gu.shape[1] // 2, pick.shape[1]
    n = units // tile
    left = lambda depth: pl.BlockSpec((depth, tile), lambda i: (0, i))
    out = pl.BlockSpec((rows, tile), lambda i: (0, i))
    return pl.pallas_call(
        gate_up_kernel,
        grid=(n,),
        out_shape=[jax.ShapeDtypeStruct((rows, units), F32)] * 2
        + [
            jax.ShapeDtypeStruct((rows, units), BF16),
            jax.ShapeDtypeStruct((rows, 2 * low), BF16),
        ],
        in_specs=[
            fixed(rows, width),
            fixed(width, 2 * low),
            fixed(rows, low),
            left(width),
            pl.BlockSpec((width, tile), lambda i: (0, i + n)),
            left(low),
            pl.BlockSpec((low, tile), lambda i: (1, i)),
        ],
        out_specs=[out, out, out, fixed(rows, 2 * low)],
        scratch_shapes=[pltpu.VMEM((rows, 2 * low), BF16)],
        compiler_params=BIG,
        cost_estimate=pl.CostEstimate(
            flops=4 * rows * width * units, bytes_accessed=4 * width * units, transcendentals=0
        ),
        name="gate_up_product",
    )(h, a_gu, pick, w_gu, w_gu, b_gu, b_gu)


def ff_back_kernel(
    parts, steps, d_ff, b_down, pick, w_down, a_down, gate, up, w_g, w_u, b_g, b_u, a_gu, *refs
):
    outs, (d_gate_out, d_up_out, u_out, u_down_out, acc, u_g, u_u, u_down) = refs[:parts], refs[parts:]
    i = pl.program_id(0)

    @pl.when(i == 0)
    def _():
        u_down[...] = (mm_nt(d_ff[...], b_down[...]) * pick[...]).astype(BF16)
        u_down_out[...] = u_down[...]

    d_act = mm(d_ff[...], w_down[...]) + mm_nt(u_down[...], a_down[...])
    g = gate[...]
    sigmoid = 1.0 / (1.0 + jnp.exp(-g))
    silu = g * sigmoid
    d_gate = (d_act * up[...] * (sigmoid + silu * (1.0 - sigmoid))).astype(BF16)
    d_up = (d_act * silu).astype(BF16)
    d_gate_out[...] = d_gate
    d_up_out[...] = d_up
    part = mm_nt(d_gate, w_g[...]) + mm_nt(d_up, w_u[...])
    part_g, part_u = mm_nt(d_gate, b_g[...]), mm_nt(d_up, b_u[...])

    @pl.when(i == 0)
    def _():
        acc[...] = part
        u_g[...] = part_g
        u_u[...] = part_u

    @pl.when(i > 0)
    def _():
        acc[...] += part
        u_g[...] += part_g
        u_u[...] += part_u

    @pl.when(i == steps - 1)
    def _():
        low = pick.shape[1]
        last_g = (u_g[...] * pick[...]).astype(BF16)
        last_u = (u_u[...] * pick[...]).astype(BF16)
        u_out[:, :low] = last_g
        u_out[:, low:] = last_u
        size = acc.shape[0] // parts
        for p in range(parts):
            at = slice(p * size, (p + 1) * size)
            outs[p][...] = (
                acc[at, :]
                + mm_nt(last_g[at], a_gu[:, :low])
                + mm_nt(last_u[at], a_gu[:, low:])
            ).astype(BF16)


def ff_back(d_ff, b_down, pick, w_down, a_down, gate, up, w_gu, b_gu, a_gu, parts, tile=512):
    rows, width = d_ff.shape
    units, low = gate.shape[1], pick.shape[1]
    n = units // tile
    size = rows // parts
    column = lambda depth: pl.BlockSpec((depth, tile), lambda i: (0, i))
    return pl.pallas_call(
        functools.partial(ff_back_kernel, parts, n),
        grid=(n,),
        out_shape=[jax.ShapeDtypeStruct((size, width), BF16)] * parts
        + [jax.ShapeDtypeStruct((rows, units), BF16)] * 2
        + [
            jax.ShapeDtypeStruct((rows, 2 * low), BF16),
            jax.ShapeDtypeStruct((rows, low), BF16),
        ],
        in_specs=[
            fixed(rows, width),
            fixed(low, width),
            fixed(rows, low),
            column(width),
            pl.BlockSpec((tile, low), lambda i: (i, 0)),
            column(rows),
            column(rows),
            column(width),
            pl.BlockSpec((width, tile), lambda i: (0, i + n)),
            column(low),
            pl.BlockSpec((low, tile), lambda i: (1, i)),
            fixed(width, 2 * low),
        ],
        out_specs=[fixed(size, width)] * parts
        + [column(rows), column(rows), fixed(rows, 2 * low), fixed(rows, low)],
        scratch_shapes=[
            pltpu.VMEM((rows, width), F32),
            pltpu.VMEM((rows, low), F32),
            pltpu.VMEM((rows, low), F32),
            pltpu.VMEM((rows, low), BF16),
        ],
        compiler_params=BIG,
        cost_estimate=pl.CostEstimate(
            flops=6 * rows * width * units, bytes_accessed=6 * width * units, transcendentals=0
        ),
        name="ff_back",
    )(d_ff, b_down, pick, w_down, a_down, gate, up, w_gu, w_gu, b_gu, b_gu, a_gu)


def blocked(parts):
    zeros = lambda a, b: jnp.zeros((a.shape[0], b.shape[1]), a.dtype)
    return jnp.concatenate(
        [
            jnp.concatenate([a if a is b else zeros(a, b) for b in parts], axis=1)
            for a in parts
        ],
        axis=0,
    )


def local(
    layer_input,
    cotangent,
    query_key_value_weight,
    output_weight,
    gate_up_weight,
    down_weight,
    input_first_factor,
    output_first_factor,
    down_first_factor,
    query_key_value_second,
    gate_up_second_factor,
    output_down_second_factor,
    norm_gain_table,
    sequence_adapter,
    block_sequence,
    block_position,
):
    tp, tp_rank = lax.axis_size("tp"), lax.axis_index("tp")
    seqs, seq_rank = lax.axis_size("seq"), lax.axis_index("seq")
    own_rows, width = layer_input.shape
    rows = own_rows * tp
    part = own_rows // 2
    my_blocks = rows // BLK
    cols = query_key_value_weight.shape[2]
    heads = cols // HEAD_DIM
    hidden_cols = gate_up_weight.shape[2]
    k_rows = query_key_value_weight.shape[1]
    slots_a = input_first_factor.shape[2]
    rank_cols = output_first_factor.shape[1]
    group = seqs // heads
    head_rank, group_rank = seq_rank // group, seq_rank % group
    n_seq = sequence_adapter.shape[0]
    groups = (0, 1)

    a_part = k_rows // tp
    b_part = width // tp
    a_mine = lax.dynamic_slice_in_dim(input_first_factor, tp_rank * a_part, a_part, 1)
    b_mine = lax.dynamic_slice_in_dim(output_down_second_factor, tp_rank * b_part, b_part, 2)
    first = jnp.concatenate(
        [
            query_key_value_weight.transpose(1, 0, 2).reshape(k_rows, 3 * cols),
            query_key_value_second.transpose(1, 0, 2).reshape(rank_cols, 3 * cols),
            a_mine[:3].reshape(-1, 3 * cols),
        ],
        axis=0,
    )
    x_parts = [layer_input] + [
        lax.ppermute(layer_input, "tp", [(i, i ^ mask) for i in range(tp)]) for mask in range(1, tp)
    ]
    first = lax.all_gather(first, "seq", axis=0)
    pieces = [
        output_weight.T,
        output_first_factor.T,
        b_mine.reshape(-1, cols),
        a_mine[3:].reshape(-1, cols),
        down_first_factor.T.reshape(-1, cols),
        gate_up_second_factor.reshape(-1, cols),
    ]
    packed = jnp.concatenate(pieces, axis=0)
    x_parts, packed, w_gu, w_down = lax.optimization_barrier(
        (
            x_parts,
            packed,
            gate_up_weight.transpose(1, 0, 2).reshape(k_rows, 2 * hidden_cols),
            down_weight.T,
        )
    )
    packed = lax.all_gather(packed, "seq", axis=0)
    split, at = [], 0
    for piece in pieces:
        split.append(packed[:, at : at + piece.shape[0]])
        at += piece.shape[0]
    w_gu = lax.all_gather(w_gu, "seq", axis=0, tiled=True)
    w_down = lax.all_gather(w_down, "seq", axis=0, tiled=True)

    tp_order, seq_order = list(range(bits_of(tp))), list(range(bits_of(seqs)))
    a_qkv = first[:, k_rows + rank_cols :].reshape(seqs, 3, a_part, slots_a)
    a_qkv = a_qkv.transpose(0, 2, 1, 3).reshape(seqs, a_part, 3 * slots_a)
    a_parts = [a_qkv] + [
        lax.ppermute(a_qkv, "tp", [(i, i ^ mask) for i in range(tp)]) for mask in range(1, tp)
    ]
    a_qkv = jnp.zeros((seqs, tp, a_part, 3 * slots_a), BF16)
    for mask, value in enumerate(a_parts):
        a_qkv = lax.dynamic_update_slice(a_qkv, value[:, None], (0, tp_rank ^ mask, 0, 0))
    a_qkv = a_qkv.reshape(width, 3 * slots_a)
    b_qkv = first[:, k_rows : k_rows + rank_cols].reshape(slots_a, 3 * cols)
    b_qkv = blocked([b_qkv[:, i * cols : (i + 1) * cols] for i in range(3)])
    w_o = split[0].reshape(width, cols)
    a_o = split[1].reshape(slots_a, cols).T
    shared = gather_order(jnp.concatenate(split[2:4], axis=1), "tp", tp, tp_order)
    b_size = split[2].shape[1]
    b_od = (
        shared[:, :, :b_size]
        .reshape(tp, seqs, 2, rank_cols, b_part)
        .transpose(2, 1, 3, 0, 4)
        .reshape(2, slots_a, width)
    )
    a_gu = (
        shared[:, :, b_size:]
        .reshape(tp, seqs, 2, a_part, slots_a)
        .transpose(1, 0, 3, 2, 4)
        .reshape(width, 2 * slots_a)
    )
    a_down = split[4].reshape(slots_a, hidden_cols).T
    b_gu = (
        split[5]
        .reshape(seqs, 2, rank_cols, hidden_cols)
        .transpose(1, 0, 2, 3)
        .reshape(2 * slots_a, hidden_cols)
    )

    runs = row_runs(tp)
    piece_at = jnp.stack([2 * (tp_rank ^ mask) + which for mask, which in runs]).astype(jnp.int32)
    token = (piece_at[:, None] * part + jnp.arange(part, dtype=jnp.int32)[None, :]).reshape(-1)
    token_block, offset = token // BLK, token % BLK
    block_ids = seq_rank * my_blocks + jnp.arange(my_blocks, dtype=jnp.int32)
    place_blocks = block_position[block_ids]
    adapter_blocks = sequence_adapter[block_sequence[block_ids]]
    in_block = token_block[:, None] == jnp.arange(my_blocks, dtype=jnp.int32)[None, :]
    pick = lambda per_block: jnp.sum(jnp.where(in_block, per_block[None, :], 0), axis=1)
    select = (
        jnp.arange(slots_a, dtype=jnp.int32)[None, :] // ADAPTER_RANK
        == pick(adapter_blocks)[:, None]
    ).astype(F32) * 2.0
    half = rows // 2
    selects = [select[:half], select[half:]]
    start = jnp.where(place_blocks < PROMPT_BLOCKS, place_blocks, PROMPT_BLOCKS) * BLK
    position = pick(start) + offset
    frequency = THETA ** (-(jnp.arange(HEAD_DIM // 2, dtype=F32) * 2.0) / HEAD_DIM)
    angles = position.astype(F32)[:, None] * frequency[None, :]
    cosine, sine = jnp.cos(angles), jnp.sin(angles)
    cs = jnp.concatenate([cosine, cosine, -sine, sine], axis=1)

    owner = (
        ((head_rank - jnp.arange(heads)) % heads)[None, :] * group
        + ((group_rank + jnp.arange(group)) % group)[:, None]
    ).reshape(-1)
    held = (owner[:, None] * my_blocks + jnp.arange(my_blocks)[None, :]).reshape(-1)
    held_seq = block_sequence[held].astype(jnp.int32)
    held_place = block_position[held].astype(jnp.int32)
    prompt_count = n_seq * PROMPT_BLOCKS
    wanted = jnp.arange(prompt_count, dtype=jnp.int32)
    code = jnp.where(held_place < PROMPT_BLOCKS, held_seq * PROMPT_BLOCKS + held_place, -1)
    prompt_at = jnp.sum(
        jnp.where(
            code[None, :] == wanted[:, None], jnp.arange(held.shape[0], dtype=jnp.int32)[None, :], 0
        ),
        axis=1,
    ).astype(jnp.int32)
    own_blocks = heads * my_blocks
    tables = (held_seq[:own_blocks], held_place[:own_blocks], prompt_at)
    head_order = ((head_rank + jnp.arange(heads)) % heads).astype(jnp.int32)

    def head_shift(value, by):
        if by == 0:
            return value
        return lax.ppermute(
            value,
            "seq",
            [
                (h * group + j, ((h + by) % heads) * group + j)
                for h in range(heads)
                for j in range(group)
            ],
        )

    def group_shift(value, by):
        return lax.ppermute(
            value,
            "seq",
            [
                (h * group + j, h * group + (j + by) % group)
                for h in range(heads)
                for j in range(group)
            ],
        )

    own = lambda value, i: value[i * part : (i + 1) * part].astype(F32)
    x = jnp.concatenate(
        [x_parts[mask][which * part : (which + 1) * part] for mask, which in runs], axis=0
    )
    gain = lax.dynamic_slice_in_dim(norm_gain_table[:2], tp_rank * cols, cols, 1)
    pick3 = jnp.tile(select, (1, 3))
    latents = (mm(x, a_qkv) * pick3).astype(BF16)
    z, squares = qkv_product(
        x, latents, first, first[:, k_rows : k_rows + rank_cols].reshape(slots_a, 3 * cols), k_rows, cols
    )
    squares = sum_rows(squares[:2].reshape(2, rows), tp)
    inv = lax.rsqrt(squares / width + EPS)
    spread = spread_heads(head_order, piece_at, z, inv.T, cs, gain, heads)
    near = [head_shift(spread[heads + k], k) for k in range(heads)]
    queries = [head_shift(spread[k], k) for k in range(heads)]
    far = [group_shift(near[k], -j) for j in range(1, group) for k in range(heads)]
    attended = attend(tables, queries, near, far, prompt_count)
    heads_out = collect_heads(
        head_order, piece_at, [head_shift(attended[k], -k) for k in range(heads)]
    )

    def norm_back(values_in, inv, scaled):
        return inv * scaled - values_in * inv**3 * jnp.mean(scaled * values_in, axis=1, keepdims=True)

    def inverse_norm(values_in):
        return lax.rsqrt(jnp.mean(values_in * values_in, axis=1, keepdims=True) + EPS)

    *far_part, o_latent1 = add_product(heads_out[1], w_o, a_o, b_od[0], selects[1], 2)
    near_part, o_latent0 = add_product(heads_out[0], w_o, a_o, b_od[0], selects[0], 1)
    attn_out = scatter_groups(near_part, far_part, tp)
    scale_o = [inverse_norm(value) for value in attn_out]
    hidden = [
        own(layer_input, i) + attn_out[i] * scale_o[i] * norm_gain_table[2] for i in groups
    ]
    h_low = gather_groups([value.astype(BF16) for value in hidden], tp)

    gates, ups, acts, gu_latents = zip(
        *[gate_up_product(h_low[g], w_gu, a_gu, b_gu, selects[g]) for g in groups]
    )
    *far_part, d_latent1 = add_product(acts[1], w_down, a_down, b_od[1], selects[1], 2)
    near_part, d_latent0 = add_product(acts[0], w_down, a_down, b_od[1], selects[0], 1)
    ff_out = scatter_groups(near_part, far_part, tp)
    scale_f = [inverse_norm(value) for value in ff_out]
    output = jnp.concatenate(
        [hidden[i] + ff_out[i] * scale_f[i] * norm_gain_table[3] for i in groups], axis=0
    )

    d_ffs = gather_groups(
        [
            norm_back(ff_out[i], scale_f[i], own(cotangent, i) * norm_gain_table[3]).astype(BF16)
            for i in groups
        ],
        tp,
    )
    backs = [
        ff_back(
            d_ffs[g], b_od[1], selects[g], w_down, a_down, gates[g], ups[g], w_gu, b_gu, a_gu, 1 + g
        )
        for g in groups
    ]
    summed = scatter_groups(backs[0][0], backs[1][:2], tp)
    d_gates, d_ups, u_gus, u_downs = zip(*[back[-4:] for back in backs])
    d_hidden = [own(cotangent, i) + summed[i] for i in groups]
    d_attn = [
        norm_back(attn_out[i], scale_o[i], d_hidden[i] * norm_gain_table[2]).astype(BF16)
        for i in groups
    ]
    d_latents = (d_latent0, d_latent1)
    both_groups = lambda f: f(0) + f(1)
    grad_a_down = both_groups(lambda g: mm_tn(u_downs[g], acts[g]))
    grad_b_down = both_groups(lambda g: mm_tn(d_latents[g], d_ffs[g]))
    grad_a_gu = both_groups(lambda g: mm_tn(h_low[g], u_gus[g]))
    grad_b_gate = both_groups(lambda g: mm_tn(gu_latents[g][:, :slots_a], d_gates[g]))
    grad_b_up = both_groups(lambda g: mm_tn(gu_latents[g][:, slots_a:], d_ups[g]))
    lane = 2 * slots_a
    shards = lambda value: value.astype(BF16).reshape(seqs, -1, lane)
    early = jnp.concatenate(
        [
            shards(grad_a_gu),
            shards(grad_b_down),
            shards(grad_a_down),
            shards(grad_b_gate),
            shards(grad_b_up),
        ],
        axis=1,
    )

    *d_rows, early = gather_groups(d_attn, tp, early)
    early = lax.psum_scatter(early, "seq", scatter_dimension=0, tiled=False)
    o_latents = (o_latent0, o_latent1)
    u_os, grads = [], []
    for g in groups:
        u_os.append((mm_nt(d_rows[g], b_od[0]) * selects[g]).astype(BF16))
        d_heads = (mm(d_rows[g], w_o) + mm_nt(u_os[g], a_o)).astype(BF16)
        grads.append(
            [
                head_shift(
                    lax.dynamic_slice_in_dim(d_heads, head_order[k] * HEAD_DIM, HEAD_DIM, 1), k
                )
                for k in range(heads)
            ]
        )
    grad_a_o = both_groups(lambda g: mm_tn(u_os[g], heads_out[g]))
    grad_b_o = both_groups(lambda g: mm_tn(o_latents[g], d_rows[g]))
    late_o = jnp.concatenate(
        [
            grad_b_o.astype(BF16).reshape(seqs, -1, cols),
            grad_a_o.astype(BF16).reshape(seqs, -1, cols),
        ],
        axis=1,
    )
    late_o = scatter_order(late_o, "seq", seqs, seq_order)
    grads = [grads[g][k] for k in range(heads) for g in groups]
    grads[-1], early = lax.optimization_barrier((grads[-1], early))
    results = list(attend_back(tables, piece_at, queries, near, far, grads, prompt_count))
    dqs = [head_shift(results[k], -k) for k in range(heads)]
    d_kv = results[heads].reshape(2, heads, rows, HEAD_DIM)
    others = [
        group_shift(results[heads + j], j).reshape(2, heads, rows, HEAD_DIM) for j in range(1, group)
    ]
    dkvs = []
    for k in range(heads):
        total = d_kv[:, k].astype(F32)
        for other in others:
            total = total + other[:, k].astype(F32)
        dkvs.append(head_shift(total.astype(BF16), -k))
    scaled, parts = unturn_heads(head_order, piece_at, dqs, dkvs, z, cs, gain)
    parts = sum_rows(parts.T, tp) / width
    coef = jnp.concatenate([inv, inv**3 * parts], axis=0)
    dz = norm_back_heads(head_order, piece_at, dkvs, scaled, z, coef.T)
    us = (mm_nt(dz, b_qkv) * pick3).astype(BF16)
    far_part = list(back_product(dz, 1, first, k_rows, us, a_qkv, 2))
    far_part[0], us = lax.optimization_barrier((far_part[0], us))
    grad_a_qkv = mm_tn(x, us)
    grad_b_qkv = mm_tn(latents, dz)
    lane3 = 3 * slots_a
    grad_b_qkv = jnp.concatenate(
        [
            grad_b_qkv[i * slots_a : (i + 1) * slots_a, i * cols : (i + 1) * cols]
            for i in range(3)
        ],
        axis=1,
    )
    late = jnp.concatenate(
        [
            grad_a_qkv.astype(BF16).reshape(seqs, k_rows, lane3),
            grad_b_qkv.astype(BF16).reshape(seqs, -1, lane3),
        ],
        axis=1,
    )
    dz, late = lax.optimization_barrier((dz, late))
    (near_part,) = back_product(dz, 0, first, k_rows, us, a_qkv, 1)
    summed = scatter_groups(near_part, far_part, tp)
    input_grad = jnp.concatenate([d_hidden[i] + summed[i] for i in groups], axis=0)

    late = scatter_order(late, "seq", seqs, seq_order)
    sum_tp = lambda value: sum_all(value.astype(BF16), "tp", tp).astype(F32)
    grad_a_qkv = sum_tp(late[:k_rows])
    grad_b_qkv = late[k_rows:].reshape(rank_cols, 3, cols).transpose(1, 0, 2)
    down_size = rank_cols * width // lane
    both = sum_tp(early[: k_rows + down_size])
    grad_a_gu, grad_b_down = both[:k_rows], both[k_rows:].reshape(rank_cols, width)
    a_size = rank_cols * hidden_cols // lane
    rest = early[k_rows + down_size :].astype(F32)
    grad_a_down = rest[:a_size].reshape(rank_cols, hidden_cols).T
    grad_b_gu = rest[a_size:].reshape(2, rank_cols, hidden_cols)
    o_size = rank_cols * width // cols
    grad_b_o = sum_tp(late_o[:o_size]).reshape(rank_cols, width)
    grad_a_o = late_o[o_size:].T
    grad_a_in = jnp.stack(
        [grad_a_qkv[:, i * slots_a : (i + 1) * slots_a] for i in range(3)]
        + [grad_a_gu[:, i * slots_a : (i + 1) * slots_a] for i in range(2)]
    )
    grad_b_out = jnp.stack([grad_b_o, grad_b_down])
    return (output, input_grad, grad_a_in, grad_a_o, grad_a_down, grad_b_qkv, grad_b_gu, grad_b_out)


def solution(mesh):
    return jax.shard_map(
        local,
        mesh=mesh,
        in_specs=(
            P(("seq", "tp"), None),
            P(("seq", "tp"), None),
            P(None, "seq", "tp"),
            P("tp", "seq"),
            P(None, "seq", "tp"),
            P("tp", "seq"),
            P(None, "seq", None),
            P("tp", "seq"),
            P("tp", "seq"),
            P(None, "seq", "tp"),
            P(None, "seq", "tp"),
            P(None, "seq", None),
            P(),
            P(),
            P(),
            P(),
        ),
        out_specs=(
            P(("seq", "tp"), None),
            P(("seq", "tp"), None),
            P(None, "seq", None),
            P("tp", "seq"),
            P("tp", "seq"),
            P(None, "seq", "tp"),
            P(None, "seq", "tp"),
            P(None, "seq", None),
        ),
        check_vma=False,
    )
```

```python
import functools

import jax
import jax.numpy as jnp
from jax import lax
from jax.experimental import pallas as pl
from jax.experimental.pallas import tpu as pltpu
from jax.sharding import PartitionSpec as P

HEAD_DIM = 128
ADAPTER_RANK = 16
BLK = 128
PROMPT_BLOCKS = 8
EPS = 1e-06
THETA = 500000.0
NEG = -1e30
LOG2E = 1.4426950408889634
F32 = jnp.float32
BF16 = jnp.bfloat16


def mm(a, b):
    return jnp.dot(a, b, preferred_element_type=F32)


def mm_nt(a, b):
    return lax.dot_general(a, b, (((1,), (1,)), ((), ())), preferred_element_type=F32)


def mm_tn(a, b):
    return lax.dot_general(a, b, (((0,), (0,)), ((), ())), preferred_element_type=F32)


def bits_of(count):
    n = count.bit_length() - 1
    assert 1 << n == count
    return n


def flip(value, axis, count, bit):
    return lax.ppermute(value, axis, [(i, i ^ (1 << bit)) for i in range(count)])


def gather_order(value, axis, count, order):
    rank = lax.axis_index(axis)
    have = []
    current = value
    for bit in order:
        other = flip(current, axis, count, bit)
        mine_low = ((rank >> bit) & 1) == 0
        at = len([b for b in have if b > bit])
        low = jnp.where(mine_low, current, other)
        high = jnp.where(mine_low, other, current)
        current = jnp.stack([low, high], axis=at)
        have = sorted(have + [bit], reverse=True)
    return current.reshape((count,) + value.shape)


def scatter_order(value, axis, count, order):
    n = bits_of(count)
    rank = lax.axis_index(axis)
    current = value.reshape((2,) * n + value.shape[1:])
    have = list(range(n - 1, -1, -1))
    for bit in order:
        at = have.index(bit)
        mine = (rank >> bit) & 1
        keep = lax.dynamic_index_in_dim(current, mine, at, keepdims=False)
        give = lax.dynamic_index_in_dim(current, 1 - mine, at, keepdims=False)
        got = flip(give.astype(BF16), axis, count, bit)
        current = keep.astype(F32) + got.astype(F32)
        have.remove(bit)
    return current


def part_orders(count):
    order = list(range(bits_of(count)))
    return (order, order[::-1])


def group_masks(count):
    groups = ([], [])
    for part, order in enumerate(part_orders(count)):
        for j in range(count):
            mask = sum(1 << bit for i, bit in enumerate(order) if (j >> i) & 1)
            groups[j >= count // 2].append((mask, part))
    return groups


def row_runs(count):
    return [run for masks in group_masks(count) for run in masks]


def gather_groups(parts, count, beside=None):
    near, far = [], []
    for value, order in zip(parts, part_orders(count)):
        for bit in order[:-1]:
            value = jnp.concatenate([value, flip(value, "tp", count, bit)], axis=0)
        near.append(value)
    if beside is not None:
        near[1], beside = lax.optimization_barrier((near[1], beside))
    for value, order in zip(near, part_orders(count)):
        far.append(flip(value, "tp", count, order[-1]))
    if beside is not None:
        return jnp.concatenate(near, axis=0), jnp.concatenate(far, axis=0), beside
    return jnp.concatenate(near, axis=0), jnp.concatenate(far, axis=0)


def scatter_groups(near, far, count):
    out = []
    size = near.shape[0] // 2
    for i, order in enumerate(part_orders(count)):
        got = flip(far[i], "tp", count, order[-1])
        total = near[i * size : (i + 1) * size].astype(F32) + got.astype(F32)
        for bit in order[-2::-1]:
            half = total.shape[0] // 2
            got = flip(total[half:].astype(BF16), "tp", count, bit)
            total = total[:half] + got.astype(F32)
        out.append(total)
    return out


def sum_rows(value, count):
    runs = row_runs(count)
    value = value.reshape(value.shape[0], len(runs), -1)
    total = value
    for mask in range(1, count):
        got = lax.ppermute(value, "tp", [(i, i ^ mask) for i in range(count)])
        order = [runs.index((other ^ mask, which)) for other, which in runs]
        total = total + jnp.concatenate([got[:, j : j + 1] for j in order], axis=1)
    return total.reshape(value.shape[0], -1)


def sum_all(value, axis, count):
    for bit in range(bits_of(count)):
        value = value + flip(value, axis, count, bit)
    return value


def copy_all(pairs, sem):
    copies = [pltpu.make_async_copy(src, dst, sem.at[i]) for i, (src, dst) in enumerate(pairs)]
    for copy in copies:
        copy.start()
    for copy in copies:
        copy.wait()


def gather_prompt(prompt_at, source, target, count):
    def step(i, carry):
        start = pl.multiple_of(prompt_at[i] * BLK, BLK)
        target[pl.ds(pl.multiple_of(i * BLK, BLK), BLK), :] = source[pl.ds(start, BLK), :]
        return carry

    lax.fori_loop(0, count, step, 0)


def masked_scores(keys, own_keys, queries, place, scale):
    prompt = mm_nt(keys, queries) * scale
    block = lax.broadcasted_iota(jnp.int32, prompt.shape, 0) // BLK
    prompt = jnp.where(block < place, prompt, NEG)
    own = mm_nt(own_keys, queries) * scale
    causal = lax.broadcasted_iota(jnp.int32, own.shape, 0) <= lax.broadcasted_iota(
        jnp.int32, own.shape, 1
    )
    own = jnp.where(causal, own, NEG)
    top = jnp.maximum(jnp.max(prompt, axis=0, keepdims=True), jnp.max(own, axis=0, keepdims=True))
    prompt = jnp.exp2(prompt - top)
    own = jnp.exp2(own - top)
    total = jnp.sum(prompt, axis=0, keepdims=True) + jnp.sum(own, axis=0, keepdims=True)
    return prompt, own, 1.0 / total


def load_plan(slots, group, rows, refs, q_buf, k_buf, v_buf):
    plan = []
    for i in range(slots):
        plan.append((refs[i], q_buf.at[pl.ds(i * rows, rows)]))
    for i in range(slots * group):
        at = pl.ds(i * rows, rows)
        ref = refs[slots + i]
        plan += [(ref.at[0], k_buf.at[at]), (ref.at[1], v_buf.at[at])]
    return plan


def attend_kernel(slots, group, rows, prompt_count, q_seq, q_place, prompt_at, *refs):
    n_in = slots + slots * group
    outs = refs[n_in : n_in + slots]
    q_buf, k_buf, v_buf, kp, vp, o_buf, sem = refs[n_in + slots :]
    copy_all(load_plan(slots, group, rows, refs, q_buf, k_buf, v_buf), sem)
    gather_prompt(prompt_at, k_buf, kp, prompt_count)
    gather_prompt(prompt_at, v_buf, vp, prompt_count)
    scale = HEAD_DIM ** (-0.5) * LOG2E
    span = PROMPT_BLOCKS * BLK

    def step(i, carry):
        at = pl.ds(pl.multiple_of(i * BLK, BLK), BLK)
        of_seq = pl.ds(pl.multiple_of(q_seq[i] * span, span), span)
        prompt, own, inverse = masked_scores(
            kp[of_seq, :], k_buf[at, :], q_buf[at, :], q_place[i], scale
        )
        result = mm_tn(vp[of_seq, :], prompt.astype(BF16)) + mm_tn(v_buf[at, :], own.astype(BF16))
        o_buf[at, :] = (result * inverse).T.astype(BF16)
        return carry

    lax.fori_loop(0, slots * rows // BLK, step, 0)
    copy_all([(o_buf.at[pl.ds(i * rows, rows)], outs[i]) for i in range(slots)], sem)


def attend_back_kernel(
    slots, group, rows, pieces, prompt_count, q_seq, q_place, prompt_at, piece_at, *refs
):
    n_in = slots + slots * group
    n_grad = slots * 2
    grads = refs[n_in : n_in + n_grad]
    outs = refs[n_in + n_grad : n_in + n_grad + slots]
    near_out = refs[n_in + n_grad + slots]
    rest = refs[n_in + n_grad + slots + 1 :]
    far_outs, rest = rest[: group - 1], rest[group - 1 :]
    q_buf, k_buf, v_buf, do_buf, kp, vp, dkp, dvp, dq_buf, dkv_buf, sem = rest
    plan = load_plan(slots, group, rows, refs, q_buf, k_buf, v_buf)
    size = rows // pieces
    for i in range(slots):
        for p in range(pieces):
            half, at = divmod(p, pieces // 2)
            to = pl.multiple_of(i * rows + piece_at[p] * size, 16)
            plan.append(
                (grads[i * 2 + half].at[pl.ds(at * size, size)], do_buf.at[pl.ds(to, size)])
            )
    copy_all(plan, sem)
    gather_prompt(prompt_at, k_buf, kp, prompt_count)
    gather_prompt(prompt_at, v_buf, vp, prompt_count)
    dkp[...] = jnp.zeros_like(dkp)
    dvp[...] = jnp.zeros_like(dvp)
    scale = HEAD_DIM ** (-0.5)
    span = PROMPT_BLOCKS * BLK
    own_rows = slots * rows
    zeros = jnp.zeros((BLK, HEAD_DIM), BF16)

    def rows_of(i):
        return pl.ds(pl.multiple_of(i * BLK, BLK), BLK)

    def clear(i, carry):
        for j in range(1, group):
            dkv_buf[j, 0, rows_of(i), :] = zeros
            dkv_buf[j, 1, rows_of(i), :] = zeros
        return carry

    lax.fori_loop(0, own_rows // BLK, clear, 0)

    def step(i, carry):
        at = rows_of(i)
        seq, place = q_seq[i], q_place[i]
        of_seq = pl.ds(pl.multiple_of(seq * span, span), span)
        queries, grad = q_buf[at, :], do_buf[at, :]
        prompt, own, inverse = masked_scores(
            kp[of_seq, :], k_buf[at, :], queries, place, scale * LOG2E
        )
        prompt, own = prompt * inverse, own * inverse
        d_prompt = mm_nt(vp[of_seq, :], grad)
        d_own = mm_nt(v_buf[at, :], grad)
        delta = jnp.sum(prompt * d_prompt, axis=0, keepdims=True) + jnp.sum(
            own * d_own, axis=0, keepdims=True
        )
        ds_prompt = (prompt * (d_prompt - delta)).astype(BF16)
        ds_own = (own * (d_own - delta)).astype(BF16)
        dq = mm_tn(ds_prompt, kp[of_seq, :]) + mm_tn(ds_own, k_buf[at, :])
        dq_buf[at, :] = (dq * scale).astype(BF16)
        dvp[of_seq, :] += mm(prompt.astype(BF16), grad)
        dkp[of_seq, :] += mm(ds_prompt, queries) * scale
        dkv_buf[0, 0, at, :] = (mm(ds_own, queries) * scale).astype(BF16)
        dkv_buf[0, 1, at, :] = mm(own.astype(BF16), grad).astype(BF16)
        return carry

    lax.fori_loop(0, own_rows // BLK, step, 0)
    blocks = own_rows // BLK

    def spread(i, carry):
        place = prompt_at[i]
        j, to = place // blocks, rows_of(place % blocks)
        dkv_buf[j, 0, to, :] = (dkv_buf[j, 0, to, :].astype(F32) + dkp[rows_of(i), :]).astype(BF16)
        dkv_buf[j, 1, to, :] = (dkv_buf[j, 1, to, :].astype(F32) + dvp[rows_of(i), :]).astype(BF16)
        return carry

    lax.fori_loop(0, prompt_count, spread, 0)
    plan = [(dq_buf.at[pl.ds(i * rows, rows)], outs[i]) for i in range(slots)]
    plan.append((dkv_buf.at[0], near_out))
    plan += [(dkv_buf.at[j], far_outs[j - 1]) for j in range(1, group)]
    copy_all(plan, sem)


ANY = pl.BlockSpec(memory_space=pl.ANY)


def attend(tables, queries, near, far, prompt_count):
    slots = len(near)
    rows = queries[0].shape[0]
    group = 1 + len(far) // slots
    own, every = slots * rows, slots * group * rows
    pairs = own * (PROMPT_BLOCKS + 1) * BLK
    wide = lambda count, kind=BF16: pltpu.VMEM((count, HEAD_DIM), kind)
    return pl.pallas_call(
        functools.partial(attend_kernel, slots, group, rows, prompt_count),
        out_shape=[jax.ShapeDtypeStruct((rows, HEAD_DIM), BF16)] * slots,
        grid_spec=pltpu.PrefetchScalarGridSpec(
            num_scalar_prefetch=3,
            in_specs=[ANY] * (slots + slots * group),
            out_specs=[ANY] * slots,
            scratch_shapes=[
                wide(own),
                wide(every),
                wide(every),
                wide(prompt_count * BLK),
                wide(prompt_count * BLK),
                wide(own),
                pltpu.SemaphoreType.DMA((slots + 2 * slots * group,)),
            ],
        ),
        cost_estimate=pl.CostEstimate(
            flops=4 * pairs * HEAD_DIM, bytes_accessed=6 * every * HEAD_DIM, transcendentals=pairs
        ),
        name="attend",
    )(*tables, *queries, *near, *far)


def attend_back(tables, piece_at, queries, near, far, grads, prompt_count):
    pieces = piece_at.shape[0]
    slots = len(near)
    rows = queries[0].shape[0]
    group = 1 + len(far) // slots
    own, every = slots * rows, slots * group * rows
    pairs = own * (PROMPT_BLOCKS + 1) * BLK
    wide = lambda count, kind=BF16: pltpu.VMEM((count, HEAD_DIM), kind)
    return pl.pallas_call(
        functools.partial(attend_back_kernel, slots, group, rows, pieces, prompt_count),
        out_shape=[jax.ShapeDtypeStruct((rows, HEAD_DIM), BF16)] * slots
        + [jax.ShapeDtypeStruct((2, own, HEAD_DIM), BF16)] * group,
        grid_spec=pltpu.PrefetchScalarGridSpec(
            num_scalar_prefetch=4,
            in_specs=[ANY] * (slots + slots * group + 2 * slots),
            out_specs=[ANY] * (slots + group),
            scratch_shapes=[
                wide(own),
                wide(every),
                wide(every),
                wide(own),
                wide(prompt_count * BLK),
                wide(prompt_count * BLK),
                wide(prompt_count * BLK, F32),
                wide(prompt_count * BLK, F32),
                wide(own),
                pltpu.VMEM((group, 2, own, HEAD_DIM), BF16),
                pltpu.SemaphoreType.DMA((slots + 2 * slots * group + slots * pieces,)),
            ],
        ),
        cost_estimate=pl.CostEstimate(
            flops=10 * pairs * HEAD_DIM, bytes_accessed=12 * every * HEAD_DIM, transcendentals=pairs
        ),
        name="attend_back",
    )(*tables, piece_at, *queries, *near, *far, *grads)


def turn(values, cosine, sine):
    return values * cosine + pltpu.roll(values, HEAD_DIM // 2, 1) * sine


def lanes(head, base=0):
    return pl.ds(pl.multiple_of(base + head * HEAD_DIM, HEAD_DIM), HEAD_DIM)


def piece_rows(index, size):
    return pl.ds(pl.multiple_of(index * size, 16), size)


def spread_kernel(slots, pieces, order, piece_at, z, inv, cs, gain, *outs):
    cols = slots * HEAD_DIM
    size = z.shape[0] // pieces

    def step(p, carry):
        at, to = piece_rows(p, size), piece_rows(piece_at[p], size)
        cosine, sine = cs[at, :HEAD_DIM], cs[at, HEAD_DIM:]
        for which in range(2):
            factor = inv[at, which : which + 1]
            for k in range(slots):
                head = order[k]
                scaled = z[at, lanes(head, which * cols)] * factor
                scaled = scaled * gain[which : which + 1, lanes(head)]
                turned = turn(scaled, cosine, sine).astype(BF16)
                if which == 0:
                    outs[k][to, :] = turned
                else:
                    outs[slots + k][0, to, :] = turned
        for k in range(slots):
            outs[slots + k][1, to, :] = z[at, lanes(order[k], 2 * cols)].astype(BF16)
        return carry

    lax.fori_loop(0, pieces, step, 0)


WHOLE = pl.BlockSpec(memory_space=pltpu.VMEM)
BIG = pltpu.CompilerParams(vmem_limit_bytes=56 * 1024 * 1024)


def spread_heads(order, piece_at, z, inv, cs, gain, slots):
    rows = z.shape[0]
    return pl.pallas_call(
        functools.partial(spread_kernel, slots, piece_at.shape[0]),
        out_shape=[jax.ShapeDtypeStruct((rows, HEAD_DIM), BF16)] * slots
        + [jax.ShapeDtypeStruct((2, rows, HEAD_DIM), BF16)] * slots,
        grid_spec=pltpu.PrefetchScalarGridSpec(
            num_scalar_prefetch=2, in_specs=[WHOLE] * 4, out_specs=[WHOLE] * (2 * slots)
        ),
        compiler_params=BIG,
        name="spread_heads",
    )(order, piece_at, z, inv, cs, gain)


def collect_kernel(slots, pieces, order, piece_at, *refs):
    outs = refs[slots:]
    size = refs[0].shape[0] // pieces
    for p in range(pieces):
        half, at = divmod(p, pieces // 2)
        for k in range(slots):
            outs[half][pl.ds(at * size, size), lanes(order[k])] = refs[k][
                piece_rows(piece_at[p], size), :
            ]


def collect_heads(order, piece_at, parts):
    slots = len(parts)
    rows = parts[0].shape[0]
    return pl.pallas_call(
        functools.partial(collect_kernel, slots, piece_at.shape[0]),
        out_shape=[jax.ShapeDtypeStruct((rows // 2, slots * HEAD_DIM), BF16)] * 2,
        grid_spec=pltpu.PrefetchScalarGridSpec(
            num_scalar_prefetch=2, in_specs=[WHOLE] * slots, out_specs=[WHOLE] * 2
        ),
        name="collect_heads",
    )(order, piece_at, *parts)


def unturn_kernel(slots, pieces, order, piece_at, *refs):
    dqs, dkvs, rest = refs[:slots], refs[slots : 2 * slots], refs[2 * slots :]
    z, cs, gain, scaled_out, part_out = rest
    cols = slots * HEAD_DIM
    size = z.shape[0] // pieces

    def step(p, carry):
        at, source = piece_rows(p, size), piece_rows(piece_at[p], size)
        cosine, sine = cs[at, :HEAD_DIM], cs[at, HEAD_DIM:]
        for which in range(2):
            total = jnp.zeros((size, HEAD_DIM), F32)
            for k in range(slots):
                head = order[k]
                grad = dqs[k][source, :] if which == 0 else dkvs[k][0, source, :]
                grad = turn(grad.astype(F32), cosine, -sine) * gain[which : which + 1, lanes(head)]
                scaled_out[at, lanes(head, which * cols)] = grad
                total = total + grad * z[at, lanes(head, which * cols)]
            part_out[at, which : which + 1] = jnp.sum(total, axis=1, keepdims=True)
        return carry

    lax.fori_loop(0, pieces, step, 0)


def unturn_heads(order, piece_at, dqs, dkvs, z, cs, gain):
    slots = len(dqs)
    rows = z.shape[0]
    cols = slots * HEAD_DIM
    return pl.pallas_call(
        functools.partial(unturn_kernel, slots, piece_at.shape[0]),
        out_shape=[
            jax.ShapeDtypeStruct((rows, 2 * cols), F32),
            jax.ShapeDtypeStruct((rows, 2), F32),
        ],
        grid_spec=pltpu.PrefetchScalarGridSpec(
            num_scalar_prefetch=2, in_specs=[WHOLE] * (2 * slots + 3), out_specs=[WHOLE] * 2
        ),
        compiler_params=BIG,
        name="unturn_heads",
    )(order, piece_at, *dqs, *dkvs, z, cs, gain)


def norm_back_kernel(slots, pieces, order, piece_at, *refs):
    dkvs, (scaled, z, coef, out) = refs[:slots], refs[slots:]
    cols = slots * HEAD_DIM
    size = z.shape[0] // pieces

    def step(p, carry):
        at, source = piece_rows(p, size), piece_rows(piece_at[p], size)
        for which in range(2):
            to = slice(which * cols, (which + 1) * cols)
            out[at, to] = (
                scaled[at, to] * coef[at, which : which + 1]
                - z[at, to] * coef[at, 2 + which : 3 + which]
            ).astype(BF16)
        for k in range(slots):
            out[at, lanes(order[k], 2 * cols)] = dkvs[k][1, source, :]
        return carry

    lax.fori_loop(0, pieces, step, 0)


def norm_back_heads(order, piece_at, dkvs, scaled, z, coef):
    slots = len(dkvs)
    return pl.pallas_call(
        functools.partial(norm_back_kernel, slots, piece_at.shape[0]),
        out_shape=jax.ShapeDtypeStruct(z.shape, BF16),
        grid_spec=pltpu.PrefetchScalarGridSpec(
            num_scalar_prefetch=2, in_specs=[WHOLE] * (slots + 3), out_specs=WHOLE
        ),
        compiler_params=BIG,
        name="norm_back_heads",
    )(order, piece_at, *dkvs, scaled, z, coef)


def fixed(*shape, at=None):
    place = at or (0,) * len(shape)
    return pl.BlockSpec(shape, lambda i: place)


def flat(value):
    return value.reshape(-1, value.shape[-1])


def qkv_kernel(x, latent, weight, second, z, squares):
    i = pl.program_id(0)
    result = mm(x[...], flat(weight[...])) + mm(latent[...], flat(second[...]))
    z[...] = result
    squares[0, :, :] = jnp.sum(result * result, axis=1, keepdims=True)


def qkv_product(x, latents, first, second, k_rows, cols):
    rows, width = x.shape
    shards, _, total = first.shape
    low = latents.shape[1] // 3
    return pl.pallas_call(
        qkv_kernel,
        grid=(3,),
        out_shape=[
            jax.ShapeDtypeStruct((rows, total), F32),
            jax.ShapeDtypeStruct((3, rows, 1), F32),
        ],
        in_specs=[
            fixed(rows, width),
            pl.BlockSpec((rows, low), lambda i: (0, i)),
            pl.BlockSpec((shards, k_rows, cols), lambda i: (0, 0, i)),
            pl.BlockSpec((low, cols), lambda i: (0, i)),
        ],
        out_specs=[
            pl.BlockSpec((rows, cols), lambda i: (0, i)),
            pl.BlockSpec((1, rows, 1), lambda i: (i, 0, 0)),
        ],
        compiler_params=BIG,
        cost_estimate=pl.CostEstimate(
            flops=2 * rows * width * total, bytes_accessed=2 * first.size, transcendentals=0
        ),
        name="qkv_product",
    )(x, latents, first, second)


def add_kernel(parts, a, weight, first, second, pick, *refs):
    outs, (latent_out, latent) = refs[:parts], refs[parts:]

    @pl.when(pl.program_id(0) == 0)
    def _():
        latent[...] = (mm(a[...], first[...]) * pick[...]).astype(BF16)
        latent_out[...] = latent[...]

    result = mm_nt(a[...], weight[...]) + mm(latent[...], second[...])
    size = result.shape[0] // parts
    for i in range(parts):
        outs[i][...] = result[i * size : (i + 1) * size].astype(BF16)


def add_product(a, weight, first, second, pick, parts, tile=512):
    rows, depth = a.shape
    width, low = weight.shape[0], first.shape[1]
    size = rows // parts
    return pl.pallas_call(
        functools.partial(add_kernel, parts),
        grid=(width // tile,),
        out_shape=[jax.ShapeDtypeStruct((size, width), BF16)] * parts
        + [jax.ShapeDtypeStruct((rows, low), BF16)],
        in_specs=[
            fixed(rows, depth),
            pl.BlockSpec((tile, depth), lambda i: (i, 0)),
            fixed(depth, low),
            pl.BlockSpec((low, tile), lambda i: (0, i)),
            fixed(rows, low),
        ],
        out_specs=[pl.BlockSpec((size, tile), lambda i: (0, i))] * parts + [fixed(rows, low)],
        scratch_shapes=[pltpu.VMEM((rows, low), BF16)],
        compiler_params=BIG,
        cost_estimate=pl.CostEstimate(
            flops=2 * rows * width * depth, bytes_accessed=2 * weight.size, transcendentals=0
        ),
        name="add_product",
    )(a, weight, first, second, pick)


def back_kernel(parts, a, weight, u, first, *outs):
    result = mm_nt(a[...], flat(weight[...])) + mm_nt(u[...], first[...])
    size = result.shape[0] // parts
    for i in range(parts):
        outs[i][...] = result[i * size : (i + 1) * size].astype(BF16)


def back_product(a, group, weight, k_rows, u, first, parts):
    rows, depth = a.shape
    rows //= 2
    shards = weight.shape[0]
    width, low = first.shape
    per = max(1, 512 // k_rows)
    size = rows // parts
    return pl.pallas_call(
        functools.partial(back_kernel, parts),
        grid=(shards // per,),
        out_shape=[jax.ShapeDtypeStruct((size, width), BF16)] * parts,
        in_specs=[
            fixed(rows, depth, at=(group, 0)),
            pl.BlockSpec((per, k_rows, depth), lambda i: (i, 0, 0)),
            fixed(rows, low, at=(group, 0)),
            pl.BlockSpec((per * k_rows, low), lambda i: (i, 0)),
        ],
        out_specs=[pl.BlockSpec((size, per * k_rows), lambda i: (0, i))] * parts,
        compiler_params=BIG,
        cost_estimate=pl.CostEstimate(
            flops=2 * rows * width * depth, bytes_accessed=2 * width * depth, transcendentals=0
        ),
        name="back_product",
    )(a, weight, u, first)


def gate_up_kernel(h, first, pick, w_g, w_u, b_g, b_u, gate_out, up_out, act, latent_out, latent):
    low = pick.shape[1]

    @pl.when(pl.program_id(0) == 0)
    def _():
        both = mm(h[...], first[...])
        latent[:, :low] = (both[:, :low] * pick[...]).astype(BF16)
        latent[:, low:] = (both[:, low:] * pick[...]).astype(BF16)
        latent_out[...] = latent[...]

    gate = mm(h[...], w_g[...]) + mm(latent[:, :low], b_g[...])
    up = mm(h[...], w_u[...]) + mm(latent[:, low:], b_u[...])
    gate_out[...] = gate
    up_out[...] = up
    act[...] = (gate / (1.0 + jnp.exp(-gate)) * up).astype(BF16)


def gate_up_product(h, w_gu, a_gu, b_gu, pick, tile=512):
    rows, width = h.shape
    units, low = w_gu.shape[1] // 2, pick.shape[1]
    n = units // tile
    left = lambda depth: pl.BlockSpec((depth, tile), lambda i: (0, i))
    out = pl.BlockSpec((rows, tile), lambda i: (0, i))
    return pl.pallas_call(
        gate_up_kernel,
        grid=(n,),
        out_shape=[jax.ShapeDtypeStruct((rows, units), F32)] * 2
        + [
            jax.ShapeDtypeStruct((rows, units), BF16),
            jax.ShapeDtypeStruct((rows, 2 * low), BF16),
        ],
        in_specs=[
            fixed(rows, width),
            fixed(width, 2 * low),
            fixed(rows, low),
            left(width),
            pl.BlockSpec((width, tile), lambda i: (0, i + n)),
            left(low),
            pl.BlockSpec((low, tile), lambda i: (1, i)),
        ],
        out_specs=[out, out, out, fixed(rows, 2 * low)],
        scratch_shapes=[pltpu.VMEM((rows, 2 * low), BF16)],
        compiler_params=BIG,
        cost_estimate=pl.CostEstimate(
            flops=4 * rows * width * units, bytes_accessed=4 * width * units, transcendentals=0
        ),
        name="gate_up_product",
    )(h, a_gu, pick, w_gu, w_gu, b_gu, b_gu)


def ff_back_kernel(
    parts, steps, d_ff, b_down, pick, w_down, a_down, gate, up, w_g, w_u, b_g, b_u, a_gu, *refs
):
    outs, (d_gate_out, d_up_out, u_out, u_down_out, acc, u_g, u_u, u_down) = refs[:parts], refs[parts:]
    i = pl.program_id(0)

    @pl.when(i == 0)
    def _():
        u_down[...] = (mm_nt(d_ff[...], b_down[...]) * pick[...]).astype(BF16)
        u_down_out[...] = u_down[...]

    d_act = mm(d_ff[...], w_down[...]) + mm_nt(u_down[...], a_down[...])
    g = gate[...]
    sigmoid = 1.0 / (1.0 + jnp.exp(-g))
    silu = g * sigmoid
    d_gate = (d_act * up[...] * (sigmoid + silu * (1.0 - sigmoid))).astype(BF16)
    d_up = (d_act * silu).astype(BF16)
    d_gate_out[...] = d_gate
    d_up_out[...] = d_up
    part = mm_nt(d_gate, w_g[...]) + mm_nt(d_up, w_u[...])
    part_g, part_u = mm_nt(d_gate, b_g[...]), mm_nt(d_up, b_u[...])

    @pl.when(i == 0)
    def _():
        acc[...] = part
        u_g[...] = part_g
        u_u[...] = part_u

    @pl.when(i > 0)
    def _():
        acc[...] += part
        u_g[...] += part_g
        u_u[...] += part_u

    @pl.when(i == steps - 1)
    def _():
        low = pick.shape[1]
        last_g = (u_g[...] * pick[...]).astype(BF16)
        last_u = (u_u[...] * pick[...]).astype(BF16)
        u_out[:, :low] = last_g
        u_out[:, low:] = last_u
        size = acc.shape[0] // parts
        for p in range(parts):
            at = slice(p * size, (p + 1) * size)
            outs[p][...] = (
                acc[at, :]
                + mm_nt(last_g[at], a_gu[:, :low])
                + mm_nt(last_u[at], a_gu[:, low:])
            ).astype(BF16)


def ff_back(d_ff, b_down, pick, w_down, a_down, gate, up, w_gu, b_gu, a_gu, parts, tile=512):
    rows, width = d_ff.shape
    units, low = gate.shape[1], pick.shape[1]
    n = units // tile
    size = rows // parts
    column = lambda depth: pl.BlockSpec((depth, tile), lambda i: (0, i))
    return pl.pallas_call(
        functools.partial(ff_back_kernel, parts, n),
        grid=(n,),
        out_shape=[jax.ShapeDtypeStruct((size, width), BF16)] * parts
        + [jax.ShapeDtypeStruct((rows, units), BF16)] * 2
        + [
            jax.ShapeDtypeStruct((rows, 2 * low), BF16),
            jax.ShapeDtypeStruct((rows, low), BF16),
        ],
        in_specs=[
            fixed(rows, width),
            fixed(low, width),
            fixed(rows, low),
            column(width),
            pl.BlockSpec((tile, low), lambda i: (i, 0)),
            column(rows),
            column(rows),
            column(width),
            pl.BlockSpec((width, tile), lambda i: (0, i + n)),
            column(low),
            pl.BlockSpec((low, tile), lambda i: (1, i)),
            fixed(width, 2 * low),
        ],
        out_specs=[fixed(size, width)] * parts
        + [column(rows), column(rows), fixed(rows, 2 * low), fixed(rows, low)],
        scratch_shapes=[
            pltpu.VMEM((rows, width), F32),
            pltpu.VMEM((rows, low), F32),
            pltpu.VMEM((rows, low), F32),
            pltpu.VMEM((rows, low), BF16),
        ],
        compiler_params=BIG,
        cost_estimate=pl.CostEstimate(
            flops=6 * rows * width * units, bytes_accessed=6 * width * units, transcendentals=0
        ),
        name="ff_back",
    )(d_ff, b_down, pick, w_down, a_down, gate, up, w_gu, w_gu, b_gu, b_gu, a_gu)


def blocked(parts):
    zeros = lambda a, b: jnp.zeros((a.shape[0], b.shape[1]), a.dtype)
    return jnp.concatenate(
        [
            jnp.concatenate([a if a is b else zeros(a, b) for b in parts], axis=1)
            for a in parts
        ],
        axis=0,
    )


def local(
    layer_input,
    cotangent,
    query_key_value_weight,
    output_weight,
    gate_up_weight,
    down_weight,
    input_first_factor,
    output_first_factor,
    down_first_factor,
    query_key_value_second,
    gate_up_second_factor,
    output_down_second_factor,
    norm_gain_table,
    sequence_adapter,
    block_sequence,
    block_position,
):
    tp, tp_rank = lax.axis_size("tp"), lax.axis_index("tp")
    seqs, seq_rank = lax.axis_size("seq"), lax.axis_index("seq")
    own_rows, width = layer_input.shape
    rows = own_rows * tp
    part = own_rows // 2
    my_blocks = rows // BLK
    cols = query_key_value_weight.shape[2]
    heads = cols // HEAD_DIM
    hidden_cols = gate_up_weight.shape[2]
    k_rows = query_key_value_weight.shape[1]
    slots_a = input_first_factor.shape[2]
    rank_cols = output_first_factor.shape[1]
    group = seqs // heads
    head_rank, group_rank = seq_rank // group, seq_rank % group
    n_seq = sequence_adapter.shape[0]
    groups = (0, 1)

    a_part = k_rows // tp
    b_part = width // tp
    a_mine = lax.dynamic_slice_in_dim(input_first_factor, tp_rank * a_part, a_part, 1)
    b_mine = lax.dynamic_slice_in_dim(output_down_second_factor, tp_rank * b_part, b_part, 2)
    first = jnp.concatenate(
        [
            query_key_value_weight.transpose(1, 0, 2).reshape(k_rows, 3 * cols),
            query_key_value_second.transpose(1, 0, 2).reshape(rank_cols, 3 * cols),
            a_mine[:3].reshape(-1, 3 * cols),
        ],
        axis=0,
    )
    x_parts = [layer_input] + [
        lax.ppermute(layer_input, "tp", [(i, i ^ mask) for i in range(tp)]) for mask in range(1, tp)
    ]
    first = lax.all_gather(first, "seq", axis=0)
    pieces = [
        output_weight.T,
        output_first_factor.T,
        b_mine.reshape(-1, cols),
        a_mine[3:].reshape(-1, cols),
        down_first_factor.T.reshape(-1, cols),
        gate_up_second_factor.reshape(-1, cols),
    ]
    packed = jnp.concatenate(pieces, axis=0)
    first, x_parts, packed, w_gu, w_down = lax.optimization_barrier(
        (
            first,
            x_parts,
            packed,
            gate_up_weight.transpose(1, 0, 2).reshape(k_rows, 2 * hidden_cols),
            down_weight.T,
        )
    )
    packed = lax.all_gather(packed, "seq", axis=0)
    w_gu = lax.all_gather(w_gu, "seq", axis=0, tiled=True)
    w_down = lax.all_gather(w_down, "seq", axis=0, tiled=True)

    tp_order, seq_order = list(range(bits_of(tp))), list(range(bits_of(seqs)))
    a_qkv = first[:, k_rows + rank_cols :].reshape(seqs, 3, a_part, slots_a)
    a_qkv = a_qkv.transpose(0, 2, 1, 3).reshape(seqs, a_part, 3 * slots_a)
    a_parts = [a_qkv] + [
        lax.ppermute(a_qkv, "tp", [(i, i ^ mask) for i in range(tp)]) for mask in range(1, tp)
    ]
    a_qkv = jnp.zeros((seqs, tp, a_part, 3 * slots_a), BF16)
    for mask, value in enumerate(a_parts):
        a_qkv = lax.dynamic_update_slice(a_qkv, value[:, None], (0, tp_rank ^ mask, 0, 0))
    a_qkv = a_qkv.reshape(width, 3 * slots_a)
    b_qkv = first[:, k_rows : k_rows + rank_cols].reshape(slots_a, 3 * cols)
    b_qkv = blocked([b_qkv[:, i * cols : (i + 1) * cols] for i in range(3)])
    runs = row_runs(tp)
    piece_at = jnp.stack([2 * (tp_rank ^ mask) + which for mask, which in runs]).astype(jnp.int32)
    token = (piece_at[:, None] * part + jnp.arange(part, dtype=jnp.int32)[None, :]).reshape(-1)
    token_block, offset = token // BLK, token % BLK
    block_ids = seq_rank * my_blocks + jnp.arange(my_blocks, dtype=jnp.int32)
    place_blocks = block_position[block_ids]
    adapter_blocks = sequence_adapter[block_sequence[block_ids]]
    in_block = token_block[:, None] == jnp.arange(my_blocks, dtype=jnp.int32)[None, :]
    pick = lambda per_block: jnp.sum(jnp.where(in_block, per_block[None, :], 0), axis=1)
    select = (
        jnp.arange(slots_a, dtype=jnp.int32)[None, :] // ADAPTER_RANK
        == pick(adapter_blocks)[:, None]
    ).astype(F32) * 2.0
    half = rows // 2
    selects = [select[:half], select[half:]]
    start = jnp.where(place_blocks < PROMPT_BLOCKS, place_blocks, PROMPT_BLOCKS) * BLK
    position = pick(start) + offset
    frequency = THETA ** (-(jnp.arange(HEAD_DIM // 2, dtype=F32) * 2.0) / HEAD_DIM)
    angles = position.astype(F32)[:, None] * frequency[None, :]
    cosine, sine = jnp.cos(angles), jnp.sin(angles)
    cs = jnp.concatenate([cosine, cosine, -sine, sine], axis=1)

    owner = (
        ((head_rank - jnp.arange(heads)) % heads)[None, :] * group
        + ((group_rank + jnp.arange(group)) % group)[:, None]
    ).reshape(-1)
    held = (owner[:, None] * my_blocks + jnp.arange(my_blocks)[None, :]).reshape(-1)
    held_seq = block_sequence[held].astype(jnp.int32)
    held_place = block_position[held].astype(jnp.int32)
    prompt_count = n_seq * PROMPT_BLOCKS
    wanted = jnp.arange(prompt_count, dtype=jnp.int32)
    code = jnp.where(held_place < PROMPT_BLOCKS, held_seq * PROMPT_BLOCKS + held_place, -1)
    prompt_at = jnp.sum(
        jnp.where(
            code[None, :] == wanted[:, None], jnp.arange(held.shape[0], dtype=jnp.int32)[None, :], 0
        ),
        axis=1,
    ).astype(jnp.int32)
    own_blocks = heads * my_blocks
    tables = (held_seq[:own_blocks], held_place[:own_blocks], prompt_at)
    head_order = ((head_rank + jnp.arange(heads)) % heads).astype(jnp.int32)

    def head_shift(value, by):
        if by == 0:
            return value
        return lax.ppermute(
            value,
            "seq",
            [
                (h * group + j, ((h + by) % heads) * group + j)
                for h in range(heads)
                for j in range(group)
            ],
        )

    def group_shift(value, by):
        return lax.ppermute(
            value,
            "seq",
            [
                (h * group + j, h * group + (j + by) % group)
                for h in range(heads)
                for j in range(group)
            ],
        )

    own = lambda value, i: value[i * part : (i + 1) * part].astype(F32)
    x = jnp.concatenate(
        [x_parts[mask][which * part : (which + 1) * part] for mask, which in runs], axis=0
    )
    gain = lax.dynamic_slice_in_dim(norm_gain_table[:2], tp_rank * cols, cols, 1)
    pick3 = jnp.tile(select, (1, 3))
    latents = (mm(x, a_qkv) * pick3).astype(BF16)
    z, squares = qkv_product(
        x, latents, first, first[:, k_rows : k_rows + rank_cols].reshape(slots_a, 3 * cols), k_rows, cols
    )
    squares = sum_rows(squares[:2].reshape(2, rows), tp)
    inv = lax.rsqrt(squares / width + EPS)
    inv, packed = lax.optimization_barrier((inv, packed))
    split, at = [], 0
    for piece in pieces:
        split.append(packed[:, at : at + piece.shape[0]])
        at += piece.shape[0]
    w_o = split[0].reshape(width, cols)
    a_o = split[1].reshape(slots_a, cols).T
    shared = gather_order(jnp.concatenate(split[2:4], axis=1), "tp", tp, tp_order)
    b_size = split[2].shape[1]
    b_od = (
        shared[:, :, :b_size]
        .reshape(tp, seqs, 2, rank_cols, b_part)
        .transpose(2, 1, 3, 0, 4)
        .reshape(2, slots_a, width)
    )
    a_gu = (
        shared[:, :, b_size:]
        .reshape(tp, seqs, 2, a_part, slots_a)
        .transpose(1, 0, 3, 2, 4)
        .reshape(width, 2 * slots_a)
    )
    a_down = split[4].reshape(slots_a, hidden_cols).T
    b_gu = (
        split[5]
        .reshape(seqs, 2, rank_cols, hidden_cols)
        .transpose(1, 0, 2, 3)
        .reshape(2 * slots_a, hidden_cols)
    )
    spread = spread_heads(head_order, piece_at, z, inv.T, cs, gain, heads)
    near = [head_shift(spread[heads + k], k) for k in range(heads)]
    queries = [head_shift(spread[k], k) for k in range(heads)]
    far = [group_shift(near[k], -j) for j in range(1, group) for k in range(heads)]
    attended = attend(tables, queries, near, far, prompt_count)
    heads_out = collect_heads(
        head_order, piece_at, [head_shift(attended[k], -k) for k in range(heads)]
    )

    def norm_back(values_in, inv, scaled):
        return inv * scaled - values_in * inv**3 * jnp.mean(scaled * values_in, axis=1, keepdims=True)

    def inverse_norm(values_in):
        return lax.rsqrt(jnp.mean(values_in * values_in, axis=1, keepdims=True) + EPS)

    *far_part, o_latent1 = add_product(heads_out[1], w_o, a_o, b_od[0], selects[1], 2)
    near_part, o_latent0 = add_product(heads_out[0], w_o, a_o, b_od[0], selects[0], 1)
    attn_out = scatter_groups(near_part, far_part, tp)
    scale_o = [inverse_norm(value) for value in attn_out]
    hidden = [
        own(layer_input, i) + attn_out[i] * scale_o[i] * norm_gain_table[2] for i in groups
    ]
    h_low = gather_groups([value.astype(BF16) for value in hidden], tp)

    gates, ups, acts, gu_latents = zip(
        *[gate_up_product(h_low[g], w_gu, a_gu, b_gu, selects[g]) for g in groups]
    )
    *far_part, d_latent1 = add_product(acts[1], w_down, a_down, b_od[1], selects[1], 2)
    near_part, d_latent0 = add_product(acts[0], w_down, a_down, b_od[1], selects[0], 1)
    ff_out = scatter_groups(near_part, far_part, tp)
    scale_f = [inverse_norm(value) for value in ff_out]
    output = jnp.concatenate(
        [hidden[i] + ff_out[i] * scale_f[i] * norm_gain_table[3] for i in groups], axis=0
    )

    d_ffs = gather_groups(
        [
            norm_back(ff_out[i], scale_f[i], own(cotangent, i) * norm_gain_table[3]).astype(BF16)
            for i in groups
        ],
        tp,
    )
    backs = [
        ff_back(
            d_ffs[g], b_od[1], selects[g], w_down, a_down, gates[g], ups[g], w_gu, b_gu, a_gu, 1 + g
        )
        for g in groups
    ]
    summed = scatter_groups(backs[0][0], backs[1][:2], tp)
    d_gates, d_ups, u_gus, u_downs = zip(*[back[-4:] for back in backs])
    d_hidden = [own(cotangent, i) + summed[i] for i in groups]
    d_attn = [
        norm_back(attn_out[i], scale_o[i], d_hidden[i] * norm_gain_table[2]).astype(BF16)
        for i in groups
    ]
    d_latents = (d_latent0, d_latent1)
    d_rows = gather_groups(d_attn, tp)
    o_latents = (o_latent0, o_latent1)
    u_os, grads = [], []
    for g in groups:
        u_os.append((mm_nt(d_rows[g], b_od[0]) * selects[g]).astype(BF16))
        d_heads = (mm(d_rows[g], w_o) + mm_nt(u_os[g], a_o)).astype(BF16)
        grads.append(
            [
                head_shift(
                    lax.dynamic_slice_in_dim(d_heads, head_order[k] * HEAD_DIM, HEAD_DIM, 1), k
                )
                for k in range(heads)
            ]
        )
    grads = [grads[g][k] for k in range(heads) for g in groups]
    results = list(attend_back(tables, piece_at, queries, near, far, grads, prompt_count))
    dqs = [head_shift(results[k], -k) for k in range(heads)]
    d_kv = results[heads].reshape(2, heads, rows, HEAD_DIM)
    others = [
        group_shift(results[heads + j], j).reshape(2, heads, rows, HEAD_DIM) for j in range(1, group)
    ]
    dkvs = []
    for k in range(heads):
        total = d_kv[:, k].astype(F32)
        for other in others:
            total = total + other[:, k].astype(F32)
        dkvs.append(head_shift(total.astype(BF16), -k))
    dkvs[1], u_os, o_latents, u_downs, d_latents, u_gus, gu_latents = lax.optimization_barrier(
        (dkvs[1], u_os, o_latents, u_downs, d_latents, u_gus, gu_latents)
    )
    both_groups = lambda f: f(0) + f(1)
    grad_a_down = both_groups(lambda g: mm_tn(u_downs[g], acts[g]))
    grad_b_down = both_groups(lambda g: mm_tn(d_latents[g], d_ffs[g]))
    grad_a_gu = both_groups(lambda g: mm_tn(h_low[g], u_gus[g]))
    grad_b_gate = both_groups(lambda g: mm_tn(gu_latents[g][:, :slots_a], d_gates[g]))
    grad_b_up = both_groups(lambda g: mm_tn(gu_latents[g][:, slots_a:], d_ups[g]))
    lane = 2 * slots_a
    shards = lambda value: value.astype(BF16).reshape(seqs, -1, lane)
    early = jnp.concatenate(
        [
            shards(grad_a_gu),
            shards(grad_b_down),
            shards(grad_a_down),
            shards(grad_b_gate),
            shards(grad_b_up),
        ],
        axis=1,
    )
    grad_a_o = both_groups(lambda g: mm_tn(u_os[g], heads_out[g]))
    grad_b_o = both_groups(lambda g: mm_tn(o_latents[g], d_rows[g]))
    late_o = jnp.concatenate(
        [
            grad_b_o.astype(BF16).reshape(seqs, -1, cols),
            grad_a_o.astype(BF16).reshape(seqs, -1, cols),
        ],
        axis=1,
    )
    dqs, dkvs, early, late_o = lax.optimization_barrier((dqs, dkvs, early, late_o))
    early = lax.psum_scatter(early, "seq", scatter_dimension=0, tiled=False)
    late_o = scatter_order(late_o, "seq", seqs, seq_order)
    scaled, parts = unturn_heads(head_order, piece_at, dqs, dkvs, z, cs, gain)
    parts = sum_rows(parts.T, tp) / width
    coef = jnp.concatenate([inv, inv**3 * parts], axis=0)
    dz = norm_back_heads(head_order, piece_at, dkvs, scaled, z, coef.T)
    us = (mm_nt(dz, b_qkv) * pick3).astype(BF16)
    grad_a_qkv = mm_tn(x, us)
    grad_b_qkv = mm_tn(latents, dz)
    lane3 = 3 * slots_a
    grad_b_qkv = jnp.concatenate(
        [
            grad_b_qkv[i * slots_a : (i + 1) * slots_a, i * cols : (i + 1) * cols]
            for i in range(3)
        ],
        axis=1,
    )
    late = jnp.concatenate(
        [
            grad_a_qkv.astype(BF16).reshape(seqs, k_rows, lane3),
            grad_b_qkv.astype(BF16).reshape(seqs, -1, lane3),
        ],
        axis=1,
    )
    dz, late = lax.optimization_barrier((dz, late))
    far_part = list(back_product(dz, 1, first, k_rows, us, a_qkv, 2))
    far_part[0], dz = lax.optimization_barrier((far_part[0], dz))
    (near_part,) = back_product(dz, 0, first, k_rows, us, a_qkv, 1)
    near_part, early, late_o = lax.optimization_barrier((near_part, early, late_o))
    summed = scatter_groups(near_part, far_part, tp)
    input_grad = jnp.concatenate([d_hidden[i] + summed[i] for i in groups], axis=0)

    late = scatter_order(late, "seq", seqs, seq_order)
    sum_tp = lambda value: sum_all(value.astype(BF16), "tp", tp).astype(F32)
    down_size = rank_cols * width // lane
    o_size = rank_cols * width // cols
    both = sum_tp(
        jnp.concatenate(
            [early[: k_rows + down_size], late_o[:o_size].astype(BF16).reshape(-1, lane)], axis=0
        )
    )
    grad_a_gu = both[:k_rows]
    grad_b_down = both[k_rows : k_rows + down_size].reshape(rank_cols, width)
    grad_b_o = both[k_rows + down_size :].reshape(rank_cols, width)
    a_size = rank_cols * hidden_cols // lane
    rest = early[k_rows + down_size :].astype(F32)
    grad_a_down = rest[:a_size].reshape(rank_cols, hidden_cols).T
    grad_b_gu = rest[a_size:].reshape(2, rank_cols, hidden_cols)
    grad_a_o = late_o[o_size:].T
    grad_a_qkv = sum_tp(late[:k_rows])
    grad_b_qkv = late[k_rows:].reshape(rank_cols, 3, cols).transpose(1, 0, 2)
    grad_a_in = jnp.stack(
        [grad_a_qkv[:, i * slots_a : (i + 1) * slots_a] for i in range(3)]
        + [grad_a_gu[:, i * slots_a : (i + 1) * slots_a] for i in range(2)]
    )
    grad_b_out = jnp.stack([grad_b_o, grad_b_down])
    return (output, input_grad, grad_a_in, grad_a_o, grad_a_down, grad_b_qkv, grad_b_gu, grad_b_out)


def solution(mesh):
    return jax.shard_map(
        local,
        mesh=mesh,
        in_specs=(
            P(("seq", "tp"), None),
            P(("seq", "tp"), None),
            P(None, "seq", "tp"),
            P("tp", "seq"),
            P(None, "seq", "tp"),
            P("tp", "seq"),
            P(None, "seq", None),
            P("tp", "seq"),
            P("tp", "seq"),
            P(None, "seq", "tp"),
            P(None, "seq", "tp"),
            P(None, "seq", None),
            P(),
            P(),
            P(),
            P(),
        ),
        out_specs=(
            P(("seq", "tp"), None),
            P(("seq", "tp"), None),
            P(None, "seq", None),
            P("tp", "seq"),
            P("tp", "seq"),
            P(None, "seq", "tp"),
            P(None, "seq", "tp"),
            P(None, "seq", None),
        ),
        check_vma=False,
    )
```

```python
import functools

import jax
import jax.numpy as jnp
from jax import lax
from jax.experimental import pallas as pl
from jax.experimental.pallas import tpu as pltpu
from jax.sharding import PartitionSpec as P

HEAD_DIM = 128
ADAPTER_RANK = 16
BLK = 128
PROMPT_BLOCKS = 8
EPS = 1e-06
THETA = 500000.0
NEG = -1e30
LOG2E = 1.4426950408889634
F32 = jnp.float32
BF16 = jnp.bfloat16


def mm(a, b):
    return jnp.dot(a, b, preferred_element_type=F32)


def mm_nt(a, b):
    return lax.dot_general(a, b, (((1,), (1,)), ((), ())), preferred_element_type=F32)


def mm_tn(a, b):
    return lax.dot_general(a, b, (((0,), (0,)), ((), ())), preferred_element_type=F32)


def bits_of(count):
    n = count.bit_length() - 1
    assert 1 << n == count
    return n


def flip(value, axis, count, bit):
    return lax.ppermute(value, axis, [(i, i ^ (1 << bit)) for i in range(count)])


def gather_order(value, axis, count, order):
    rank = lax.axis_index(axis)
    have = []
    current = value
    for bit in order:
        other = flip(current, axis, count, bit)
        mine_low = ((rank >> bit) & 1) == 0
        at = len([b for b in have if b > bit])
        low = jnp.where(mine_low, current, other)
        high = jnp.where(mine_low, other, current)
        current = jnp.stack([low, high], axis=at)
        have = sorted(have + [bit], reverse=True)
    return current.reshape((count,) + value.shape)


def scatter_order(value, axis, count, order):
    n = bits_of(count)
    rank = lax.axis_index(axis)
    current = value.reshape((2,) * n + value.shape[1:])
    have = list(range(n - 1, -1, -1))
    for bit in order:
        at = have.index(bit)
        mine = (rank >> bit) & 1
        keep = lax.dynamic_index_in_dim(current, mine, at, keepdims=False)
        give = lax.dynamic_index_in_dim(current, 1 - mine, at, keepdims=False)
        got = flip(give.astype(BF16), axis, count, bit)
        current = keep.astype(F32) + got.astype(F32)
        have.remove(bit)
    return current


def part_orders(count):
    order = list(range(bits_of(count)))
    return (order, order[::-1])


def group_masks(count):
    groups = ([], [])
    for part, order in enumerate(part_orders(count)):
        for j in range(count):
            mask = sum(1 << bit for i, bit in enumerate(order) if (j >> i) & 1)
            groups[j >= count // 2].append((mask, part))
    return groups


def row_runs(count):
    return [run for masks in group_masks(count) for run in masks]


def gather_groups(parts, count, beside=None):
    near, far = [], []
    for value, order in zip(parts, part_orders(count)):
        for bit in order[:-1]:
            value = jnp.concatenate([value, flip(value, "tp", count, bit)], axis=0)
        near.append(value)
    if beside is not None:
        near[1], beside = lax.optimization_barrier((near[1], beside))
    for value, order in zip(near, part_orders(count)):
        far.append(flip(value, "tp", count, order[-1]))
    if beside is not None:
        return jnp.concatenate(near, axis=0), jnp.concatenate(far, axis=0), beside
    return jnp.concatenate(near, axis=0), jnp.concatenate(far, axis=0)


def scatter_groups(near, far, count):
    return scatter_rest(scatter_first(near, far, count), count)


def scatter_first(near, far, count):
    out = []
    size = near.shape[0] // 2
    for i, order in enumerate(part_orders(count)):
        got = flip(far[i], "tp", count, order[-1])
        out.append(near[i * size : (i + 1) * size].astype(F32) + got.astype(F32))
    return out


def scatter_rest(totals, count):
    out = []
    for total, order in zip(totals, part_orders(count)):
        for bit in order[-2::-1]:
            half = total.shape[0] // 2
            got = flip(total[half:].astype(BF16), "tp", count, bit)
            total = total[:half] + got.astype(F32)
        out.append(total)
    return out


def sum_rows(value, count):
    runs = row_runs(count)
    value = value.reshape(value.shape[0], len(runs), -1)
    total = value
    for mask in range(1, count):
        got = lax.ppermute(value, "tp", [(i, i ^ mask) for i in range(count)])
        order = [runs.index((other ^ mask, which)) for other, which in runs]
        total = total + jnp.concatenate([got[:, j : j + 1] for j in order], axis=1)
    return total.reshape(value.shape[0], -1)


def sum_all(value, axis, count):
    for bit in range(bits_of(count)):
        value = value + flip(value, axis, count, bit)
    return value


def copy_all(pairs, sem):
    copies = [pltpu.make_async_copy(src, dst, sem.at[i]) for i, (src, dst) in enumerate(pairs)]
    for copy in copies:
        copy.start()
    for copy in copies:
        copy.wait()


def gather_prompt(prompt_at, source, target, count):
    def step(i, carry):
        start = pl.multiple_of(prompt_at[i] * BLK, BLK)
        target[pl.ds(pl.multiple_of(i * BLK, BLK), BLK), :] = source[pl.ds(start, BLK), :]
        return carry

    lax.fori_loop(0, count, step, 0)


def masked_scores(keys, own_keys, queries, place, scale):
    prompt = mm_nt(keys, queries) * scale
    block = lax.broadcasted_iota(jnp.int32, prompt.shape, 0) // BLK
    prompt = jnp.where(block < place, prompt, NEG)
    own = mm_nt(own_keys, queries) * scale
    causal = lax.broadcasted_iota(jnp.int32, own.shape, 0) <= lax.broadcasted_iota(
        jnp.int32, own.shape, 1
    )
    own = jnp.where(causal, own, NEG)
    top = jnp.maximum(jnp.max(prompt, axis=0, keepdims=True), jnp.max(own, axis=0, keepdims=True))
    prompt = jnp.exp2(prompt - top)
    own = jnp.exp2(own - top)
    total = jnp.sum(prompt, axis=0, keepdims=True) + jnp.sum(own, axis=0, keepdims=True)
    return prompt, own, 1.0 / total


def load_plan(slots, group, rows, refs, q_buf, k_buf, v_buf):
    plan = []
    for i in range(slots):
        plan.append((refs[i].at[0], q_buf.at[pl.ds(i * rows, rows)]))
    for i in range(slots * group):
        at = pl.ds(i * rows, rows)
        skip = int(i < slots)
        plan += [(refs[i].at[skip], k_buf.at[at]), (refs[i].at[skip + 1], v_buf.at[at])]
    return plan


def attend_kernel(slots, group, rows, prompt_count, q_seq, q_place, prompt_at, *refs):
    n_in = slots * group
    outs = refs[n_in : n_in + slots]
    q_buf, k_buf, v_buf, kp, vp, o_buf, sem = refs[n_in + slots :]
    copy_all(load_plan(slots, group, rows, refs, q_buf, k_buf, v_buf), sem)
    gather_prompt(prompt_at, k_buf, kp, prompt_count)
    gather_prompt(prompt_at, v_buf, vp, prompt_count)
    scale = HEAD_DIM ** (-0.5) * LOG2E
    span = PROMPT_BLOCKS * BLK

    def block(i):
        at = pl.ds(pl.multiple_of(i * BLK, BLK), BLK)
        of_seq = pl.ds(pl.multiple_of(q_seq[i] * span, span), span)
        prompt, own, inverse = masked_scores(
            kp[of_seq, :], k_buf[at, :], q_buf[at, :], q_place[i], scale
        )
        result = mm_tn(vp[of_seq, :], prompt.astype(BF16)) + mm_tn(v_buf[at, :], own.astype(BF16))
        return at, (result * inverse).T.astype(BF16)

    blocks = slots * rows // BLK
    pair = 2 if blocks % 2 == 0 else 1

    def step(i, carry):
        for at, result in [block(i * pair + j) for j in range(pair)]:
            o_buf[at, :] = result
        return carry

    lax.fori_loop(0, blocks // pair, step, 0)
    copy_all([(o_buf.at[pl.ds(i * rows, rows)], outs[i]) for i in range(slots)], sem)


def attend_back_kernel(
    slots, group, rows, pieces, prompt_count, q_seq, q_place, prompt_at, piece_at, *refs
):
    n_in = slots * group
    n_grad = slots * 2
    grads = refs[n_in : n_in + n_grad]
    outs = refs[n_in + n_grad : n_in + n_grad + slots]
    near_out = refs[n_in + n_grad + slots]
    rest = refs[n_in + n_grad + slots + 1 :]
    far_outs, rest = rest[: group - 1], rest[group - 1 :]
    q_buf, k_buf, v_buf, do_buf, kp, vp, dkp, dvp, dq_buf, dkv_buf, sem = rest
    plan = load_plan(slots, group, rows, refs, q_buf, k_buf, v_buf)
    size = rows // pieces
    for i in range(slots):
        for p in range(pieces):
            half, at = divmod(p, pieces // 2)
            to = pl.multiple_of(i * rows + piece_at[p] * size, 16)
            plan.append(
                (grads[i * 2 + half].at[pl.ds(at * size, size)], do_buf.at[pl.ds(to, size)])
            )
    copy_all(plan, sem)
    gather_prompt(prompt_at, k_buf, kp, prompt_count)
    gather_prompt(prompt_at, v_buf, vp, prompt_count)
    dkp[...] = jnp.zeros_like(dkp)
    dvp[...] = jnp.zeros_like(dvp)
    scale = HEAD_DIM ** (-0.5)
    span = PROMPT_BLOCKS * BLK
    own_rows = slots * rows
    zeros = jnp.zeros((BLK, HEAD_DIM), BF16)

    def rows_of(i):
        return pl.ds(pl.multiple_of(i * BLK, BLK), BLK)

    def clear(i, carry):
        for j in range(1, group):
            dkv_buf[j, 0, rows_of(i), :] = zeros
            dkv_buf[j, 1, rows_of(i), :] = zeros
        return carry

    lax.fori_loop(0, own_rows // BLK, clear, 0)

    def block(i):
        at = rows_of(i)
        seq, place = q_seq[i], q_place[i]
        of_seq = pl.ds(pl.multiple_of(seq * span, span), span)
        queries, grad = q_buf[at, :], do_buf[at, :]
        prompt, own, inverse = masked_scores(
            kp[of_seq, :], k_buf[at, :], queries, place, scale * LOG2E
        )
        prompt, own = prompt * inverse, own * inverse
        d_prompt = mm_nt(vp[of_seq, :], grad)
        d_own = mm_nt(v_buf[at, :], grad)
        delta = jnp.sum(prompt * d_prompt, axis=0, keepdims=True) + jnp.sum(
            own * d_own, axis=0, keepdims=True
        )
        ds_prompt = (prompt * (d_prompt - delta)).astype(BF16)
        ds_own = (own * (d_own - delta)).astype(BF16)
        dq = mm_tn(ds_prompt, kp[of_seq, :]) + mm_tn(ds_own, k_buf[at, :])
        return (
            at,
            of_seq,
            (dq * scale).astype(BF16),
            mm(prompt.astype(BF16), grad),
            mm(ds_prompt, queries) * scale,
            (mm(ds_own, queries) * scale).astype(BF16),
            mm(own.astype(BF16), grad).astype(BF16),
        )

    blocks = own_rows // BLK
    pair = 2 if blocks % 2 == 0 else 1

    def step(i, carry):
        for at, of_seq, dq, dv_prompt, dk_prompt, dk_own, dv_own in [
            block(i * pair + j) for j in range(pair)
        ]:
            dq_buf[at, :] = dq
            dvp[of_seq, :] += dv_prompt
            dkp[of_seq, :] += dk_prompt
            dkv_buf[0, 0, at, :] = dk_own
            dkv_buf[0, 1, at, :] = dv_own
        return carry

    lax.fori_loop(0, blocks // pair, step, 0)

    def spread(i, carry):
        place = prompt_at[i]
        j, to = place // blocks, rows_of(place % blocks)
        dkv_buf[j, 0, to, :] = (dkv_buf[j, 0, to, :].astype(F32) + dkp[rows_of(i), :]).astype(BF16)
        dkv_buf[j, 1, to, :] = (dkv_buf[j, 1, to, :].astype(F32) + dvp[rows_of(i), :]).astype(BF16)
        return carry

    lax.fori_loop(0, prompt_count, spread, 0)
    plan = [(dq_buf.at[pl.ds(i * rows, rows)], outs[i]) for i in range(slots)]
    plan.append((dkv_buf.at[0], near_out))
    plan += [(dkv_buf.at[j], far_outs[j - 1]) for j in range(1, group)]
    copy_all(plan, sem)


ANY = pl.BlockSpec(memory_space=pl.ANY)


def attend(tables, near, far, prompt_count):
    slots = len(near)
    rows = near[0].shape[1]
    group = 1 + len(far) // slots
    own, every = slots * rows, slots * group * rows
    pairs = own * (PROMPT_BLOCKS + 1) * BLK
    wide = lambda count, kind=BF16: pltpu.VMEM((count, HEAD_DIM), kind)
    return pl.pallas_call(
        functools.partial(attend_kernel, slots, group, rows, prompt_count),
        out_shape=[jax.ShapeDtypeStruct((rows, HEAD_DIM), BF16)] * slots,
        grid_spec=pltpu.PrefetchScalarGridSpec(
            num_scalar_prefetch=3,
            in_specs=[ANY] * (slots * group),
            out_specs=[ANY] * slots,
            scratch_shapes=[
                wide(own),
                wide(every),
                wide(every),
                wide(prompt_count * BLK),
                wide(prompt_count * BLK),
                wide(own),
                pltpu.SemaphoreType.DMA((slots + 2 * slots * group,)),
            ],
        ),
        cost_estimate=pl.CostEstimate(
            flops=4 * pairs * HEAD_DIM, bytes_accessed=6 * every * HEAD_DIM, transcendentals=pairs
        ),
        name="attend",
    )(*tables, *near, *far)


def attend_back(tables, piece_at, near, far, grads, prompt_count):
    pieces = piece_at.shape[0]
    slots = len(near)
    rows = near[0].shape[1]
    group = 1 + len(far) // slots
    own, every = slots * rows, slots * group * rows
    pairs = own * (PROMPT_BLOCKS + 1) * BLK
    wide = lambda count, kind=BF16: pltpu.VMEM((count, HEAD_DIM), kind)
    return pl.pallas_call(
        functools.partial(attend_back_kernel, slots, group, rows, pieces, prompt_count),
        out_shape=[jax.ShapeDtypeStruct((rows, HEAD_DIM), BF16)] * slots
        + [jax.ShapeDtypeStruct((2, own, HEAD_DIM), BF16)] * group,
        grid_spec=pltpu.PrefetchScalarGridSpec(
            num_scalar_prefetch=4,
            in_specs=[ANY] * (slots * group + 2 * slots),
            out_specs=[ANY] * (slots + group),
            scratch_shapes=[
                wide(own),
                wide(every),
                wide(every),
                wide(own),
                wide(prompt_count * BLK),
                wide(prompt_count * BLK),
                wide(prompt_count * BLK, F32),
                wide(prompt_count * BLK, F32),
                wide(own),
                pltpu.VMEM((group, 2, own, HEAD_DIM), BF16),
                pltpu.SemaphoreType.DMA((slots + 2 * slots * group + slots * pieces,)),
            ],
        ),
        cost_estimate=pl.CostEstimate(
            flops=10 * pairs * HEAD_DIM, bytes_accessed=12 * every * HEAD_DIM, transcendentals=pairs
        ),
        name="attend_back",
    )(*tables, piece_at, *near, *far, *grads)


def turn(values, cosine, sine):
    return values * cosine + pltpu.roll(values, HEAD_DIM // 2, 1) * sine


def lanes(head, base=0):
    return pl.ds(pl.multiple_of(base + head * HEAD_DIM, HEAD_DIM), HEAD_DIM)


def piece_rows(index, size):
    return pl.ds(pl.multiple_of(index * size, 16), size)


def spread_kernel(slots, pieces, order, piece_at, z, inv, cs, gain, *outs):
    cols = slots * HEAD_DIM
    size = z.shape[0] // pieces

    def step(p, carry):
        at, to = piece_rows(p, size), piece_rows(piece_at[p], size)
        cosine, sine = cs[at, :HEAD_DIM], cs[at, HEAD_DIM:]
        for which in range(2):
            factor = inv[at, which : which + 1]
            for k in range(slots):
                head = order[k]
                scaled = z[at, lanes(head, which * cols)] * factor
                scaled = scaled * gain[which : which + 1, lanes(head)]
                turned = turn(scaled, cosine, sine).astype(BF16)
                outs[k][which, to, :] = turned
        for k in range(slots):
            outs[k][2, to, :] = z[at, lanes(order[k], 2 * cols)].astype(BF16)
        return carry

    lax.fori_loop(0, pieces, step, 0)


WHOLE = pl.BlockSpec(memory_space=pltpu.VMEM)
BIG = pltpu.CompilerParams(vmem_limit_bytes=56 * 1024 * 1024)


def spread_heads(order, piece_at, z, inv, cs, gain, slots):
    rows = z.shape[0]
    return pl.pallas_call(
        functools.partial(spread_kernel, slots, piece_at.shape[0]),
        out_shape=[jax.ShapeDtypeStruct((3, rows, HEAD_DIM), BF16)] * slots,
        grid_spec=pltpu.PrefetchScalarGridSpec(
            num_scalar_prefetch=2, in_specs=[WHOLE] * 4, out_specs=[WHOLE] * slots
        ),
        compiler_params=BIG,
        name="spread_heads",
    )(order, piece_at, z, inv, cs, gain)


def collect_kernel(slots, pieces, order, piece_at, *refs):
    outs = refs[slots:]
    size = refs[0].shape[0] // pieces
    for p in range(pieces):
        half, at = divmod(p, pieces // 2)
        for k in range(slots):
            outs[half][pl.ds(at * size, size), lanes(order[k])] = refs[k][
                piece_rows(piece_at[p], size), :
            ]


def collect_heads(order, piece_at, parts):
    slots = len(parts)
    rows = parts[0].shape[0]
    return pl.pallas_call(
        functools.partial(collect_kernel, slots, piece_at.shape[0]),
        out_shape=[jax.ShapeDtypeStruct((rows // 2, slots * HEAD_DIM), BF16)] * 2,
        grid_spec=pltpu.PrefetchScalarGridSpec(
            num_scalar_prefetch=2, in_specs=[WHOLE] * slots, out_specs=[WHOLE] * 2
        ),
        name="collect_heads",
    )(order, piece_at, *parts)


def unturn_kernel(slots, pieces, order, piece_at, *refs):
    dqs, dkvs, rest = refs[:slots], refs[slots : 2 * slots], refs[2 * slots :]
    z, cs, gain, scaled_out, part_out = rest
    cols = slots * HEAD_DIM
    size = z.shape[0] // pieces

    def step(p, carry):
        at, source = piece_rows(p, size), piece_rows(piece_at[p], size)
        cosine, sine = cs[at, :HEAD_DIM], cs[at, HEAD_DIM:]
        for which in range(2):
            total = jnp.zeros((size, HEAD_DIM), F32)
            for k in range(slots):
                head = order[k]
                grad = dqs[k][source, :] if which == 0 else dkvs[k][0, source, :]
                grad = turn(grad.astype(F32), cosine, -sine) * gain[which : which + 1, lanes(head)]
                scaled_out[at, lanes(head, which * cols)] = grad
                total = total + grad * z[at, lanes(head, which * cols)]
            part_out[at, which : which + 1] = jnp.sum(total, axis=1, keepdims=True)
        return carry

    lax.fori_loop(0, pieces, step, 0)


def unturn_heads(order, piece_at, dqs, dkvs, z, cs, gain):
    slots = len(dqs)
    rows = z.shape[0]
    cols = slots * HEAD_DIM
    return pl.pallas_call(
        functools.partial(unturn_kernel, slots, piece_at.shape[0]),
        out_shape=[
            jax.ShapeDtypeStruct((rows, 2 * cols), F32),
            jax.ShapeDtypeStruct((rows, 2), F32),
        ],
        grid_spec=pltpu.PrefetchScalarGridSpec(
            num_scalar_prefetch=2, in_specs=[WHOLE] * (2 * slots + 3), out_specs=[WHOLE] * 2
        ),
        compiler_params=BIG,
        name="unturn_heads",
    )(order, piece_at, *dqs, *dkvs, z, cs, gain)


def norm_back_kernel(slots, pieces, order, piece_at, *refs):
    dkvs, (scaled, z, coef, out) = refs[:slots], refs[slots:]
    cols = slots * HEAD_DIM
    size = z.shape[0] // pieces

    def step(p, carry):
        at, source = piece_rows(p, size), piece_rows(piece_at[p], size)
        for which in range(2):
            to = slice(which * cols, (which + 1) * cols)
            out[at, to] = (
                scaled[at, to] * coef[at, which : which + 1]
                - z[at, to] * coef[at, 2 + which : 3 + which]
            ).astype(BF16)
        for k in range(slots):
            out[at, lanes(order[k], 2 * cols)] = dkvs[k][1, source, :]
        return carry

    lax.fori_loop(0, pieces, step, 0)


def norm_back_heads(order, piece_at, dkvs, scaled, z, coef):
    slots = len(dkvs)
    return pl.pallas_call(
        functools.partial(norm_back_kernel, slots, piece_at.shape[0]),
        out_shape=jax.ShapeDtypeStruct(z.shape, BF16),
        grid_spec=pltpu.PrefetchScalarGridSpec(
            num_scalar_prefetch=2, in_specs=[WHOLE] * (slots + 3), out_specs=WHOLE
        ),
        compiler_params=BIG,
        name="norm_back_heads",
    )(order, piece_at, *dkvs, scaled, z, coef)


def fixed(*shape, at=None):
    place = at or (0,) * len(shape)
    return pl.BlockSpec(shape, lambda i: place)


def flat(value):
    return value.reshape(-1, value.shape[-1])


def qkv_kernel(x, latent, weight, second, z, squares):
    i = pl.program_id(0)
    result = mm(x[...], flat(weight[...])) + mm(latent[...], flat(second[...]))
    z[...] = result
    squares[0, :, :] = jnp.sum(result * result, axis=1, keepdims=True)


def qkv_product(x, latents, first, second, k_rows, cols):
    rows, width = x.shape
    shards, _, total = first.shape
    low = latents.shape[1] // 3
    return pl.pallas_call(
        qkv_kernel,
        grid=(3,),
        out_shape=[
            jax.ShapeDtypeStruct((rows, total), F32),
            jax.ShapeDtypeStruct((3, rows, 1), F32),
        ],
        in_specs=[
            fixed(rows, width),
            pl.BlockSpec((rows, low), lambda i: (0, i)),
            pl.BlockSpec((shards, k_rows, cols), lambda i: (0, 0, i)),
            pl.BlockSpec((low, cols), lambda i: (0, i)),
        ],
        out_specs=[
            pl.BlockSpec((rows, cols), lambda i: (0, i)),
            pl.BlockSpec((1, rows, 1), lambda i: (i, 0, 0)),
        ],
        compiler_params=BIG,
        cost_estimate=pl.CostEstimate(
            flops=2 * rows * width * total, bytes_accessed=2 * first.size, transcendentals=0
        ),
        name="qkv_product",
    )(x, latents, first, second)


def add_kernel(parts, a, weight, first, second, pick, *refs):
    outs, (latent_out, latent) = refs[:parts], refs[parts:]

    @pl.when(pl.program_id(0) == 0)
    def _():
        latent[...] = (mm(a[...], first[...]) * pick[...]).astype(BF16)
        latent_out[...] = latent[...]

    result = mm_nt(a[...], weight[...]) + mm(latent[...], second[...])
    size = result.shape[0] // parts
    for i in range(parts):
        outs[i][...] = result[i * size : (i + 1) * size].astype(BF16)


def add_product(a, weight, first, second, pick, parts, tile=512):
    rows, depth = a.shape
    width, low = weight.shape[0], first.shape[1]
    size = rows // parts
    return pl.pallas_call(
        functools.partial(add_kernel, parts),
        grid=(width // tile,),
        out_shape=[jax.ShapeDtypeStruct((size, width), BF16)] * parts
        + [jax.ShapeDtypeStruct((rows, low), BF16)],
        in_specs=[
            fixed(rows, depth),
            pl.BlockSpec((tile, depth), lambda i: (i, 0)),
            fixed(depth, low),
            pl.BlockSpec((low, tile), lambda i: (0, i)),
            fixed(rows, low),
        ],
        out_specs=[pl.BlockSpec((size, tile), lambda i: (0, i))] * parts + [fixed(rows, low)],
        scratch_shapes=[pltpu.VMEM((rows, low), BF16)],
        compiler_params=BIG,
        cost_estimate=pl.CostEstimate(
            flops=2 * rows * width * depth, bytes_accessed=2 * weight.size, transcendentals=0
        ),
        name="add_product",
    )(a, weight, first, second, pick)


def back_kernel(parts, a, weight, u, first, *outs):
    result = mm_nt(a[...], flat(weight[...])) + mm_nt(u[...], first[...])
    size = result.shape[0] // parts
    for i in range(parts):
        outs[i][...] = result[i * size : (i + 1) * size].astype(BF16)


def back_product(a, group, weight, k_rows, u, first, parts):
    rows, depth = a.shape
    rows //= 2
    shards = weight.shape[0]
    width, low = first.shape
    per = max(1, 512 // k_rows)
    size = rows // parts
    return pl.pallas_call(
        functools.partial(back_kernel, parts),
        grid=(shards // per,),
        out_shape=[jax.ShapeDtypeStruct((size, width), BF16)] * parts,
        in_specs=[
            fixed(rows, depth, at=(group, 0)),
            pl.BlockSpec((per, k_rows, depth), lambda i: (i, 0, 0)),
            fixed(rows, low, at=(group, 0)),
            pl.BlockSpec((per * k_rows, low), lambda i: (i, 0)),
        ],
        out_specs=[pl.BlockSpec((size, per * k_rows), lambda i: (0, i))] * parts,
        compiler_params=BIG,
        cost_estimate=pl.CostEstimate(
            flops=2 * rows * width * depth, bytes_accessed=2 * width * depth, transcendentals=0
        ),
        name="back_product",
    )(a, weight, u, first)


def gate_up_kernel(h, first, pick, w_g, w_u, b_g, b_u, gate_out, up_out, act, latent_out, latent):
    low = pick.shape[1]

    @pl.when(pl.program_id(0) == 0)
    def _():
        both = mm(h[...], first[...])
        latent[:, :low] = (both[:, :low] * pick[...]).astype(BF16)
        latent[:, low:] = (both[:, low:] * pick[...]).astype(BF16)
        latent_out[...] = latent[...]

    gate = mm(h[...], w_g[...]) + mm(latent[:, :low], b_g[...])
    up = mm(h[...], w_u[...]) + mm(latent[:, low:], b_u[...])
    gate_out[...] = gate
    up_out[...] = up
    act[...] = (gate / (1.0 + jnp.exp(-gate)) * up).astype(BF16)


def gate_up_product(h, w_gu, a_gu, b_gu, pick, tile=512):
    rows, width = h.shape
    units, low = w_gu.shape[1] // 2, pick.shape[1]
    n = units // tile
    left = lambda depth: pl.BlockSpec((depth, tile), lambda i: (0, i))
    out = pl.BlockSpec((rows, tile), lambda i: (0, i))
    return pl.pallas_call(
        gate_up_kernel,
        grid=(n,),
        out_shape=[jax.ShapeDtypeStruct((rows, units), F32)] * 2
        + [
            jax.ShapeDtypeStruct((rows, units), BF16),
            jax.ShapeDtypeStruct((rows, 2 * low), BF16),
        ],
        in_specs=[
            fixed(rows, width),
            fixed(width, 2 * low),
            fixed(rows, low),
            left(width),
            pl.BlockSpec((width, tile), lambda i: (0, i + n)),
            left(low),
            pl.BlockSpec((low, tile), lambda i: (1, i)),
        ],
        out_specs=[out, out, out, fixed(rows, 2 * low)],
        scratch_shapes=[pltpu.VMEM((rows, 2 * low), BF16)],
        compiler_params=BIG,
        cost_estimate=pl.CostEstimate(
            flops=4 * rows * width * units, bytes_accessed=4 * width * units, transcendentals=0
        ),
        name="gate_up_product",
    )(h, a_gu, pick, w_gu, w_gu, b_gu, b_gu)


def ff_back_kernel(
    parts, steps, d_ff, b_down, pick, w_down, a_down, gate, up, w_g, w_u, b_g, b_u, a_gu, *refs
):
    outs, (d_gate_out, d_up_out, u_out, u_down_out, acc, u_g, u_u, u_down) = refs[:parts], refs[parts:]
    i = pl.program_id(0)

    @pl.when(i == 0)
    def _():
        u_down[...] = (mm_nt(d_ff[...], b_down[...]) * pick[...]).astype(BF16)
        u_down_out[...] = u_down[...]

    d_act = mm(d_ff[...], w_down[...]) + mm_nt(u_down[...], a_down[...])
    g = gate[...]
    sigmoid = 1.0 / (1.0 + jnp.exp(-g))
    silu = g * sigmoid
    d_gate = (d_act * up[...] * (sigmoid + silu * (1.0 - sigmoid))).astype(BF16)
    d_up = (d_act * silu).astype(BF16)
    d_gate_out[...] = d_gate
    d_up_out[...] = d_up
    part = mm_nt(d_gate, w_g[...]) + mm_nt(d_up, w_u[...])
    part_g, part_u = mm_nt(d_gate, b_g[...]), mm_nt(d_up, b_u[...])

    @pl.when(i == 0)
    def _():
        acc[...] = part
        u_g[...] = part_g
        u_u[...] = part_u

    @pl.when(i > 0)
    def _():
        acc[...] += part
        u_g[...] += part_g
        u_u[...] += part_u

    @pl.when(i == steps - 1)
    def _():
        low = pick.shape[1]
        last_g = (u_g[...] * pick[...]).astype(BF16)
        last_u = (u_u[...] * pick[...]).astype(BF16)
        u_out[:, :low] = last_g
        u_out[:, low:] = last_u
        size = acc.shape[0] // parts
        for p in range(parts):
            at = slice(p * size, (p + 1) * size)
            outs[p][...] = (
                acc[at, :]
                + mm_nt(last_g[at], a_gu[:, :low])
                + mm_nt(last_u[at], a_gu[:, low:])
            ).astype(BF16)


def ff_back(d_ff, b_down, pick, w_down, a_down, gate, up, w_gu, b_gu, a_gu, parts, tile=512):
    rows, width = d_ff.shape
    units, low = gate.shape[1], pick.shape[1]
    n = units // tile
    size = rows // parts
    column = lambda depth: pl.BlockSpec((depth, tile), lambda i: (0, i))
    return pl.pallas_call(
        functools.partial(ff_back_kernel, parts, n),
        grid=(n,),
        out_shape=[jax.ShapeDtypeStruct((size, width), BF16)] * parts
        + [jax.ShapeDtypeStruct((rows, units), BF16)] * 2
        + [
            jax.ShapeDtypeStruct((rows, 2 * low), BF16),
            jax.ShapeDtypeStruct((rows, low), BF16),
        ],
        in_specs=[
            fixed(rows, width),
            fixed(low, width),
            fixed(rows, low),
            column(width),
            pl.BlockSpec((tile, low), lambda i: (i, 0)),
            column(rows),
            column(rows),
            column(width),
            pl.BlockSpec((width, tile), lambda i: (0, i + n)),
            column(low),
            pl.BlockSpec((low, tile), lambda i: (1, i)),
            fixed(width, 2 * low),
        ],
        out_specs=[fixed(size, width)] * parts
        + [column(rows), column(rows), fixed(rows, 2 * low), fixed(rows, low)],
        scratch_shapes=[
            pltpu.VMEM((rows, width), F32),
            pltpu.VMEM((rows, low), F32),
            pltpu.VMEM((rows, low), F32),
            pltpu.VMEM((rows, low), BF16),
        ],
        compiler_params=BIG,
        cost_estimate=pl.CostEstimate(
            flops=6 * rows * width * units, bytes_accessed=6 * width * units, transcendentals=0
        ),
        name="ff_back",
    )(d_ff, b_down, pick, w_down, a_down, gate, up, w_gu, w_gu, b_gu, b_gu, a_gu)


def blocked(parts):
    zeros = lambda a, b: jnp.zeros((a.shape[0], b.shape[1]), a.dtype)
    return jnp.concatenate(
        [
            jnp.concatenate([a if a is b else zeros(a, b) for b in parts], axis=1)
            for a in parts
        ],
        axis=0,
    )


def local(
    layer_input,
    cotangent,
    query_key_value_weight,
    output_weight,
    gate_up_weight,
    down_weight,
    input_first_factor,
    output_first_factor,
    down_first_factor,
    query_key_value_second,
    gate_up_second_factor,
    output_down_second_factor,
    norm_gain_table,
    sequence_adapter,
    block_sequence,
    block_position,
):
    tp, tp_rank = lax.axis_size("tp"), lax.axis_index("tp")
    seqs, seq_rank = lax.axis_size("seq"), lax.axis_index("seq")
    own_rows, width = layer_input.shape
    rows = own_rows * tp
    part = own_rows // 2
    my_blocks = rows // BLK
    cols = query_key_value_weight.shape[2]
    heads = cols // HEAD_DIM
    hidden_cols = gate_up_weight.shape[2]
    k_rows = query_key_value_weight.shape[1]
    slots_a = input_first_factor.shape[2]
    rank_cols = output_first_factor.shape[1]
    group = seqs // heads
    head_rank, group_rank = seq_rank // group, seq_rank % group
    n_seq = sequence_adapter.shape[0]
    groups = (0, 1)

    a_part = k_rows // tp
    b_part = width // tp
    a_mine = lax.dynamic_slice_in_dim(input_first_factor, tp_rank * a_part, a_part, 1)
    b_mine = lax.dynamic_slice_in_dim(output_down_second_factor, tp_rank * b_part, b_part, 2)
    first = jnp.concatenate(
        [
            query_key_value_weight.transpose(1, 0, 2).reshape(k_rows, 3 * cols),
            query_key_value_second.transpose(1, 0, 2).reshape(rank_cols, 3 * cols),
            a_mine[:3].reshape(-1, 3 * cols),
        ],
        axis=0,
    )
    x_parts = [layer_input] + [
        lax.ppermute(layer_input, "tp", [(i, i ^ mask) for i in range(tp)]) for mask in range(1, tp)
    ]
    first = lax.all_gather(first, "seq", axis=0)
    pieces = [
        output_weight.T,
        output_first_factor.T,
        b_mine.reshape(-1, cols),
        a_mine[3:].reshape(-1, cols),
        down_first_factor.T.reshape(-1, cols),
        gate_up_second_factor.reshape(-1, cols),
    ]
    packed = jnp.concatenate(pieces, axis=0)
    first, x_parts, packed, w_gu, w_down = lax.optimization_barrier(
        (
            first,
            x_parts,
            packed,
            gate_up_weight.transpose(1, 0, 2).reshape(k_rows, 2 * hidden_cols),
            down_weight.T,
        )
    )
    packed = lax.all_gather(packed, "seq", axis=0)
    w_gu = lax.all_gather(w_gu, "seq", axis=0, tiled=True)
    w_down = lax.all_gather(w_down, "seq", axis=0, tiled=True)

    tp_order, seq_order = list(range(bits_of(tp))), list(range(bits_of(seqs)))
    a_qkv = first[:, k_rows + rank_cols :].reshape(seqs, 3, a_part, slots_a)
    a_qkv = a_qkv.transpose(0, 2, 1, 3).reshape(seqs, a_part, 3 * slots_a)
    a_parts = [a_qkv] + [
        lax.ppermute(a_qkv, "tp", [(i, i ^ mask) for i in range(tp)]) for mask in range(1, tp)
    ]
    a_qkv = jnp.zeros((seqs, tp, a_part, 3 * slots_a), BF16)
    for mask, value in enumerate(a_parts):
        a_qkv = lax.dynamic_update_slice(a_qkv, value[:, None], (0, tp_rank ^ mask, 0, 0))
    a_qkv = a_qkv.reshape(width, 3 * slots_a)
    b_qkv = first[:, k_rows : k_rows + rank_cols].reshape(slots_a, 3 * cols)
    b_qkv = blocked([b_qkv[:, i * cols : (i + 1) * cols] for i in range(3)])
    runs = row_runs(tp)
    piece_at = jnp.stack([2 * (tp_rank ^ mask) + which for mask, which in runs]).astype(jnp.int32)
    token = (piece_at[:, None] * part + jnp.arange(part, dtype=jnp.int32)[None, :]).reshape(-1)
    token_block, offset = token // BLK, token % BLK
    block_ids = seq_rank * my_blocks + jnp.arange(my_blocks, dtype=jnp.int32)
    place_blocks = block_position[block_ids]
    adapter_blocks = sequence_adapter[block_sequence[block_ids]]
    in_block = token_block[:, None] == jnp.arange(my_blocks, dtype=jnp.int32)[None, :]
    pick = lambda per_block: jnp.sum(jnp.where(in_block, per_block[None, :], 0), axis=1)
    select = (
        jnp.arange(slots_a, dtype=jnp.int32)[None, :] // ADAPTER_RANK
        == pick(adapter_blocks)[:, None]
    ).astype(F32) * 2.0
    half = rows // 2
    selects = [select[:half], select[half:]]
    start = jnp.where(place_blocks < PROMPT_BLOCKS, place_blocks, PROMPT_BLOCKS) * BLK
    position = pick(start) + offset
    frequency = THETA ** (-(jnp.arange(HEAD_DIM // 2, dtype=F32) * 2.0) / HEAD_DIM)
    angles = position.astype(F32)[:, None] * frequency[None, :]
    cosine, sine = jnp.cos(angles), jnp.sin(angles)
    cs = jnp.concatenate([cosine, cosine, -sine, sine], axis=1)

    owner = (
        ((head_rank - jnp.arange(heads)) % heads)[None, :] * group
        + ((group_rank + jnp.arange(group)) % group)[:, None]
    ).reshape(-1)
    held = (owner[:, None] * my_blocks + jnp.arange(my_blocks)[None, :]).reshape(-1)
    held_seq = block_sequence[held].astype(jnp.int32)
    held_place = block_position[held].astype(jnp.int32)
    prompt_count = n_seq * PROMPT_BLOCKS
    wanted = jnp.arange(prompt_count, dtype=jnp.int32)
    code = jnp.where(held_place < PROMPT_BLOCKS, held_seq * PROMPT_BLOCKS + held_place, -1)
    prompt_at = jnp.sum(
        jnp.where(
            code[None, :] == wanted[:, None], jnp.arange(held.shape[0], dtype=jnp.int32)[None, :], 0
        ),
        axis=1,
    ).astype(jnp.int32)
    own_blocks = heads * my_blocks
    tables = (held_seq[:own_blocks], held_place[:own_blocks], prompt_at)
    head_order = ((head_rank + jnp.arange(heads)) % heads).astype(jnp.int32)

    def head_shift(value, by):
        if by == 0:
            return value
        return lax.ppermute(
            value,
            "seq",
            [
                (h * group + j, ((h + by) % heads) * group + j)
                for h in range(heads)
                for j in range(group)
            ],
        )

    def group_shift(value, by):
        return lax.ppermute(
            value,
            "seq",
            [
                (h * group + j, h * group + (j + by) % group)
                for h in range(heads)
                for j in range(group)
            ],
        )

    own = lambda value, i: value[i * part : (i + 1) * part].astype(F32)
    x = jnp.concatenate(
        [x_parts[mask][which * part : (which + 1) * part] for mask, which in runs], axis=0
    )
    gain = lax.dynamic_slice_in_dim(norm_gain_table[:2], tp_rank * cols, cols, 1)
    pick3 = jnp.tile(select, (1, 3))
    latents = (mm(x, a_qkv) * pick3).astype(BF16)
    z, squares = qkv_product(
        x, latents, first, first[:, k_rows : k_rows + rank_cols].reshape(slots_a, 3 * cols), k_rows, cols
    )
    squares = sum_rows(squares[:2].reshape(2, rows), tp)
    inv = lax.rsqrt(squares / width + EPS)
    inv, packed = lax.optimization_barrier((inv, packed))
    split, at = [], 0
    for piece in pieces:
        split.append(packed[:, at : at + piece.shape[0]])
        at += piece.shape[0]
    w_o = split[0].reshape(width, cols)
    a_o = split[1].reshape(slots_a, cols).T
    shared = gather_order(jnp.concatenate(split[2:4], axis=1), "tp", tp, tp_order)
    b_size = split[2].shape[1]
    b_od = (
        shared[:, :, :b_size]
        .reshape(tp, seqs, 2, rank_cols, b_part)
        .transpose(2, 1, 3, 0, 4)
        .reshape(2, slots_a, width)
    )
    a_gu = (
        shared[:, :, b_size:]
        .reshape(tp, seqs, 2, a_part, slots_a)
        .transpose(1, 0, 3, 2, 4)
        .reshape(width, 2 * slots_a)
    )
    a_down = split[4].reshape(slots_a, hidden_cols).T
    b_gu = (
        split[5]
        .reshape(seqs, 2, rank_cols, hidden_cols)
        .transpose(1, 0, 2, 3)
        .reshape(2 * slots_a, hidden_cols)
    )
    spread = spread_heads(head_order, piece_at, z, inv.T, cs, gain, heads)
    near = [head_shift(spread[k], k) for k in range(heads)]
    far = [group_shift(near[k][1:], -j) for j in range(1, group) for k in range(heads)]
    attended = attend(tables, near, far, prompt_count)
    heads_out = collect_heads(
        head_order, piece_at, [head_shift(attended[k], -k) for k in range(heads)]
    )

    def norm_back(values_in, inv, scaled):
        return inv * scaled - values_in * inv**3 * jnp.mean(scaled * values_in, axis=1, keepdims=True)

    def inverse_norm(values_in):
        return lax.rsqrt(jnp.mean(values_in * values_in, axis=1, keepdims=True) + EPS)

    *far_part, o_latent1 = add_product(heads_out[1], w_o, a_o, b_od[0], selects[1], 2)
    near_part, o_latent0 = add_product(heads_out[0], w_o, a_o, b_od[0], selects[0], 1)
    attn_out = scatter_groups(near_part, far_part, tp)
    scale_o = [inverse_norm(value) for value in attn_out]
    hidden = [
        own(layer_input, i) + attn_out[i] * scale_o[i] * norm_gain_table[2] for i in groups
    ]
    h_low = gather_groups([value.astype(BF16) for value in hidden], tp)

    gates, ups, acts, gu_latents = zip(
        *[gate_up_product(h_low[g], w_gu, a_gu, b_gu, selects[g]) for g in groups]
    )
    acts, w_down = lax.optimization_barrier((acts, w_down))
    *far_part, d_latent1 = add_product(acts[1], w_down, a_down, b_od[1], selects[1], 2)
    near_part, d_latent0 = add_product(acts[0], w_down, a_down, b_od[1], selects[0], 1)
    ff_out = scatter_groups(near_part, far_part, tp)
    scale_f = [inverse_norm(value) for value in ff_out]
    output = jnp.concatenate(
        [hidden[i] + ff_out[i] * scale_f[i] * norm_gain_table[3] for i in groups], axis=0
    )

    d_ffs = gather_groups(
        [
            norm_back(ff_out[i], scale_f[i], own(cotangent, i) * norm_gain_table[3]).astype(BF16)
            for i in groups
        ],
        tp,
    )
    backs = [
        ff_back(
            d_ffs[g], b_od[1], selects[g], w_down, a_down, gates[g], ups[g], w_gu, b_gu, a_gu, 1 + g
        )
        for g in groups
    ]
    summed = scatter_groups(backs[0][0], backs[1][:2], tp)
    d_gates, d_ups, u_gus, u_downs = zip(*[back[-4:] for back in backs])
    d_hidden = [own(cotangent, i) + summed[i] for i in groups]
    d_attn = [
        norm_back(attn_out[i], scale_o[i], d_hidden[i] * norm_gain_table[2]).astype(BF16)
        for i in groups
    ]
    d_latents = (d_latent0, d_latent1)
    d_rows = gather_groups(d_attn, tp)
    o_latents = (o_latent0, o_latent1)
    u_os, grads = [], []
    for g in groups:
        u_os.append((mm_nt(d_rows[g], b_od[0]) * selects[g]).astype(BF16))
        d_heads = (mm(d_rows[g], w_o) + mm_nt(u_os[g], a_o)).astype(BF16)
        grads.append(
            [
                head_shift(
                    lax.dynamic_slice_in_dim(d_heads, head_order[k] * HEAD_DIM, HEAD_DIM, 1), k
                )
                for k in range(heads)
            ]
        )
    grads = [grads[g][k] for k in range(heads) for g in groups]
    results = list(attend_back(tables, piece_at, near, far, grads, prompt_count))
    dqs = [head_shift(results[k], -k) for k in range(heads)]
    d_kv = results[heads].reshape(2, heads, rows, HEAD_DIM)
    others = [
        group_shift(results[heads + j], j).reshape(2, heads, rows, HEAD_DIM) for j in range(1, group)
    ]
    dkvs = []
    for k in range(heads):
        total = d_kv[:, k].astype(F32)
        for other in others:
            total = total + other[:, k].astype(F32)
        dkvs.append(head_shift(total.astype(BF16), -k))
    dkvs[1], u_os, o_latents, u_downs, d_latents, u_gus, gu_latents = lax.optimization_barrier(
        (dkvs[1], u_os, o_latents, u_downs, d_latents, u_gus, gu_latents)
    )
    both_groups = lambda f: f(0) + f(1)
    grad_a_down = both_groups(lambda g: mm_tn(u_downs[g], acts[g]))
    grad_b_down = both_groups(lambda g: mm_tn(d_latents[g], d_ffs[g]))
    grad_a_gu = both_groups(lambda g: mm_tn(h_low[g], u_gus[g]))
    grad_b_gate = both_groups(lambda g: mm_tn(gu_latents[g][:, :slots_a], d_gates[g]))
    grad_b_up = both_groups(lambda g: mm_tn(gu_latents[g][:, slots_a:], d_ups[g]))
    lane = 2 * slots_a
    shards = lambda value: value.astype(BF16).reshape(seqs, -1, lane)
    early = jnp.concatenate(
        [
            shards(grad_a_gu),
            shards(grad_b_down),
            shards(grad_a_down),
            shards(grad_b_gate),
            shards(grad_b_up),
        ],
        axis=1,
    )
    grad_a_o = both_groups(lambda g: mm_tn(u_os[g], heads_out[g]))
    grad_b_o = both_groups(lambda g: mm_tn(o_latents[g], d_rows[g]))
    late_o = jnp.concatenate(
        [
            grad_b_o.astype(BF16).reshape(seqs, -1, cols),
            grad_a_o.astype(BF16).reshape(seqs, -1, cols),
        ],
        axis=1,
    )
    dqs, dkvs, early, late_o = lax.optimization_barrier((dqs, dkvs, early, late_o))
    early = lax.psum_scatter(early, "seq", scatter_dimension=0, tiled=False)
    late_o = scatter_order(late_o, "seq", seqs, seq_order)
    scaled, parts = unturn_heads(head_order, piece_at, dqs, dkvs, z, cs, gain)
    parts = sum_rows(parts.T, tp) / width
    coef = jnp.concatenate([inv, inv**3 * parts], axis=0)
    dz = norm_back_heads(head_order, piece_at, dkvs, scaled, z, coef.T)
    us = (mm_nt(dz, b_qkv) * pick3).astype(BF16)
    grad_a_qkv = mm_tn(x, us)
    grad_b_qkv = mm_tn(latents, dz)
    lane3 = 3 * slots_a
    grad_b_qkv = jnp.concatenate(
        [
            grad_b_qkv[i * slots_a : (i + 1) * slots_a, i * cols : (i + 1) * cols]
            for i in range(3)
        ],
        axis=1,
    )
    late = jnp.concatenate(
        [
            grad_a_qkv.astype(BF16).reshape(seqs, k_rows, lane3),
            grad_b_qkv.astype(BF16).reshape(seqs, -1, lane3),
        ],
        axis=1,
    )
    dz, late = lax.optimization_barrier((dz, late))
    far_part = list(back_product(dz, 1, first, k_rows, us, a_qkv, 2))
    far_part[0], dz = lax.optimization_barrier((far_part[0], dz))
    (near_part,) = back_product(dz, 0, first, k_rows, us, a_qkv, 1)
    near_part, early, late_o = lax.optimization_barrier((near_part, early, late_o))

    down_size = rank_cols * width // lane
    o_size = rank_cols * width // cols
    both = jnp.concatenate(
        [early[: k_rows + down_size], late_o[:o_size].astype(BF16).reshape(-1, lane)], axis=0
    )
    both = both + flip(both, "tp", tp, 0)
    totals = scatter_first(near_part, far_part, tp)
    late = scatter_order(late, "seq", seqs, seq_order)
    totals, both, late = lax.optimization_barrier((totals, both, late))
    for bit in range(1, bits_of(tp)):
        both = both + flip(both, "tp", tp, bit)
    both = both.astype(F32)
    summed = scatter_rest(totals, tp)
    input_grad = jnp.concatenate([d_hidden[i] + summed[i] for i in groups], axis=0)
    grad_a_qkv = sum_all(late[:k_rows].astype(BF16), "tp", tp).astype(F32)
    grad_a_gu = both[:k_rows]
    grad_b_down = both[k_rows : k_rows + down_size].reshape(rank_cols, width)
    grad_b_o = both[k_rows + down_size :].reshape(rank_cols, width)
    a_size = rank_cols * hidden_cols // lane
    rest = early[k_rows + down_size :].astype(F32)
    grad_a_down = rest[:a_size].reshape(rank_cols, hidden_cols).T
    grad_b_gu = rest[a_size:].reshape(2, rank_cols, hidden_cols)
    grad_a_o = late_o[o_size:].T
    grad_b_qkv = late[k_rows:].reshape(rank_cols, 3, cols).transpose(1, 0, 2)
    grad_a_in = jnp.stack(
        [grad_a_qkv[:, i * slots_a : (i + 1) * slots_a] for i in range(3)]
        + [grad_a_gu[:, i * slots_a : (i + 1) * slots_a] for i in range(2)]
    )
    grad_b_out = jnp.stack([grad_b_o, grad_b_down])
    return (output, input_grad, grad_a_in, grad_a_o, grad_a_down, grad_b_qkv, grad_b_gu, grad_b_out)


def solution(mesh):
    return jax.shard_map(
        local,
        mesh=mesh,
        in_specs=(
            P(("seq", "tp"), None),
            P(("seq", "tp"), None),
            P(None, "seq", "tp"),
            P("tp", "seq"),
            P(None, "seq", "tp"),
            P("tp", "seq"),
            P(None, "seq", None),
            P("tp", "seq"),
            P("tp", "seq"),
            P(None, "seq", "tp"),
            P(None, "seq", "tp"),
            P(None, "seq", None),
            P(),
            P(),
            P(),
            P(),
        ),
        out_specs=(
            P(("seq", "tp"), None),
            P(("seq", "tp"), None),
            P(None, "seq", None),
            P("tp", "seq"),
            P("tp", "seq"),
            P(None, "seq", "tp"),
            P(None, "seq", "tp"),
            P(None, "seq", None),
        ),
        check_vma=False,
    )
```

```python
import functools

import jax
import jax.numpy as jnp
from jax import lax
from jax.experimental import pallas as pl
from jax.experimental.pallas import tpu as pltpu
from jax.sharding import PartitionSpec as P

HEAD_DIM = 128
ADAPTER_RANK = 16
BLK = 128
PROMPT_BLOCKS = 8
EPS = 1e-06
THETA = 500000.0
NEG = -1e30
LOG2E = 1.4426950408889634
F32 = jnp.float32
BF16 = jnp.bfloat16


def mm(a, b):
    return jnp.dot(a, b, preferred_element_type=F32)


def mm_nt(a, b):
    return lax.dot_general(a, b, (((1,), (1,)), ((), ())), preferred_element_type=F32)


def mm_tn(a, b):
    return lax.dot_general(a, b, (((0,), (0,)), ((), ())), preferred_element_type=F32)


def bits_of(count):
    n = count.bit_length() - 1
    assert 1 << n == count
    return n


def flip(value, axis, count, bit):
    return lax.ppermute(value, axis, [(i, i ^ (1 << bit)) for i in range(count)])


def gather_order(value, axis, count, order):
    rank = lax.axis_index(axis)
    have = []
    current = value
    for bit in order:
        other = flip(current, axis, count, bit)
        mine_low = ((rank >> bit) & 1) == 0
        at = len([b for b in have if b > bit])
        low = jnp.where(mine_low, current, other)
        high = jnp.where(mine_low, other, current)
        current = jnp.stack([low, high], axis=at)
        have = sorted(have + [bit], reverse=True)
    return current.reshape((count,) + value.shape)


def scatter_order(value, axis, count, order):
    n = bits_of(count)
    rank = lax.axis_index(axis)
    current = value.reshape((2,) * n + value.shape[1:])
    have = list(range(n - 1, -1, -1))
    for bit in order:
        at = have.index(bit)
        mine = (rank >> bit) & 1
        keep = lax.dynamic_index_in_dim(current, mine, at, keepdims=False)
        give = lax.dynamic_index_in_dim(current, 1 - mine, at, keepdims=False)
        got = flip(give.astype(BF16), axis, count, bit)
        current = keep.astype(F32) + got.astype(F32)
        have.remove(bit)
    return current


def part_orders(count):
    order = list(range(bits_of(count)))
    return (order, order[::-1])


def group_masks(count):
    groups = ([], [])
    for part, order in enumerate(part_orders(count)):
        for j in range(count):
            mask = sum(1 << bit for i, bit in enumerate(order) if (j >> i) & 1)
            groups[j >= count // 2].append((mask, part))
    return groups


def row_runs(count):
    return [run for masks in group_masks(count) for run in masks]


def gather_groups(parts, count, beside=None):
    near, far = [], []
    for value, order in zip(parts, part_orders(count)):
        for bit in order[:-1]:
            value = jnp.concatenate([value, flip(value, "tp", count, bit)], axis=0)
        near.append(value)
    if beside is not None:
        near[1], beside = lax.optimization_barrier((near[1], beside))
    for value, order in zip(near, part_orders(count)):
        far.append(flip(value, "tp", count, order[-1]))
    if beside is not None:
        return jnp.concatenate(near, axis=0), jnp.concatenate(far, axis=0), beside
    return jnp.concatenate(near, axis=0), jnp.concatenate(far, axis=0)


def scatter_groups(near, far, count):
    return scatter_rest(scatter_first(near, far, count), count)


def scatter_first(near, far, count):
    out = []
    size = near.shape[0] // 2
    for i, order in enumerate(part_orders(count)):
        got = flip(far[i], "tp", count, order[-1])
        out.append(near[i * size : (i + 1) * size].astype(F32) + got.astype(F32))
    return out


def scatter_rest(totals, count):
    out = []
    for total, order in zip(totals, part_orders(count)):
        for bit in order[-2::-1]:
            half = total.shape[0] // 2
            got = flip(total[half:].astype(BF16), "tp", count, bit)
            total = total[:half] + got.astype(F32)
        out.append(total)
    return out


def sum_rows(value, count):
    runs = row_runs(count)
    value = value.reshape(value.shape[0], len(runs), -1)
    total = value
    for mask in range(1, count):
        got = lax.ppermute(value, "tp", [(i, i ^ mask) for i in range(count)])
        order = [runs.index((other ^ mask, which)) for other, which in runs]
        total = total + jnp.concatenate([got[:, j : j + 1] for j in order], axis=1)
    return total.reshape(value.shape[0], -1)


def sum_all(value, axis, count):
    for bit in range(bits_of(count)):
        value = value + flip(value, axis, count, bit)
    return value


def copy_all(pairs, sem):
    copies = [pltpu.make_async_copy(src, dst, sem.at[i]) for i, (src, dst) in enumerate(pairs)]
    for copy in copies:
        copy.start()
    for copy in copies:
        copy.wait()


def gather_prompt(prompt_at, source, target, count):
    def step(i, carry):
        start = pl.multiple_of(prompt_at[i] * BLK, BLK)
        target[pl.ds(pl.multiple_of(i * BLK, BLK), BLK), :] = source[pl.ds(start, BLK), :]
        return carry

    lax.fori_loop(0, count, step, 0)


def masked_scores(keys, own_keys, queries, place, scale):
    prompt = mm_nt(keys, queries) * scale
    block = lax.broadcasted_iota(jnp.int32, prompt.shape, 0) // BLK
    prompt = jnp.where(block < place, prompt, NEG)
    own = mm_nt(own_keys, queries) * scale
    causal = lax.broadcasted_iota(jnp.int32, own.shape, 0) <= lax.broadcasted_iota(
        jnp.int32, own.shape, 1
    )
    own = jnp.where(causal, own, NEG)
    top = jnp.maximum(jnp.max(prompt, axis=0, keepdims=True), jnp.max(own, axis=0, keepdims=True))
    prompt = jnp.exp2(prompt - top)
    own = jnp.exp2(own - top)
    total = jnp.sum(prompt, axis=0, keepdims=True) + jnp.sum(own, axis=0, keepdims=True)
    return prompt, own, 1.0 / total


def load_plan(slots, group, rows, refs, q_buf, k_buf, v_buf):
    plan = []
    for i in range(slots):
        plan.append((refs[i].at[0], q_buf.at[pl.ds(i * rows, rows)]))
    for i in range(slots * group):
        at = pl.ds(i * rows, rows)
        skip = int(i < slots)
        plan += [(refs[i].at[skip], k_buf.at[at]), (refs[i].at[skip + 1], v_buf.at[at])]
    return plan


def attend_kernel(slots, group, rows, prompt_count, q_seq, q_place, prompt_at, *refs):
    n_in = slots * group
    outs = refs[n_in : n_in + slots]
    q_buf, k_buf, v_buf, kp, vp, o_buf, sem = refs[n_in + slots :]
    copy_all(load_plan(slots, group, rows, refs, q_buf, k_buf, v_buf), sem)
    gather_prompt(prompt_at, k_buf, kp, prompt_count)
    gather_prompt(prompt_at, v_buf, vp, prompt_count)
    scale = HEAD_DIM ** (-0.5) * LOG2E
    span = PROMPT_BLOCKS * BLK

    def block(i):
        at = pl.ds(pl.multiple_of(i * BLK, BLK), BLK)
        of_seq = pl.ds(pl.multiple_of(q_seq[i] * span, span), span)
        prompt, own, inverse = masked_scores(
            kp[of_seq, :], k_buf[at, :], q_buf[at, :], q_place[i], scale
        )
        result = mm_tn(vp[of_seq, :], prompt.astype(BF16)) + mm_tn(v_buf[at, :], own.astype(BF16))
        return at, (result * inverse).T.astype(BF16)

    blocks = slots * rows // BLK
    pair = 2 if blocks % 2 == 0 else 1

    def step(i, carry):
        for at, result in [block(i * pair + j) for j in range(pair)]:
            o_buf[at, :] = result
        return carry

    lax.fori_loop(0, blocks // pair, step, 0)
    copy_all([(o_buf.at[pl.ds(i * rows, rows)], outs[i]) for i in range(slots)], sem)


def attend_back_kernel(
    slots, group, rows, pieces, prompt_count, q_seq, q_place, prompt_at, piece_at, *refs
):
    n_in = slots * group
    n_grad = slots * 2
    grads = refs[n_in : n_in + n_grad]
    outs = refs[n_in + n_grad : n_in + n_grad + slots]
    near_out = refs[n_in + n_grad + slots]
    rest = refs[n_in + n_grad + slots + 1 :]
    far_outs, rest = rest[: group - 1], rest[group - 1 :]
    q_buf, k_buf, v_buf, do_buf, kp, vp, dkp, dvp, dq_buf, dkv_buf, sem = rest
    plan = load_plan(slots, group, rows, refs, q_buf, k_buf, v_buf)
    size = rows // pieces
    for i in range(slots):
        for p in range(pieces):
            half, at = divmod(p, pieces // 2)
            to = pl.multiple_of(i * rows + piece_at[p] * size, 16)
            plan.append(
                (grads[i * 2 + half].at[pl.ds(at * size, size)], do_buf.at[pl.ds(to, size)])
            )
    copy_all(plan, sem)
    gather_prompt(prompt_at, k_buf, kp, prompt_count)
    gather_prompt(prompt_at, v_buf, vp, prompt_count)
    dkp[...] = jnp.zeros_like(dkp)
    dvp[...] = jnp.zeros_like(dvp)
    scale = HEAD_DIM ** (-0.5)
    span = PROMPT_BLOCKS * BLK
    own_rows = slots * rows
    zeros = jnp.zeros((BLK, HEAD_DIM), BF16)

    def rows_of(i):
        return pl.ds(pl.multiple_of(i * BLK, BLK), BLK)

    def clear(i, carry):
        for j in range(1, group):
            dkv_buf[j, 0, rows_of(i), :] = zeros
            dkv_buf[j, 1, rows_of(i), :] = zeros
        return carry

    lax.fori_loop(0, own_rows // BLK, clear, 0)

    def block(i):
        at = rows_of(i)
        seq, place = q_seq[i], q_place[i]
        of_seq = pl.ds(pl.multiple_of(seq * span, span), span)
        queries, grad = q_buf[at, :], do_buf[at, :]
        prompt, own, inverse = masked_scores(
            kp[of_seq, :], k_buf[at, :], queries, place, scale * LOG2E
        )
        prompt, own = prompt * inverse, own * inverse
        d_prompt = mm_nt(vp[of_seq, :], grad)
        d_own = mm_nt(v_buf[at, :], grad)
        delta = jnp.sum(prompt * d_prompt, axis=0, keepdims=True) + jnp.sum(
            own * d_own, axis=0, keepdims=True
        )
        ds_prompt = (prompt * (d_prompt - delta)).astype(BF16)
        ds_own = (own * (d_own - delta)).astype(BF16)
        dq = mm_tn(ds_prompt, kp[of_seq, :]) + mm_tn(ds_own, k_buf[at, :])
        return (
            at,
            of_seq,
            (dq * scale).astype(BF16),
            mm(prompt.astype(BF16), grad),
            mm(ds_prompt, queries) * scale,
            (mm(ds_own, queries) * scale).astype(BF16),
            mm(own.astype(BF16), grad).astype(BF16),
        )

    blocks = own_rows // BLK
    pair = 2 if blocks % 2 == 0 else 1

    def step(i, carry):
        for at, of_seq, dq, dv_prompt, dk_prompt, dk_own, dv_own in [
            block(i * pair + j) for j in range(pair)
        ]:
            dq_buf[at, :] = dq
            dvp[of_seq, :] += dv_prompt
            dkp[of_seq, :] += dk_prompt
            dkv_buf[0, 0, at, :] = dk_own
            dkv_buf[0, 1, at, :] = dv_own
        return carry

    lax.fori_loop(0, blocks // pair, step, 0)

    def spread(i, carry):
        place = prompt_at[i]
        j, to = place // blocks, rows_of(place % blocks)
        dkv_buf[j, 0, to, :] = (dkv_buf[j, 0, to, :].astype(F32) + dkp[rows_of(i), :]).astype(BF16)
        dkv_buf[j, 1, to, :] = (dkv_buf[j, 1, to, :].astype(F32) + dvp[rows_of(i), :]).astype(BF16)
        return carry

    lax.fori_loop(0, prompt_count, spread, 0)
    plan = [(dq_buf.at[pl.ds(i * rows, rows)], outs[i]) for i in range(slots)]
    plan.append((dkv_buf.at[0], near_out))
    plan += [(dkv_buf.at[j], far_outs[j - 1]) for j in range(1, group)]
    copy_all(plan, sem)


ANY = pl.BlockSpec(memory_space=pl.ANY)


def attend(tables, near, far, prompt_count):
    slots = len(near)
    rows = near[0].shape[1]
    group = 1 + len(far) // slots
    own, every = slots * rows, slots * group * rows
    pairs = own * (PROMPT_BLOCKS + 1) * BLK
    wide = lambda count, kind=BF16: pltpu.VMEM((count, HEAD_DIM), kind)
    return pl.pallas_call(
        functools.partial(attend_kernel, slots, group, rows, prompt_count),
        out_shape=[jax.ShapeDtypeStruct((rows, HEAD_DIM), BF16)] * slots,
        grid_spec=pltpu.PrefetchScalarGridSpec(
            num_scalar_prefetch=3,
            in_specs=[ANY] * (slots * group),
            out_specs=[ANY] * slots,
            scratch_shapes=[
                wide(own),
                wide(every),
                wide(every),
                wide(prompt_count * BLK),
                wide(prompt_count * BLK),
                wide(own),
                pltpu.SemaphoreType.DMA((slots + 2 * slots * group,)),
            ],
        ),
        cost_estimate=pl.CostEstimate(
            flops=4 * pairs * HEAD_DIM, bytes_accessed=6 * every * HEAD_DIM, transcendentals=pairs
        ),
        name="attend",
    )(*tables, *near, *far)


def attend_back(tables, piece_at, near, far, grads, prompt_count):
    pieces = piece_at.shape[0]
    slots = len(near)
    rows = near[0].shape[1]
    group = 1 + len(far) // slots
    own, every = slots * rows, slots * group * rows
    pairs = own * (PROMPT_BLOCKS + 1) * BLK
    wide = lambda count, kind=BF16: pltpu.VMEM((count, HEAD_DIM), kind)
    return pl.pallas_call(
        functools.partial(attend_back_kernel, slots, group, rows, pieces, prompt_count),
        out_shape=[jax.ShapeDtypeStruct((rows, HEAD_DIM), BF16)] * slots
        + [jax.ShapeDtypeStruct((2, own, HEAD_DIM), BF16)] * group,
        grid_spec=pltpu.PrefetchScalarGridSpec(
            num_scalar_prefetch=4,
            in_specs=[ANY] * (slots * group + 2 * slots),
            out_specs=[ANY] * (slots + group),
            scratch_shapes=[
                wide(own),
                wide(every),
                wide(every),
                wide(own),
                wide(prompt_count * BLK),
                wide(prompt_count * BLK),
                wide(prompt_count * BLK, F32),
                wide(prompt_count * BLK, F32),
                wide(own),
                pltpu.VMEM((group, 2, own, HEAD_DIM), BF16),
                pltpu.SemaphoreType.DMA((slots + 2 * slots * group + slots * pieces,)),
            ],
        ),
        cost_estimate=pl.CostEstimate(
            flops=10 * pairs * HEAD_DIM, bytes_accessed=12 * every * HEAD_DIM, transcendentals=pairs
        ),
        name="attend_back",
    )(*tables, piece_at, *near, *far, *grads)


def turn(values, cosine, sine):
    return values * cosine + pltpu.roll(values, HEAD_DIM // 2, 1) * sine


def lanes(head, base=0):
    return pl.ds(pl.multiple_of(base + head * HEAD_DIM, HEAD_DIM), HEAD_DIM)


def piece_rows(index, size):
    return pl.ds(pl.multiple_of(index * size, 16), size)


def spread_kernel(slots, pieces, order, piece_at, z, inv, cs, gain, *outs):
    cols = slots * HEAD_DIM
    size = z.shape[0] // pieces

    def step(p, carry):
        at, to = piece_rows(p, size), piece_rows(piece_at[p], size)
        cosine, sine = cs[at, :HEAD_DIM], cs[at, HEAD_DIM:]
        for which in range(2):
            factor = inv[at, which : which + 1]
            for k in range(slots):
                head = order[k]
                scaled = z[at, lanes(head, which * cols)] * factor
                scaled = scaled * gain[which : which + 1, lanes(head)]
                turned = turn(scaled, cosine, sine).astype(BF16)
                outs[k][which, to, :] = turned
        for k in range(slots):
            outs[k][2, to, :] = z[at, lanes(order[k], 2 * cols)].astype(BF16)
        return carry

    lax.fori_loop(0, pieces, step, 0)


WHOLE = pl.BlockSpec(memory_space=pltpu.VMEM)
BIG = pltpu.CompilerParams(vmem_limit_bytes=56 * 1024 * 1024)


def spread_heads(order, piece_at, z, inv, cs, gain, slots):
    rows = z.shape[0]
    return pl.pallas_call(
        functools.partial(spread_kernel, slots, piece_at.shape[0]),
        out_shape=[jax.ShapeDtypeStruct((3, rows, HEAD_DIM), BF16)] * slots,
        grid_spec=pltpu.PrefetchScalarGridSpec(
            num_scalar_prefetch=2, in_specs=[WHOLE] * 4, out_specs=[WHOLE] * slots
        ),
        compiler_params=BIG,
        name="spread_heads",
    )(order, piece_at, z, inv, cs, gain)


def collect_kernel(slots, pieces, order, piece_at, *refs):
    outs = refs[slots:]
    size = refs[0].shape[0] // pieces
    for p in range(pieces):
        half, at = divmod(p, pieces // 2)
        for k in range(slots):
            outs[half][pl.ds(at * size, size), lanes(order[k])] = refs[k][
                piece_rows(piece_at[p], size), :
            ]


def collect_heads(order, piece_at, parts):
    slots = len(parts)
    rows = parts[0].shape[0]
    return pl.pallas_call(
        functools.partial(collect_kernel, slots, piece_at.shape[0]),
        out_shape=[jax.ShapeDtypeStruct((rows // 2, slots * HEAD_DIM), BF16)] * 2,
        grid_spec=pltpu.PrefetchScalarGridSpec(
            num_scalar_prefetch=2, in_specs=[WHOLE] * slots, out_specs=[WHOLE] * 2
        ),
        name="collect_heads",
    )(order, piece_at, *parts)


def unturn_kernel(slots, pieces, order, piece_at, *refs):
    dqs, dkvs, rest = refs[:slots], refs[slots : 2 * slots], refs[2 * slots :]
    z, cs, gain, scaled_out, part_out = rest
    cols = slots * HEAD_DIM
    size = z.shape[0] // pieces

    def step(p, carry):
        at, source = piece_rows(p, size), piece_rows(piece_at[p], size)
        cosine, sine = cs[at, :HEAD_DIM], cs[at, HEAD_DIM:]
        for which in range(2):
            total = jnp.zeros((size, HEAD_DIM), F32)
            for k in range(slots):
                head = order[k]
                grad = dqs[k][source, :] if which == 0 else dkvs[k][0, source, :]
                grad = turn(grad.astype(F32), cosine, -sine) * gain[which : which + 1, lanes(head)]
                scaled_out[at, lanes(head, which * cols)] = grad
                total = total + grad * z[at, lanes(head, which * cols)]
            part_out[at, which : which + 1] = jnp.sum(total, axis=1, keepdims=True)
        return carry

    lax.fori_loop(0, pieces, step, 0)


def unturn_heads(order, piece_at, dqs, dkvs, z, cs, gain):
    slots = len(dqs)
    rows = z.shape[0]
    cols = slots * HEAD_DIM
    return pl.pallas_call(
        functools.partial(unturn_kernel, slots, piece_at.shape[0]),
        out_shape=[
            jax.ShapeDtypeStruct((rows, 2 * cols), F32),
            jax.ShapeDtypeStruct((rows, 2), F32),
        ],
        grid_spec=pltpu.PrefetchScalarGridSpec(
            num_scalar_prefetch=2, in_specs=[WHOLE] * (2 * slots + 3), out_specs=[WHOLE] * 2
        ),
        compiler_params=BIG,
        name="unturn_heads",
    )(order, piece_at, *dqs, *dkvs, z, cs, gain)


def norm_back_kernel(slots, pieces, order, piece_at, *refs):
    dkvs, (scaled, z, coef, out) = refs[:slots], refs[slots:]
    cols = slots * HEAD_DIM
    size = z.shape[0] // pieces

    def step(p, carry):
        at, source = piece_rows(p, size), piece_rows(piece_at[p], size)
        for which in range(2):
            to = slice(which * cols, (which + 1) * cols)
            out[at, to] = (
                scaled[at, to] * coef[at, which : which + 1]
                - z[at, to] * coef[at, 2 + which : 3 + which]
            ).astype(BF16)
        for k in range(slots):
            out[at, lanes(order[k], 2 * cols)] = dkvs[k][1, source, :]
        return carry

    lax.fori_loop(0, pieces, step, 0)


def norm_back_heads(order, piece_at, dkvs, scaled, z, coef):
    slots = len(dkvs)
    return pl.pallas_call(
        functools.partial(norm_back_kernel, slots, piece_at.shape[0]),
        out_shape=jax.ShapeDtypeStruct(z.shape, BF16),
        grid_spec=pltpu.PrefetchScalarGridSpec(
            num_scalar_prefetch=2, in_specs=[WHOLE] * (slots + 3), out_specs=WHOLE
        ),
        compiler_params=BIG,
        name="norm_back_heads",
    )(order, piece_at, *dkvs, scaled, z, coef)


def fixed(*shape, at=None):
    place = at or (0,) * len(shape)
    return pl.BlockSpec(shape, lambda i: place)


def flat(value):
    return value.reshape(-1, value.shape[-1])


def qkv_kernel(x, latent, weight, second, z, squares):
    i = pl.program_id(0)
    result = mm(x[...], flat(weight[...])) + mm(latent[...], flat(second[...]))
    z[...] = result
    squares[0, :, :] = jnp.sum(result * result, axis=1, keepdims=True)


def qkv_product(x, latents, first, second, k_rows, cols):
    rows, width = x.shape
    shards, _, total = first.shape
    low = latents.shape[1] // 3
    return pl.pallas_call(
        qkv_kernel,
        grid=(3,),
        out_shape=[
            jax.ShapeDtypeStruct((rows, total), F32),
            jax.ShapeDtypeStruct((3, rows, 1), F32),
        ],
        in_specs=[
            fixed(rows, width),
            pl.BlockSpec((rows, low), lambda i: (0, i)),
            pl.BlockSpec((shards, k_rows, cols), lambda i: (0, 0, i)),
            pl.BlockSpec((low, cols), lambda i: (0, i)),
        ],
        out_specs=[
            pl.BlockSpec((rows, cols), lambda i: (0, i)),
            pl.BlockSpec((1, rows, 1), lambda i: (i, 0, 0)),
        ],
        compiler_params=BIG,
        cost_estimate=pl.CostEstimate(
            flops=2 * rows * width * total, bytes_accessed=2 * first.size, transcendentals=0
        ),
        name="qkv_product",
    )(x, latents, first, second)


def add_kernel(parts, a, weight, first, second, pick, *refs):
    outs, (latent_out, latent) = refs[:parts], refs[parts:]

    @pl.when(pl.program_id(0) == 0)
    def _():
        latent[...] = (mm(a[...], first[...]) * pick[...]).astype(BF16)
        latent_out[...] = latent[...]

    result = mm_nt(a[...], weight[...]) + mm(latent[...], second[...])
    size = result.shape[0] // parts
    for i in range(parts):
        outs[i][...] = result[i * size : (i + 1) * size].astype(BF16)


def add_product(a, weight, first, second, pick, parts, tile=512):
    rows, depth = a.shape
    width, low = weight.shape[0], first.shape[1]
    size = rows // parts
    return pl.pallas_call(
        functools.partial(add_kernel, parts),
        grid=(width // tile,),
        out_shape=[jax.ShapeDtypeStruct((size, width), BF16)] * parts
        + [jax.ShapeDtypeStruct((rows, low), BF16)],
        in_specs=[
            fixed(rows, depth),
            pl.BlockSpec((tile, depth), lambda i: (i, 0)),
            fixed(depth, low),
            pl.BlockSpec((low, tile), lambda i: (0, i)),
            fixed(rows, low),
        ],
        out_specs=[pl.BlockSpec((size, tile), lambda i: (0, i))] * parts + [fixed(rows, low)],
        scratch_shapes=[pltpu.VMEM((rows, low), BF16)],
        compiler_params=BIG,
        cost_estimate=pl.CostEstimate(
            flops=2 * rows * width * depth, bytes_accessed=2 * weight.size, transcendentals=0
        ),
        name="add_product",
    )(a, weight, first, second, pick)


def back_kernel(parts, a, weight, u, first, *outs):
    result = mm_nt(a[...], flat(weight[...])) + mm_nt(u[...], first[...])
    size = result.shape[0] // parts
    for i in range(parts):
        outs[i][...] = result[i * size : (i + 1) * size].astype(BF16)


def back_product(a, group, weight, k_rows, u, first, parts):
    rows, depth = a.shape
    rows //= 2
    shards = weight.shape[0]
    width, low = first.shape
    per = max(1, 512 // k_rows)
    size = rows // parts
    return pl.pallas_call(
        functools.partial(back_kernel, parts),
        grid=(shards // per,),
        out_shape=[jax.ShapeDtypeStruct((size, width), BF16)] * parts,
        in_specs=[
            fixed(rows, depth, at=(group, 0)),
            pl.BlockSpec((per, k_rows, depth), lambda i: (i, 0, 0)),
            fixed(rows, low, at=(group, 0)),
            pl.BlockSpec((per * k_rows, low), lambda i: (i, 0)),
        ],
        out_specs=[pl.BlockSpec((size, per * k_rows), lambda i: (0, i))] * parts,
        compiler_params=BIG,
        cost_estimate=pl.CostEstimate(
            flops=2 * rows * width * depth, bytes_accessed=2 * width * depth, transcendentals=0
        ),
        name="back_product",
    )(a, weight, u, first)


def gate_up_kernel(h, first, pick, w_g, w_u, b_g, b_u, gate_out, up_out, act, latent_out, latent):
    low = pick.shape[1]

    @pl.when(pl.program_id(0) == 0)
    def _():
        both = mm(h[...], first[...])
        latent[:, :low] = (both[:, :low] * pick[...]).astype(BF16)
        latent[:, low:] = (both[:, low:] * pick[...]).astype(BF16)
        latent_out[...] = latent[...]

    gate = mm(h[...], w_g[...]) + mm(latent[:, :low], b_g[...])
    up = mm(h[...], w_u[...]) + mm(latent[:, low:], b_u[...])
    gate_out[...] = gate
    up_out[...] = up
    act[...] = (gate / (1.0 + jnp.exp(-gate)) * up).astype(BF16)


def gate_up_product(h, w_gu, a_gu, b_gu, pick, tile=512):
    rows, width = h.shape
    units, low = w_gu.shape[1] // 2, pick.shape[1]
    n = units // tile
    left = lambda depth: pl.BlockSpec((depth, tile), lambda i: (0, i))
    out = pl.BlockSpec((rows, tile), lambda i: (0, i))
    return pl.pallas_call(
        gate_up_kernel,
        grid=(n,),
        out_shape=[jax.ShapeDtypeStruct((rows, units), F32)] * 2
        + [
            jax.ShapeDtypeStruct((rows, units), BF16),
            jax.ShapeDtypeStruct((rows, 2 * low), BF16),
        ],
        in_specs=[
            fixed(rows, width),
            fixed(width, 2 * low),
            fixed(rows, low),
            left(width),
            pl.BlockSpec((width, tile), lambda i: (0, i + n)),
            left(low),
            pl.BlockSpec((low, tile), lambda i: (1, i)),
        ],
        out_specs=[out, out, out, fixed(rows, 2 * low)],
        scratch_shapes=[pltpu.VMEM((rows, 2 * low), BF16)],
        compiler_params=BIG,
        cost_estimate=pl.CostEstimate(
            flops=4 * rows * width * units, bytes_accessed=4 * width * units, transcendentals=0
        ),
        name="gate_up_product",
    )(h, a_gu, pick, w_gu, w_gu, b_gu, b_gu)


def ff_back_kernel(
    parts, steps, d_ff, b_down, pick, w_down, a_down, gate, up, w_g, w_u, b_g, b_u, a_gu, *refs
):
    outs, (d_gate_out, d_up_out, u_out, u_down_out, acc, u_g, u_u, u_down) = refs[:parts], refs[parts:]
    i = pl.program_id(0)

    @pl.when(i == 0)
    def _():
        u_down[...] = (mm_nt(d_ff[...], b_down[...]) * pick[...]).astype(BF16)
        u_down_out[...] = u_down[...]

    d_act = mm(d_ff[...], w_down[...]) + mm_nt(u_down[...], a_down[...])
    g = gate[...]
    sigmoid = 1.0 / (1.0 + jnp.exp(-g))
    silu = g * sigmoid
    d_gate = (d_act * up[...] * (sigmoid + silu * (1.0 - sigmoid))).astype(BF16)
    d_up = (d_act * silu).astype(BF16)
    d_gate_out[...] = d_gate
    d_up_out[...] = d_up
    part = mm_nt(d_gate, w_g[...]) + mm_nt(d_up, w_u[...])
    part_g, part_u = mm_nt(d_gate, b_g[...]), mm_nt(d_up, b_u[...])

    @pl.when(i == 0)
    def _():
        acc[...] = part
        u_g[...] = part_g
        u_u[...] = part_u

    @pl.when(i > 0)
    def _():
        acc[...] += part
        u_g[...] += part_g
        u_u[...] += part_u

    @pl.when(i == steps - 1)
    def _():
        low = pick.shape[1]
        last_g = (u_g[...] * pick[...]).astype(BF16)
        last_u = (u_u[...] * pick[...]).astype(BF16)
        u_out[:, :low] = last_g
        u_out[:, low:] = last_u
        size = acc.shape[0] // parts
        for p in range(parts):
            at = slice(p * size, (p + 1) * size)
            outs[p][...] = (
                acc[at, :]
                + mm_nt(last_g[at], a_gu[:, :low])
                + mm_nt(last_u[at], a_gu[:, low:])
            ).astype(BF16)


def ff_back(d_ff, b_down, pick, w_down, a_down, gate, up, w_gu, b_gu, a_gu, parts, tile=512):
    rows, width = d_ff.shape
    units, low = gate.shape[1], pick.shape[1]
    n = units // tile
    size = rows // parts
    column = lambda depth: pl.BlockSpec((depth, tile), lambda i: (0, i))
    return pl.pallas_call(
        functools.partial(ff_back_kernel, parts, n),
        grid=(n,),
        out_shape=[jax.ShapeDtypeStruct((size, width), BF16)] * parts
        + [jax.ShapeDtypeStruct((rows, units), BF16)] * 2
        + [
            jax.ShapeDtypeStruct((rows, 2 * low), BF16),
            jax.ShapeDtypeStruct((rows, low), BF16),
        ],
        in_specs=[
            fixed(rows, width),
            fixed(low, width),
            fixed(rows, low),
            column(width),
            pl.BlockSpec((tile, low), lambda i: (i, 0)),
            column(rows),
            column(rows),
            column(width),
            pl.BlockSpec((width, tile), lambda i: (0, i + n)),
            column(low),
            pl.BlockSpec((low, tile), lambda i: (1, i)),
            fixed(width, 2 * low),
        ],
        out_specs=[fixed(size, width)] * parts
        + [column(rows), column(rows), fixed(rows, 2 * low), fixed(rows, low)],
        scratch_shapes=[
            pltpu.VMEM((rows, width), F32),
            pltpu.VMEM((rows, low), F32),
            pltpu.VMEM((rows, low), F32),
            pltpu.VMEM((rows, low), BF16),
        ],
        compiler_params=BIG,
        cost_estimate=pl.CostEstimate(
            flops=6 * rows * width * units, bytes_accessed=6 * width * units, transcendentals=0
        ),
        name="ff_back",
    )(d_ff, b_down, pick, w_down, a_down, gate, up, w_gu, w_gu, b_gu, b_gu, a_gu)


def blocked(parts):
    zeros = lambda a, b: jnp.zeros((a.shape[0], b.shape[1]), a.dtype)
    return jnp.concatenate(
        [
            jnp.concatenate([a if a is b else zeros(a, b) for b in parts], axis=1)
            for a in parts
        ],
        axis=0,
    )


def local(
    layer_input,
    cotangent,
    query_key_value_weight,
    output_weight,
    gate_up_weight,
    down_weight,
    input_first_factor,
    output_first_factor,
    down_first_factor,
    query_key_value_second,
    gate_up_second_factor,
    output_down_second_factor,
    norm_gain_table,
    sequence_adapter,
    block_sequence,
    block_position,
):
    tp, tp_rank = lax.axis_size("tp"), lax.axis_index("tp")
    seqs, seq_rank = lax.axis_size("seq"), lax.axis_index("seq")
    own_rows, width = layer_input.shape
    rows = own_rows * tp
    part = own_rows // 2
    my_blocks = rows // BLK
    cols = query_key_value_weight.shape[2]
    heads = cols // HEAD_DIM
    hidden_cols = gate_up_weight.shape[2]
    k_rows = query_key_value_weight.shape[1]
    slots_a = input_first_factor.shape[2]
    rank_cols = output_first_factor.shape[1]
    group = seqs // heads
    head_rank, group_rank = seq_rank // group, seq_rank % group
    n_seq = sequence_adapter.shape[0]
    groups = (0, 1)

    runs = row_runs(tp)
    piece_at = jnp.stack([2 * (tp_rank ^ mask) + which for mask, which in runs]).astype(jnp.int32)
    token = (piece_at[:, None] * part + jnp.arange(part, dtype=jnp.int32)[None, :]).reshape(-1)
    token_block, offset = token // BLK, token % BLK
    block_ids = seq_rank * my_blocks + jnp.arange(my_blocks, dtype=jnp.int32)
    place_blocks = block_position[block_ids]
    adapter_blocks = sequence_adapter[block_sequence[block_ids]]
    in_block = token_block[:, None] == jnp.arange(my_blocks, dtype=jnp.int32)[None, :]
    pick = lambda per_block: jnp.sum(jnp.where(in_block, per_block[None, :], 0), axis=1)
    select = (
        jnp.arange(slots_a, dtype=jnp.int32)[None, :] // ADAPTER_RANK
        == pick(adapter_blocks)[:, None]
    ).astype(F32) * 2.0
    half = rows // 2
    selects = [select[:half], select[half:]]
    start = jnp.where(place_blocks < PROMPT_BLOCKS, place_blocks, PROMPT_BLOCKS) * BLK
    position = pick(start) + offset
    frequency = THETA ** (-(jnp.arange(HEAD_DIM // 2, dtype=F32) * 2.0) / HEAD_DIM)
    angles = position.astype(F32)[:, None] * frequency[None, :]
    cosine, sine = jnp.cos(angles), jnp.sin(angles)
    cs = jnp.concatenate([cosine, cosine, -sine, sine], axis=1)

    a_part = k_rows // tp
    b_part = width // tp
    a_mine = lax.dynamic_slice_in_dim(input_first_factor, tp_rank * a_part, a_part, 1)
    b_mine = lax.dynamic_slice_in_dim(output_down_second_factor, tp_rank * b_part, b_part, 2)
    first = jnp.concatenate(
        [
            query_key_value_weight.transpose(1, 0, 2).reshape(k_rows, 3 * cols),
            query_key_value_second.transpose(1, 0, 2).reshape(rank_cols, 3 * cols),
            a_mine[:3].reshape(-1, 3 * cols),
        ],
        axis=0,
    )
    x_parts = [layer_input] + [
        lax.ppermute(layer_input, "tp", [(i, i ^ mask) for i in range(tp)]) for mask in range(1, tp)
    ]
    x = jnp.concatenate(
        [x_parts[mask][which * part : (which + 1) * part] for mask, which in runs], axis=0
    )
    pick3 = jnp.tile(select, (1, 3))
    first = lax.all_gather(first, "seq", axis=0)
    pieces = [
        output_weight.T,
        output_first_factor.T,
        b_mine.reshape(-1, cols),
        a_mine[3:].reshape(-1, cols),
        down_first_factor.T.reshape(-1, cols),
        gate_up_second_factor.reshape(-1, cols),
    ]
    packed = jnp.concatenate(pieces, axis=0)
    first, x, cs, pick3, packed, w_gu, w_down = lax.optimization_barrier(
        (
            first,
            x,
            cs,
            pick3,
            packed,
            gate_up_weight.transpose(1, 0, 2).reshape(k_rows, 2 * hidden_cols),
            down_weight.T,
        )
    )
    packed = lax.all_gather(packed, "seq", axis=0)
    w_gu = lax.all_gather(w_gu, "seq", axis=0, tiled=True)
    w_down = lax.all_gather(w_down, "seq", axis=0, tiled=True)

    tp_order, seq_order = list(range(bits_of(tp))), list(range(bits_of(seqs)))
    a_qkv = first[:, k_rows + rank_cols :].reshape(seqs, 3, a_part, slots_a)
    a_qkv = a_qkv.transpose(0, 2, 1, 3).reshape(seqs, a_part, 3 * slots_a)
    a_parts = [a_qkv] + [
        lax.ppermute(a_qkv, "tp", [(i, i ^ mask) for i in range(tp)]) for mask in range(1, tp)
    ]
    a_qkv = jnp.zeros((seqs, tp, a_part, 3 * slots_a), BF16)
    for mask, value in enumerate(a_parts):
        a_qkv = lax.dynamic_update_slice(a_qkv, value[:, None], (0, tp_rank ^ mask, 0, 0))
    a_qkv = a_qkv.reshape(width, 3 * slots_a)
    b_qkv = first[:, k_rows : k_rows + rank_cols].reshape(slots_a, 3 * cols)
    b_qkv = blocked([b_qkv[:, i * cols : (i + 1) * cols] for i in range(3)])
    owner = (
        ((head_rank - jnp.arange(heads)) % heads)[None, :] * group
        + ((group_rank + jnp.arange(group)) % group)[:, None]
    ).reshape(-1)
    held = (owner[:, None] * my_blocks + jnp.arange(my_blocks)[None, :]).reshape(-1)
    held_seq = block_sequence[held].astype(jnp.int32)
    held_place = block_position[held].astype(jnp.int32)
    prompt_count = n_seq * PROMPT_BLOCKS
    wanted = jnp.arange(prompt_count, dtype=jnp.int32)
    code = jnp.where(held_place < PROMPT_BLOCKS, held_seq * PROMPT_BLOCKS + held_place, -1)
    prompt_at = jnp.sum(
        jnp.where(
            code[None, :] == wanted[:, None], jnp.arange(held.shape[0], dtype=jnp.int32)[None, :], 0
        ),
        axis=1,
    ).astype(jnp.int32)
    own_blocks = heads * my_blocks
    tables = (held_seq[:own_blocks], held_place[:own_blocks], prompt_at)
    head_order = ((head_rank + jnp.arange(heads)) % heads).astype(jnp.int32)

    def head_shift(value, by):
        if by == 0:
            return value
        return lax.ppermute(
            value,
            "seq",
            [
                (h * group + j, ((h + by) % heads) * group + j)
                for h in range(heads)
                for j in range(group)
            ],
        )

    def group_shift(value, by):
        return lax.ppermute(
            value,
            "seq",
            [
                (h * group + j, h * group + (j + by) % group)
                for h in range(heads)
                for j in range(group)
            ],
        )

    own = lambda value, i: value[i * part : (i + 1) * part].astype(F32)
    gain = lax.dynamic_slice_in_dim(norm_gain_table[:2], tp_rank * cols, cols, 1)
    latents = (mm(x, a_qkv) * pick3).astype(BF16)
    z, squares = qkv_product(
        x, latents, first, first[:, k_rows : k_rows + rank_cols].reshape(slots_a, 3 * cols), k_rows, cols
    )
    squares = sum_rows(squares[:2].reshape(2, rows), tp)
    inv = lax.rsqrt(squares / width + EPS)
    inv, packed = lax.optimization_barrier((inv, packed))
    split, at = [], 0
    for piece in pieces:
        split.append(packed[:, at : at + piece.shape[0]])
        at += piece.shape[0]
    w_o = split[0].reshape(width, cols)
    a_o = split[1].reshape(slots_a, cols).T
    shared = gather_order(jnp.concatenate(split[2:4], axis=1), "tp", tp, tp_order)
    b_size = split[2].shape[1]
    b_od = (
        shared[:, :, :b_size]
        .reshape(tp, seqs, 2, rank_cols, b_part)
        .transpose(2, 1, 3, 0, 4)
        .reshape(2, slots_a, width)
    )
    a_gu = (
        shared[:, :, b_size:]
        .reshape(tp, seqs, 2, a_part, slots_a)
        .transpose(1, 0, 3, 2, 4)
        .reshape(width, 2 * slots_a)
    )
    a_down = split[4].reshape(slots_a, hidden_cols).T
    b_gu = (
        split[5]
        .reshape(seqs, 2, rank_cols, hidden_cols)
        .transpose(1, 0, 2, 3)
        .reshape(2 * slots_a, hidden_cols)
    )
    spread = spread_heads(head_order, piece_at, z, inv.T, cs, gain, heads)
    near = [head_shift(spread[k], k) for k in range(heads)]
    far = [group_shift(near[k][1:], -j) for j in range(1, group) for k in range(heads)]
    far, w_o, a_o, b_od, a_gu, a_down, b_gu = lax.optimization_barrier(
        (far, w_o, a_o, b_od, a_gu, a_down, b_gu)
    )
    attended = attend(tables, near, far, prompt_count)
    heads_out = collect_heads(
        head_order, piece_at, [head_shift(attended[k], -k) for k in range(heads)]
    )

    def norm_back(values_in, inv, scaled):
        return inv * scaled - values_in * inv**3 * jnp.mean(scaled * values_in, axis=1, keepdims=True)

    def inverse_norm(values_in):
        return lax.rsqrt(jnp.mean(values_in * values_in, axis=1, keepdims=True) + EPS)

    *far_part, o_latent1 = add_product(heads_out[1], w_o, a_o, b_od[0], selects[1], 2)
    near_part, o_latent0 = add_product(heads_out[0], w_o, a_o, b_od[0], selects[0], 1)
    attn_out = scatter_groups(near_part, far_part, tp)
    scale_o = [inverse_norm(value) for value in attn_out]
    hidden = [
        own(layer_input, i) + attn_out[i] * scale_o[i] * norm_gain_table[2] for i in groups
    ]
    h_low = gather_groups([value.astype(BF16) for value in hidden], tp)

    gates, ups, acts, gu_latents = zip(
        *[gate_up_product(h_low[g], w_gu, a_gu, b_gu, selects[g]) for g in groups]
    )
    acts, w_down = lax.optimization_barrier((acts, w_down))
    *far_part, d_latent1 = add_product(acts[1], w_down, a_down, b_od[1], selects[1], 2)
    near_part, d_latent0 = add_product(acts[0], w_down, a_down, b_od[1], selects[0], 1)
    ff_out = scatter_groups(near_part, far_part, tp)
    scale_f = [inverse_norm(value) for value in ff_out]
    output = jnp.concatenate(
        [hidden[i] + ff_out[i] * scale_f[i] * norm_gain_table[3] for i in groups], axis=0
    )

    d_ffs = gather_groups(
        [
            norm_back(ff_out[i], scale_f[i], own(cotangent, i) * norm_gain_table[3]).astype(BF16)
            for i in groups
        ],
        tp,
    )
    backs = [
        ff_back(
            d_ffs[g], b_od[1], selects[g], w_down, a_down, gates[g], ups[g], w_gu, b_gu, a_gu, 1 + g
        )
        for g in groups
    ]
    summed = scatter_groups(backs[0][0], backs[1][:2], tp)
    d_gates, d_ups, u_gus, u_downs = zip(*[back[-4:] for back in backs])
    d_hidden = [own(cotangent, i) + summed[i] for i in groups]
    d_attn = [
        norm_back(attn_out[i], scale_o[i], d_hidden[i] * norm_gain_table[2]).astype(BF16)
        for i in groups
    ]
    d_latents = (d_latent0, d_latent1)
    d_rows = gather_groups(d_attn, tp)
    o_latents = (o_latent0, o_latent1)
    u_os, grads = [], []
    for g in groups:
        u_os.append((mm_nt(d_rows[g], b_od[0]) * selects[g]).astype(BF16))
        d_heads = (mm(d_rows[g], w_o) + mm_nt(u_os[g], a_o)).astype(BF16)
        grads.append(
            [
                head_shift(
                    lax.dynamic_slice_in_dim(d_heads, head_order[k] * HEAD_DIM, HEAD_DIM, 1), k
                )
                for k in range(heads)
            ]
        )
    grads = [grads[g][k] for k in range(heads) for g in groups]
    results = list(attend_back(tables, piece_at, near, far, grads, prompt_count))
    dqs = [head_shift(results[k], -k) for k in range(heads)]
    d_kv = results[heads].reshape(2, heads, rows, HEAD_DIM)
    others = [
        group_shift(results[heads + j], j).reshape(2, heads, rows, HEAD_DIM) for j in range(1, group)
    ]
    dkvs = []
    for k in range(heads):
        total = d_kv[:, k].astype(F32)
        for other in others:
            total = total + other[:, k].astype(F32)
        dkvs.append(head_shift(total.astype(BF16), -k))
    dkvs[1], u_os, o_latents, u_downs, d_latents, u_gus, gu_latents = lax.optimization_barrier(
        (dkvs[1], u_os, o_latents, u_downs, d_latents, u_gus, gu_latents)
    )
    both_groups = lambda f: f(0) + f(1)
    grad_a_down = both_groups(lambda g: mm_tn(u_downs[g], acts[g]))
    grad_b_down = both_groups(lambda g: mm_tn(d_latents[g], d_ffs[g]))
    grad_a_gu = both_groups(lambda g: mm_tn(h_low[g], u_gus[g]))
    grad_b_gate = both_groups(lambda g: mm_tn(gu_latents[g][:, :slots_a], d_gates[g]))
    grad_b_up = both_groups(lambda g: mm_tn(gu_latents[g][:, slots_a:], d_ups[g]))
    lane = 2 * slots_a
    shards = lambda value: value.astype(BF16).reshape(seqs, -1, lane)
    early = jnp.concatenate(
        [
            shards(grad_a_gu),
            shards(grad_b_down),
            shards(grad_a_down),
            shards(grad_b_gate),
            shards(grad_b_up),
        ],
        axis=1,
    )
    grad_a_o = both_groups(lambda g: mm_tn(u_os[g], heads_out[g]))
    grad_b_o = both_groups(lambda g: mm_tn(o_latents[g], d_rows[g]))
    late_o = jnp.concatenate(
        [
            grad_b_o.astype(BF16).reshape(seqs, -1, cols),
            grad_a_o.astype(BF16).reshape(seqs, -1, cols),
        ],
        axis=1,
    )
    dqs, dkvs, early, late_o = lax.optimization_barrier((dqs, dkvs, early, late_o))
    early = lax.psum_scatter(early, "seq", scatter_dimension=0, tiled=False)
    dqs, dkvs, late_o = lax.optimization_barrier((dqs, dkvs, late_o))
    late_o = scatter_order(late_o, "seq", seqs, seq_order)
    scaled, parts = unturn_heads(head_order, piece_at, dqs, dkvs, z, cs, gain)
    parts = sum_rows(parts.T, tp) / width
    coef = jnp.concatenate([inv, inv**3 * parts], axis=0)
    dz = norm_back_heads(head_order, piece_at, dkvs, scaled, z, coef.T)
    us = (mm_nt(dz, b_qkv) * pick3).astype(BF16)
    grad_a_qkv = mm_tn(x, us)
    grad_b_qkv = mm_tn(latents, dz)
    lane3 = 3 * slots_a
    grad_b_qkv = jnp.concatenate(
        [
            grad_b_qkv[i * slots_a : (i + 1) * slots_a, i * cols : (i + 1) * cols]
            for i in range(3)
        ],
        axis=1,
    )
    late = jnp.concatenate(
        [
            grad_a_qkv.astype(BF16).reshape(seqs, k_rows, lane3),
            grad_b_qkv.astype(BF16).reshape(seqs, -1, lane3),
        ],
        axis=1,
    )
    dz, late = lax.optimization_barrier((dz, late))
    far_part = list(back_product(dz, 1, first, k_rows, us, a_qkv, 2))
    far_part[0], dz = lax.optimization_barrier((far_part[0], dz))
    (near_part,) = back_product(dz, 0, first, k_rows, us, a_qkv, 1)
    near_part, early, late_o = lax.optimization_barrier((near_part, early, late_o))

    down_size = rank_cols * width // lane
    o_size = rank_cols * width // cols
    both = jnp.concatenate(
        [early[: k_rows + down_size], late_o[:o_size].astype(BF16).reshape(-1, lane)], axis=0
    )
    both = sum_all(both, "tp", tp).astype(F32)
    late = lax.psum_scatter(late, "seq", scatter_dimension=0, tiled=False)
    summed = scatter_groups(near_part, far_part, tp)
    summed, late = lax.optimization_barrier((summed, late))
    late = late.astype(F32)
    input_grad = jnp.concatenate([d_hidden[i] + summed[i] for i in groups], axis=0)
    grad_a_qkv = sum_all(late[:k_rows].astype(BF16), "tp", tp).astype(F32)
    grad_a_gu = both[:k_rows]
    grad_b_down = both[k_rows : k_rows + down_size].reshape(rank_cols, width)
    grad_b_o = both[k_rows + down_size :].reshape(rank_cols, width)
    a_size = rank_cols * hidden_cols // lane
    rest = early[k_rows + down_size :].astype(F32)
    grad_a_down = rest[:a_size].reshape(rank_cols, hidden_cols).T
    grad_b_gu = rest[a_size:].reshape(2, rank_cols, hidden_cols)
    grad_a_o = late_o[o_size:].T
    grad_b_qkv = late[k_rows:].reshape(rank_cols, 3, cols).transpose(1, 0, 2)
    grad_a_in = jnp.stack(
        [grad_a_qkv[:, i * slots_a : (i + 1) * slots_a] for i in range(3)]
        + [grad_a_gu[:, i * slots_a : (i + 1) * slots_a] for i in range(2)]
    )
    grad_b_out = jnp.stack([grad_b_o, grad_b_down])
    return (output, input_grad, grad_a_in, grad_a_o, grad_a_down, grad_b_qkv, grad_b_gu, grad_b_out)


def solution(mesh):
    return jax.shard_map(
        local,
        mesh=mesh,
        in_specs=(
            P(("seq", "tp"), None),
            P(("seq", "tp"), None),
            P(None, "seq", "tp"),
            P("tp", "seq"),
            P(None, "seq", "tp"),
            P("tp", "seq"),
            P(None, "seq", None),
            P("tp", "seq"),
            P("tp", "seq"),
            P(None, "seq", "tp"),
            P(None, "seq", "tp"),
            P(None, "seq", None),
            P(),
            P(),
            P(),
            P(),
        ),
        out_specs=(
            P(("seq", "tp"), None),
            P(("seq", "tp"), None),
            P(None, "seq", None),
            P("tp", "seq"),
            P("tp", "seq"),
            P(None, "seq", "tp"),
            P(None, "seq", "tp"),
            P(None, "seq", None),
        ),
        check_vma=False,
    )
```

```python
import functools

import jax
import jax.numpy as jnp
from jax import lax
from jax.experimental import pallas as pl
from jax.experimental.pallas import tpu as pltpu
from jax.sharding import PartitionSpec as P

HEAD_DIM = 128
ADAPTER_RANK = 16
BLK = 128
PROMPT_BLOCKS = 8
EPS = 1e-06
THETA = 500000.0
NEG = -1e30
LOG2E = 1.4426950408889634
F32 = jnp.float32
BF16 = jnp.bfloat16


def mm(a, b):
    return jnp.dot(a, b, preferred_element_type=F32)


def mm_nt(a, b):
    return lax.dot_general(a, b, (((1,), (1,)), ((), ())), preferred_element_type=F32)


def mm_tn(a, b):
    return lax.dot_general(a, b, (((0,), (0,)), ((), ())), preferred_element_type=F32)


def bits_of(count):
    n = count.bit_length() - 1
    assert 1 << n == count
    return n


def flip(value, axis, count, bit):
    return lax.ppermute(value, axis, [(i, i ^ (1 << bit)) for i in range(count)])


def gather_order(value, axis, count, order):
    rank = lax.axis_index(axis)
    have = []
    current = value
    for bit in order:
        other = flip(current, axis, count, bit)
        mine_low = ((rank >> bit) & 1) == 0
        at = len([b for b in have if b > bit])
        low = jnp.where(mine_low, current, other)
        high = jnp.where(mine_low, other, current)
        current = jnp.stack([low, high], axis=at)
        have = sorted(have + [bit], reverse=True)
    return current.reshape((count,) + value.shape)


def scatter_order(value, axis, count, order):
    n = bits_of(count)
    rank = lax.axis_index(axis)
    current = value.reshape((2,) * n + value.shape[1:])
    have = list(range(n - 1, -1, -1))
    for bit in order:
        at = have.index(bit)
        mine = (rank >> bit) & 1
        keep = lax.dynamic_index_in_dim(current, mine, at, keepdims=False)
        give = lax.dynamic_index_in_dim(current, 1 - mine, at, keepdims=False)
        got = flip(give.astype(BF16), axis, count, bit)
        current = keep.astype(F32) + got.astype(F32)
        have.remove(bit)
    return current


def part_orders(count):
    order = list(range(bits_of(count)))
    return (order, order[::-1])


def group_masks(count):
    groups = ([], [])
    for part, order in enumerate(part_orders(count)):
        for j in range(count):
            mask = sum(1 << bit for i, bit in enumerate(order) if (j >> i) & 1)
            groups[j >= count // 2].append((mask, part))
    return groups


def row_runs(count):
    return [run for masks in group_masks(count) for run in masks]


def gather_groups(parts, count, beside=None):
    near, far = [], []
    for value, order in zip(parts, part_orders(count)):
        for bit in order[:-1]:
            value = jnp.concatenate([value, flip(value, "tp", count, bit)], axis=0)
        near.append(value)
    if beside is not None:
        near[1], beside = lax.optimization_barrier((near[1], beside))
    for value, order in zip(near, part_orders(count)):
        far.append(flip(value, "tp", count, order[-1]))
    if beside is not None:
        return jnp.concatenate(near, axis=0), jnp.concatenate(far, axis=0), beside
    return jnp.concatenate(near, axis=0), jnp.concatenate(far, axis=0)


def scatter_groups(near, far, count):
    return scatter_rest(scatter_first(near, far, count), count)


def scatter_first(near, far, count):
    out = []
    size = near.shape[0] // 2
    for i, order in enumerate(part_orders(count)):
        got = flip(far[i], "tp", count, order[-1])
        out.append(near[i * size : (i + 1) * size].astype(F32) + got.astype(F32))
    return out


def scatter_rest(totals, count):
    out = []
    for total, order in zip(totals, part_orders(count)):
        for bit in order[-2::-1]:
            half = total.shape[0] // 2
            got = flip(total[half:].astype(BF16), "tp", count, bit)
            total = total[:half] + got.astype(F32)
        out.append(total)
    return out


def sum_rows(value, count):
    runs = row_runs(count)
    value = value.reshape(value.shape[0], len(runs), -1)
    total = value
    for mask in range(1, count):
        got = lax.ppermute(value, "tp", [(i, i ^ mask) for i in range(count)])
        order = [runs.index((other ^ mask, which)) for other, which in runs]
        total = total + jnp.concatenate([got[:, j : j + 1] for j in order], axis=1)
    return total.reshape(value.shape[0], -1)


def sum_all(value, axis, count):
    for bit in range(bits_of(count)):
        value = value + flip(value, axis, count, bit)
    return value


def copy_all(pairs, sem):
    copies = [pltpu.make_async_copy(src, dst, sem.at[i]) for i, (src, dst) in enumerate(pairs)]
    for copy in copies:
        copy.start()
    for copy in copies:
        copy.wait()


def gather_prompt(prompt_at, source, target, count):
    def step(i, carry):
        start = pl.multiple_of(prompt_at[i] * BLK, BLK)
        target[pl.ds(pl.multiple_of(i * BLK, BLK), BLK), :] = source[pl.ds(start, BLK), :]
        return carry

    lax.fori_loop(0, count, step, 0)


def masked_scores(keys, own_keys, queries, place, scale):
    prompt = mm_nt(keys, queries) * scale
    block = lax.broadcasted_iota(jnp.int32, prompt.shape, 0) // BLK
    prompt = jnp.where(block < place, prompt, NEG)
    own = mm_nt(own_keys, queries) * scale
    causal = lax.broadcasted_iota(jnp.int32, own.shape, 0) <= lax.broadcasted_iota(
        jnp.int32, own.shape, 1
    )
    own = jnp.where(causal, own, NEG)
    top = jnp.maximum(jnp.max(prompt, axis=0, keepdims=True), jnp.max(own, axis=0, keepdims=True))
    prompt = jnp.exp2(prompt - top)
    own = jnp.exp2(own - top)
    total = jnp.sum(prompt, axis=0, keepdims=True) + jnp.sum(own, axis=0, keepdims=True)
    return prompt, own, 1.0 / total


def load_plan(slots, group, rows, refs, q_buf, k_buf, v_buf):
    plan = []
    for i in range(slots):
        plan.append((refs[i].at[0], q_buf.at[pl.ds(i * rows, rows)]))
    for i in range(slots * group):
        at = pl.ds(i * rows, rows)
        skip = int(i < slots)
        plan += [(refs[i].at[skip], k_buf.at[at]), (refs[i].at[skip + 1], v_buf.at[at])]
    return plan


def attend_kernel(slots, group, rows, prompt_count, q_seq, q_place, prompt_at, *refs):
    n_in = slots * group
    outs = refs[n_in : n_in + slots]
    q_buf, k_buf, v_buf, kp, vp, o_buf, sem = refs[n_in + slots :]
    copy_all(load_plan(slots, group, rows, refs, q_buf, k_buf, v_buf), sem)
    gather_prompt(prompt_at, k_buf, kp, prompt_count)
    gather_prompt(prompt_at, v_buf, vp, prompt_count)
    scale = HEAD_DIM ** (-0.5) * LOG2E
    span = PROMPT_BLOCKS * BLK

    def block(i):
        at = pl.ds(pl.multiple_of(i * BLK, BLK), BLK)
        of_seq = pl.ds(pl.multiple_of(q_seq[i] * span, span), span)
        prompt, own, inverse = masked_scores(
            kp[of_seq, :], k_buf[at, :], q_buf[at, :], q_place[i], scale
        )
        result = mm_tn(vp[of_seq, :], prompt.astype(BF16)) + mm_tn(v_buf[at, :], own.astype(BF16))
        return at, (result * inverse).T.astype(BF16)

    blocks = slots * rows // BLK
    pair = 2 if blocks % 2 == 0 else 1

    def step(i, carry):
        for at, result in [block(i * pair + j) for j in range(pair)]:
            o_buf[at, :] = result
        return carry

    lax.fori_loop(0, blocks // pair, step, 0)
    copy_all([(o_buf.at[pl.ds(i * rows, rows)], outs[i]) for i in range(slots)], sem)


def attend_back_kernel(
    slots, group, rows, pieces, prompt_count, q_seq, q_place, prompt_at, piece_at, *refs
):
    n_in = slots * group
    n_grad = slots * 2
    grads = refs[n_in : n_in + n_grad]
    outs = refs[n_in + n_grad : n_in + n_grad + slots]
    near_out = refs[n_in + n_grad + slots]
    rest = refs[n_in + n_grad + slots + 1 :]
    far_outs, rest = rest[: group - 1], rest[group - 1 :]
    q_buf, k_buf, v_buf, do_buf, kp, vp, dkp, dvp, dq_buf, dkv_buf, sem = rest
    plan = load_plan(slots, group, rows, refs, q_buf, k_buf, v_buf)
    size = rows // pieces
    for i in range(slots):
        for p in range(pieces):
            half, at = divmod(p, pieces // 2)
            to = pl.multiple_of(i * rows + piece_at[p] * size, 16)
            plan.append(
                (grads[i * 2 + half].at[pl.ds(at * size, size)], do_buf.at[pl.ds(to, size)])
            )
    copy_all(plan, sem)
    gather_prompt(prompt_at, k_buf, kp, prompt_count)
    gather_prompt(prompt_at, v_buf, vp, prompt_count)
    dkp[...] = jnp.zeros_like(dkp)
    dvp[...] = jnp.zeros_like(dvp)
    scale = HEAD_DIM ** (-0.5)
    span = PROMPT_BLOCKS * BLK
    own_rows = slots * rows
    zeros = jnp.zeros((BLK, HEAD_DIM), BF16)

    def rows_of(i):
        return pl.ds(pl.multiple_of(i * BLK, BLK), BLK)

    def clear(i, carry):
        for j in range(1, group):
            dkv_buf[j, 0, rows_of(i), :] = zeros
            dkv_buf[j, 1, rows_of(i), :] = zeros
        return carry

    lax.fori_loop(0, own_rows // BLK, clear, 0)

    def block(i):
        at = rows_of(i)
        seq, place = q_seq[i], q_place[i]
        of_seq = pl.ds(pl.multiple_of(seq * span, span), span)
        queries, grad = q_buf[at, :], do_buf[at, :]
        prompt, own, inverse = masked_scores(
            kp[of_seq, :], k_buf[at, :], queries, place, scale * LOG2E
        )
        prompt, own = prompt * inverse, own * inverse
        d_prompt = mm_nt(vp[of_seq, :], grad)
        d_own = mm_nt(v_buf[at, :], grad)
        delta = jnp.sum(prompt * d_prompt, axis=0, keepdims=True) + jnp.sum(
            own * d_own, axis=0, keepdims=True
        )
        ds_prompt = (prompt * (d_prompt - delta)).astype(BF16)
        ds_own = (own * (d_own - delta)).astype(BF16)
        dq = mm_tn(ds_prompt, kp[of_seq, :]) + mm_tn(ds_own, k_buf[at, :])
        return (
            at,
            of_seq,
            (dq * scale).astype(BF16),
            mm(prompt.astype(BF16), grad),
            mm(ds_prompt, queries) * scale,
            (mm(ds_own, queries) * scale).astype(BF16),
            mm(own.astype(BF16), grad).astype(BF16),
        )

    blocks = own_rows // BLK
    pair = 2 if blocks % 2 == 0 else 1

    def step(i, carry):
        for at, of_seq, dq, dv_prompt, dk_prompt, dk_own, dv_own in [
            block(i * pair + j) for j in range(pair)
        ]:
            dq_buf[at, :] = dq
            dvp[of_seq, :] += dv_prompt
            dkp[of_seq, :] += dk_prompt
            dkv_buf[0, 0, at, :] = dk_own
            dkv_buf[0, 1, at, :] = dv_own
        return carry

    lax.fori_loop(0, blocks // pair, step, 0)

    def spread(i, carry):
        place = prompt_at[i]
        j, to = place // blocks, rows_of(place % blocks)
        dkv_buf[j, 0, to, :] = (dkv_buf[j, 0, to, :].astype(F32) + dkp[rows_of(i), :]).astype(BF16)
        dkv_buf[j, 1, to, :] = (dkv_buf[j, 1, to, :].astype(F32) + dvp[rows_of(i), :]).astype(BF16)
        return carry

    lax.fori_loop(0, prompt_count, spread, 0)
    plan = [(dq_buf.at[pl.ds(i * rows, rows)], outs[i]) for i in range(slots)]
    plan.append((dkv_buf.at[0], near_out))
    plan += [(dkv_buf.at[j], far_outs[j - 1]) for j in range(1, group)]
    copy_all(plan, sem)


ANY = pl.BlockSpec(memory_space=pl.ANY)


def attend(tables, near, far, prompt_count):
    slots = len(near)
    rows = near[0].shape[1]
    group = 1 + len(far) // slots
    own, every = slots * rows, slots * group * rows
    pairs = own * (PROMPT_BLOCKS + 1) * BLK
    wide = lambda count, kind=BF16: pltpu.VMEM((count, HEAD_DIM), kind)
    return pl.pallas_call(
        functools.partial(attend_kernel, slots, group, rows, prompt_count),
        out_shape=[jax.ShapeDtypeStruct((rows, HEAD_DIM), BF16)] * slots,
        grid_spec=pltpu.PrefetchScalarGridSpec(
            num_scalar_prefetch=3,
            in_specs=[ANY] * (slots * group),
            out_specs=[ANY] * slots,
            scratch_shapes=[
                wide(own),
                wide(every),
                wide(every),
                wide(prompt_count * BLK),
                wide(prompt_count * BLK),
                wide(own),
                pltpu.SemaphoreType.DMA((slots + 2 * slots * group,)),
            ],
        ),
        cost_estimate=pl.CostEstimate(
            flops=4 * pairs * HEAD_DIM, bytes_accessed=6 * every * HEAD_DIM, transcendentals=pairs
        ),
        name="attend",
    )(*tables, *near, *far)


def attend_back(tables, piece_at, near, far, grads, prompt_count):
    pieces = piece_at.shape[0]
    slots = len(near)
    rows = near[0].shape[1]
    group = 1 + len(far) // slots
    own, every = slots * rows, slots * group * rows
    pairs = own * (PROMPT_BLOCKS + 1) * BLK
    wide = lambda count, kind=BF16: pltpu.VMEM((count, HEAD_DIM), kind)
    return pl.pallas_call(
        functools.partial(attend_back_kernel, slots, group, rows, pieces, prompt_count),
        out_shape=[jax.ShapeDtypeStruct((rows, HEAD_DIM), BF16)] * slots
        + [jax.ShapeDtypeStruct((2, own, HEAD_DIM), BF16)] * group,
        grid_spec=pltpu.PrefetchScalarGridSpec(
            num_scalar_prefetch=4,
            in_specs=[ANY] * (slots * group + 2 * slots),
            out_specs=[ANY] * (slots + group),
            scratch_shapes=[
                wide(own),
                wide(every),
                wide(every),
                wide(own),
                wide(prompt_count * BLK),
                wide(prompt_count * BLK),
                wide(prompt_count * BLK, F32),
                wide(prompt_count * BLK, F32),
                wide(own),
                pltpu.VMEM((group, 2, own, HEAD_DIM), BF16),
                pltpu.SemaphoreType.DMA((slots + 2 * slots * group + slots * pieces,)),
            ],
        ),
        cost_estimate=pl.CostEstimate(
            flops=10 * pairs * HEAD_DIM, bytes_accessed=12 * every * HEAD_DIM, transcendentals=pairs
        ),
        name="attend_back",
    )(*tables, piece_at, *near, *far, *grads)


def turn(values, cosine, sine):
    return values * cosine + pltpu.roll(values, HEAD_DIM // 2, 1) * sine


def lanes(head, base=0):
    return pl.ds(pl.multiple_of(base + head * HEAD_DIM, HEAD_DIM), HEAD_DIM)


def here(size, width):
    return pl.BlockSpec((size, width), lambda p, order, piece_at: (p, 0))


def there(size, at=None, count=1):
    if at is None:
        return pl.BlockSpec((size, HEAD_DIM), lambda p, order, piece_at: (piece_at[p], 0))
    return pl.BlockSpec((count, size, HEAD_DIM), lambda p, order, piece_at: (at, piece_at[p], 0))


def all_of(value):
    return pl.BlockSpec(value.shape, lambda p, order, piece_at: (0, 0))


def piece_rows(index, size):
    return pl.ds(pl.multiple_of(index * size, 16), size)


def spread_kernel(slots, order, piece_at, z, inv, cs, gain, *outs):
    cols = slots * HEAD_DIM
    cosine, sine = cs[:, :HEAD_DIM], cs[:, HEAD_DIM:]
    for which in range(2):
        factor = inv[:, which : which + 1]
        for k in range(slots):
            head = order[k]
            scaled = z[:, lanes(head, which * cols)] * factor
            scaled = scaled * gain[which : which + 1, lanes(head)]
            outs[k][which, :, :] = turn(scaled, cosine, sine).astype(BF16)
    for k in range(slots):
        outs[k][2, :, :] = z[:, lanes(order[k], 2 * cols)].astype(BF16)


WHOLE = pl.BlockSpec(memory_space=pltpu.VMEM)
BIG = pltpu.CompilerParams(vmem_limit_bytes=56 * 1024 * 1024)


def spread_heads(order, piece_at, z, inv, cs, gain, slots):
    rows = z.shape[0]
    pieces = piece_at.shape[0]
    size = rows // pieces
    return pl.pallas_call(
        functools.partial(spread_kernel, slots),
        out_shape=[jax.ShapeDtypeStruct((3, rows, HEAD_DIM), BF16)] * slots,
        grid_spec=pltpu.PrefetchScalarGridSpec(
            num_scalar_prefetch=2,
            grid=(pieces,),
            in_specs=[
                here(size, z.shape[1]),
                here(size, inv.shape[1]),
                here(size, cs.shape[1]),
                all_of(gain),
            ],
            out_specs=[there(size, 0, 3)] * slots,
        ),
        compiler_params=BIG,
        name="spread_heads",
    )(order, piece_at, z, inv, cs, gain)


def collect_kernel(slots, pieces, order, piece_at, *refs):
    outs = refs[slots:]
    size = refs[0].shape[0] // pieces
    for p in range(pieces):
        half, at = divmod(p, pieces // 2)
        for k in range(slots):
            outs[half][pl.ds(at * size, size), lanes(order[k])] = refs[k][
                piece_rows(piece_at[p], size), :
            ]


def collect_heads(order, piece_at, parts):
    slots = len(parts)
    rows = parts[0].shape[0]
    return pl.pallas_call(
        functools.partial(collect_kernel, slots, piece_at.shape[0]),
        out_shape=[jax.ShapeDtypeStruct((rows // 2, slots * HEAD_DIM), BF16)] * 2,
        grid_spec=pltpu.PrefetchScalarGridSpec(
            num_scalar_prefetch=2, in_specs=[WHOLE] * slots, out_specs=[WHOLE] * 2
        ),
        name="collect_heads",
    )(order, piece_at, *parts)


def unturn_kernel(slots, order, piece_at, *refs):
    dqs, dkvs, rest = refs[:slots], refs[slots : 2 * slots], refs[2 * slots :]
    z, cs, gain, scaled_out, part_out = rest
    cols = slots * HEAD_DIM
    cosine, sine = cs[:, :HEAD_DIM], cs[:, HEAD_DIM:]
    for which in range(2):
        total = jnp.zeros((z.shape[0], HEAD_DIM), F32)
        for k in range(slots):
            head = order[k]
            grad = dqs[k][...] if which == 0 else dkvs[k][0, :, :]
            grad = turn(grad.astype(F32), cosine, -sine) * gain[which : which + 1, lanes(head)]
            scaled_out[:, lanes(head, which * cols)] = grad
            total = total + grad * z[:, lanes(head, which * cols)]
        part_out[:, which : which + 1] = jnp.sum(total, axis=1, keepdims=True)


def unturn_heads(order, piece_at, dqs, dkvs, z, cs, gain):
    slots = len(dqs)
    rows = z.shape[0]
    cols = slots * HEAD_DIM
    pieces = piece_at.shape[0]
    size = rows // pieces
    return pl.pallas_call(
        functools.partial(unturn_kernel, slots),
        out_shape=[
            jax.ShapeDtypeStruct((rows, 2 * cols), F32),
            jax.ShapeDtypeStruct((rows, 2), F32),
        ],
        grid_spec=pltpu.PrefetchScalarGridSpec(
            num_scalar_prefetch=2,
            grid=(pieces,),
            in_specs=[there(size)] * slots
            + [there(size, 0)] * slots
            + [here(size, 2 * cols), here(size, cs.shape[1]), all_of(gain)],
            out_specs=[here(size, 2 * cols), here(size, 2)],
        ),
        compiler_params=BIG,
        name="unturn_heads",
    )(order, piece_at, *dqs, *dkvs, z, cs, gain)


def norm_back_kernel(slots, order, piece_at, *refs):
    dkvs, (scaled, z, coef, second, pick, out, latent_out) = refs[:slots], refs[slots:]
    cols = slots * HEAD_DIM
    low = second.shape[0]
    for which in range(2):
        to = slice(which * cols, (which + 1) * cols)
        out[:, to] = (
            scaled[:, to] * coef[:, which : which + 1] - z[:, to] * coef[:, 2 + which : 3 + which]
        ).astype(BF16)
    for k in range(slots):
        out[:, lanes(order[k], 2 * cols)] = dkvs[k][0, :, :]
    for which in range(3):
        to = slice(which * cols, (which + 1) * cols)
        at = slice(which * low, (which + 1) * low)
        latent_out[:, at] = (mm_nt(out[:, to], second[:, to]) * pick[...]).astype(BF16)


def norm_back_heads(order, piece_at, dkvs, scaled, z, coef, second, pick):
    slots = len(dkvs)
    rows = z.shape[0]
    cols = slots * HEAD_DIM
    low = second.shape[0]
    pieces = piece_at.shape[0]
    size = rows // pieces
    return pl.pallas_call(
        functools.partial(norm_back_kernel, slots),
        out_shape=[
            jax.ShapeDtypeStruct((rows, 3 * cols), BF16),
            jax.ShapeDtypeStruct((rows, 3 * low), BF16),
        ],
        grid_spec=pltpu.PrefetchScalarGridSpec(
            num_scalar_prefetch=2,
            grid=(pieces,),
            in_specs=[there(size, 1)] * slots
            + [
                here(size, 2 * cols),
                here(size, 2 * cols),
                here(size, 4),
                all_of(second),
                here(size, low),
            ],
            out_specs=[here(size, 3 * cols), here(size, 3 * low)],
        ),
        compiler_params=BIG,
        name="norm_back_heads",
    )(order, piece_at, *dkvs, scaled, z, coef, second, pick)


def fixed(*shape, at=None):
    place = at or (0,) * len(shape)
    return pl.BlockSpec(shape, lambda i: place)


def flat(value):
    return value.reshape(-1, value.shape[-1])


def qkv_kernel(x, latent, weight, second, z, squares):
    i = pl.program_id(0)
    result = mm(x[...], flat(weight[...])) + mm(latent[...], flat(second[...]))
    z[...] = result
    squares[0, :, :] = jnp.sum(result * result, axis=1, keepdims=True)


def qkv_product(x, latents, first, second, k_rows, cols):
    rows, width = x.shape
    shards, _, total = first.shape
    low = latents.shape[1] // 3
    return pl.pallas_call(
        qkv_kernel,
        grid=(3,),
        out_shape=[
            jax.ShapeDtypeStruct((rows, total), F32),
            jax.ShapeDtypeStruct((3, rows, 1), F32),
        ],
        in_specs=[
            fixed(rows, width),
            pl.BlockSpec((rows, low), lambda i: (0, i)),
            pl.BlockSpec((shards, k_rows, cols), lambda i: (0, 0, i)),
            pl.BlockSpec((low, cols), lambda i: (0, i)),
        ],
        out_specs=[
            pl.BlockSpec((rows, cols), lambda i: (0, i)),
            pl.BlockSpec((1, rows, 1), lambda i: (i, 0, 0)),
        ],
        compiler_params=BIG,
        cost_estimate=pl.CostEstimate(
            flops=2 * rows * width * total, bytes_accessed=2 * first.size, transcendentals=0
        ),
        name="qkv_product",
    )(x, latents, first, second)


def add_kernel(parts, a, weight, first, second, pick, *refs):
    outs, (latent_out, latent) = refs[:parts], refs[parts:]

    @pl.when(pl.program_id(0) == 0)
    def _():
        latent[...] = (mm(a[...], first[...]) * pick[...]).astype(BF16)
        latent_out[...] = latent[...]

    result = mm_nt(a[...], weight[...]) + mm(latent[...], second[...])
    size = result.shape[0] // parts
    for i in range(parts):
        outs[i][...] = result[i * size : (i + 1) * size].astype(BF16)


def add_product(a, weight, first, second, pick, parts, tile=512):
    rows, depth = a.shape
    width, low = weight.shape[0], first.shape[1]
    size = rows // parts
    return pl.pallas_call(
        functools.partial(add_kernel, parts),
        grid=(width // tile,),
        out_shape=[jax.ShapeDtypeStruct((size, width), BF16)] * parts
        + [jax.ShapeDtypeStruct((rows, low), BF16)],
        in_specs=[
            fixed(rows, depth),
            pl.BlockSpec((tile, depth), lambda i: (i, 0)),
            fixed(depth, low),
            pl.BlockSpec((low, tile), lambda i: (0, i)),
            fixed(rows, low),
        ],
        out_specs=[pl.BlockSpec((size, tile), lambda i: (0, i))] * parts + [fixed(rows, low)],
        scratch_shapes=[pltpu.VMEM((rows, low), BF16)],
        compiler_params=BIG,
        cost_estimate=pl.CostEstimate(
            flops=2 * rows * width * depth, bytes_accessed=2 * weight.size, transcendentals=0
        ),
        name="add_product",
    )(a, weight, first, second, pick)


def back_kernel(parts, a, weight, u, first, *outs):
    result = mm_nt(a[...], flat(weight[...])) + mm_nt(u[...], first[...])
    size = result.shape[0] // parts
    for i in range(parts):
        outs[i][...] = result[i * size : (i + 1) * size].astype(BF16)


def back_product(a, group, weight, k_rows, u, first, parts):
    rows, depth = a.shape
    rows //= 2
    shards = weight.shape[0]
    width, low = first.shape
    per = max(1, 512 // k_rows)
    size = rows // parts
    return pl.pallas_call(
        functools.partial(back_kernel, parts),
        grid=(shards // per,),
        out_shape=[jax.ShapeDtypeStruct((size, width), BF16)] * parts,
        in_specs=[
            fixed(rows, depth, at=(group, 0)),
            pl.BlockSpec((per, k_rows, depth), lambda i: (i, 0, 0)),
            fixed(rows, low, at=(group, 0)),
            pl.BlockSpec((per * k_rows, low), lambda i: (i, 0)),
        ],
        out_specs=[pl.BlockSpec((size, per * k_rows), lambda i: (0, i))] * parts,
        compiler_params=BIG,
        cost_estimate=pl.CostEstimate(
            flops=2 * rows * width * depth, bytes_accessed=2 * width * depth, transcendentals=0
        ),
        name="back_product",
    )(a, weight, u, first)


def gate_up_kernel(h, first, pick, w_g, w_u, b_g, b_u, gate_out, up_out, act, latent_out, latent):
    low = pick.shape[1]

    @pl.when(pl.program_id(0) == 0)
    def _():
        both = mm(h[...], first[...])
        latent[:, :low] = (both[:, :low] * pick[...]).astype(BF16)
        latent[:, low:] = (both[:, low:] * pick[...]).astype(BF16)
        latent_out[...] = latent[...]

    gate = mm(h[...], w_g[...]) + mm(latent[:, :low], b_g[...])
    up = mm(h[...], w_u[...]) + mm(latent[:, low:], b_u[...])
    gate_out[...] = gate
    up_out[...] = up
    act[...] = (gate / (1.0 + jnp.exp(-gate)) * up).astype(BF16)


def gate_up_product(h, w_gu, a_gu, b_gu, pick, tile=512):
    rows, width = h.shape
    units, low = w_gu.shape[1] // 2, pick.shape[1]
    n = units // tile
    left = lambda depth: pl.BlockSpec((depth, tile), lambda i: (0, i))
    out = pl.BlockSpec((rows, tile), lambda i: (0, i))
    return pl.pallas_call(
        gate_up_kernel,
        grid=(n,),
        out_shape=[jax.ShapeDtypeStruct((rows, units), F32)] * 2
        + [
            jax.ShapeDtypeStruct((rows, units), BF16),
            jax.ShapeDtypeStruct((rows, 2 * low), BF16),
        ],
        in_specs=[
            fixed(rows, width),
            fixed(width, 2 * low),
            fixed(rows, low),
            left(width),
            pl.BlockSpec((width, tile), lambda i: (0, i + n)),
            left(low),
            pl.BlockSpec((low, tile), lambda i: (1, i)),
        ],
        out_specs=[out, out, out, fixed(rows, 2 * low)],
        scratch_shapes=[pltpu.VMEM((rows, 2 * low), BF16)],
        compiler_params=BIG,
        cost_estimate=pl.CostEstimate(
            flops=4 * rows * width * units, bytes_accessed=4 * width * units, transcendentals=0
        ),
        name="gate_up_product",
    )(h, a_gu, pick, w_gu, w_gu, b_gu, b_gu)


def ff_back_kernel(
    parts, steps, d_ff, b_down, pick, w_down, a_down, gate, up, w_g, w_u, b_g, b_u, a_gu, *refs
):
    outs, (d_gate_out, d_up_out, u_out, u_down_out, acc, u_g, u_u, u_down) = refs[:parts], refs[parts:]
    i = pl.program_id(0)

    @pl.when(i == 0)
    def _():
        u_down[...] = (mm_nt(d_ff[...], b_down[...]) * pick[...]).astype(BF16)
        u_down_out[...] = u_down[...]

    d_act = mm(d_ff[...], w_down[...]) + mm_nt(u_down[...], a_down[...])
    g = gate[...]
    sigmoid = 1.0 / (1.0 + jnp.exp(-g))
    silu = g * sigmoid
    d_gate = (d_act * up[...] * (sigmoid + silu * (1.0 - sigmoid))).astype(BF16)
    d_up = (d_act * silu).astype(BF16)
    d_gate_out[...] = d_gate
    d_up_out[...] = d_up
    part = mm_nt(d_gate, w_g[...]) + mm_nt(d_up, w_u[...])
    part_g, part_u = mm_nt(d_gate, b_g[...]), mm_nt(d_up, b_u[...])

    @pl.when(i == 0)
    def _():
        acc[...] = part
        u_g[...] = part_g
        u_u[...] = part_u

    @pl.when(i > 0)
    def _():
        acc[...] += part
        u_g[...] += part_g
        u_u[...] += part_u

    @pl.when(i == steps - 1)
    def _():
        low = pick.shape[1]
        last_g = (u_g[...] * pick[...]).astype(BF16)
        last_u = (u_u[...] * pick[...]).astype(BF16)
        u_out[:, :low] = last_g
        u_out[:, low:] = last_u
        size = acc.shape[0] // parts
        for p in range(parts):
            at = slice(p * size, (p + 1) * size)
            outs[p][...] = (
                acc[at, :]
                + mm_nt(last_g[at], a_gu[:, :low])
                + mm_nt(last_u[at], a_gu[:, low:])
            ).astype(BF16)


def ff_back(d_ff, b_down, pick, w_down, a_down, gate, up, w_gu, b_gu, a_gu, parts, tile=512):
    rows, width = d_ff.shape
    units, low = gate.shape[1], pick.shape[1]
    n = units // tile
    size = rows // parts
    column = lambda depth: pl.BlockSpec((depth, tile), lambda i: (0, i))
    return pl.pallas_call(
        functools.partial(ff_back_kernel, parts, n),
        grid=(n,),
        out_shape=[jax.ShapeDtypeStruct((size, width), BF16)] * parts
        + [jax.ShapeDtypeStruct((rows, units), BF16)] * 2
        + [
            jax.ShapeDtypeStruct((rows, 2 * low), BF16),
            jax.ShapeDtypeStruct((rows, low), BF16),
        ],
        in_specs=[
            fixed(rows, width),
            fixed(low, width),
            fixed(rows, low),
            column(width),
            pl.BlockSpec((tile, low), lambda i: (i, 0)),
            column(rows),
            column(rows),
            column(width),
            pl.BlockSpec((width, tile), lambda i: (0, i + n)),
            column(low),
            pl.BlockSpec((low, tile), lambda i: (1, i)),
            fixed(width, 2 * low),
        ],
        out_specs=[fixed(size, width)] * parts
        + [column(rows), column(rows), fixed(rows, 2 * low), fixed(rows, low)],
        scratch_shapes=[
            pltpu.VMEM((rows, width), F32),
            pltpu.VMEM((rows, low), F32),
            pltpu.VMEM((rows, low), F32),
            pltpu.VMEM((rows, low), BF16),
        ],
        compiler_params=BIG,
        cost_estimate=pl.CostEstimate(
            flops=6 * rows * width * units, bytes_accessed=6 * width * units, transcendentals=0
        ),
        name="ff_back",
    )(d_ff, b_down, pick, w_down, a_down, gate, up, w_gu, w_gu, b_gu, b_gu, a_gu)


def local(
    layer_input,
    cotangent,
    query_key_value_weight,
    output_weight,
    gate_up_weight,
    down_weight,
    input_first_factor,
    output_first_factor,
    down_first_factor,
    query_key_value_second,
    gate_up_second_factor,
    output_down_second_factor,
    norm_gain_table,
    sequence_adapter,
    block_sequence,
    block_position,
):
    tp, tp_rank = lax.axis_size("tp"), lax.axis_index("tp")
    seqs, seq_rank = lax.axis_size("seq"), lax.axis_index("seq")
    own_rows, width = layer_input.shape
    rows = own_rows * tp
    part = own_rows // 2
    my_blocks = rows // BLK
    cols = query_key_value_weight.shape[2]
    heads = cols // HEAD_DIM
    hidden_cols = gate_up_weight.shape[2]
    k_rows = query_key_value_weight.shape[1]
    slots_a = input_first_factor.shape[2]
    rank_cols = output_first_factor.shape[1]
    group = seqs // heads
    head_rank, group_rank = seq_rank // group, seq_rank % group
    n_seq = sequence_adapter.shape[0]
    groups = (0, 1)

    runs = row_runs(tp)
    piece_at = jnp.stack([2 * (tp_rank ^ mask) + which for mask, which in runs]).astype(jnp.int32)
    token = (piece_at[:, None] * part + jnp.arange(part, dtype=jnp.int32)[None, :]).reshape(-1)
    token_block, offset = token // BLK, token % BLK
    block_ids = seq_rank * my_blocks + jnp.arange(my_blocks, dtype=jnp.int32)
    place_blocks = block_position[block_ids]
    adapter_blocks = sequence_adapter[block_sequence[block_ids]]
    in_block = token_block[:, None] == jnp.arange(my_blocks, dtype=jnp.int32)[None, :]
    pick = lambda per_block: jnp.sum(jnp.where(in_block, per_block[None, :], 0), axis=1)
    select = (
        jnp.arange(slots_a, dtype=jnp.int32)[None, :] // ADAPTER_RANK
        == pick(adapter_blocks)[:, None]
    ).astype(F32) * 2.0
    half = rows // 2
    selects = [select[:half], select[half:]]
    start = jnp.where(place_blocks < PROMPT_BLOCKS, place_blocks, PROMPT_BLOCKS) * BLK
    position = pick(start) + offset
    frequency = THETA ** (-(jnp.arange(HEAD_DIM // 2, dtype=F32) * 2.0) / HEAD_DIM)
    angles = position.astype(F32)[:, None] * frequency[None, :]
    cosine, sine = jnp.cos(angles), jnp.sin(angles)
    cs = jnp.concatenate([cosine, cosine, -sine, sine], axis=1)

    a_part = k_rows // tp
    b_part = width // tp
    a_mine = lax.dynamic_slice_in_dim(input_first_factor, tp_rank * a_part, a_part, 1)
    b_mine = lax.dynamic_slice_in_dim(output_down_second_factor, tp_rank * b_part, b_part, 2)
    first = jnp.concatenate(
        [
            query_key_value_weight.transpose(1, 0, 2).reshape(k_rows, 3 * cols),
            query_key_value_second.transpose(1, 0, 2).reshape(rank_cols, 3 * cols),
            a_mine[:3].reshape(-1, 3 * cols),
        ],
        axis=0,
    )
    x_parts = [layer_input] + [
        lax.ppermute(layer_input, "tp", [(i, i ^ mask) for i in range(tp)]) for mask in range(1, tp)
    ]
    x = jnp.concatenate(
        [x_parts[mask][which * part : (which + 1) * part] for mask, which in runs], axis=0
    )
    pick3 = jnp.tile(select, (1, 3))
    first = lax.all_gather(first, "seq", axis=0)
    pieces = [
        output_weight.T,
        output_first_factor.T,
        b_mine.reshape(-1, cols),
        a_mine[3:].reshape(-1, cols),
        down_first_factor.T.reshape(-1, cols),
        gate_up_second_factor.reshape(-1, cols),
    ]
    packed = jnp.concatenate(pieces, axis=0)
    first, x, cs, pick3, packed, w_gu, w_down = lax.optimization_barrier(
        (
            first,
            x,
            cs,
            pick3,
            packed,
            gate_up_weight.transpose(1, 0, 2).reshape(k_rows, 2 * hidden_cols),
            down_weight.T,
        )
    )
    packed = lax.all_gather(packed, "seq", axis=0)
    w_gu = lax.all_gather(w_gu, "seq", axis=0, tiled=True)
    w_down = lax.all_gather(w_down, "seq", axis=0, tiled=True)

    tp_order, seq_order = list(range(bits_of(tp))), list(range(bits_of(seqs)))
    a_qkv = first[:, k_rows + rank_cols :].reshape(seqs, 3, a_part, slots_a)
    a_qkv = a_qkv.transpose(0, 2, 1, 3).reshape(seqs, a_part, 3 * slots_a)
    a_parts = [a_qkv] + [
        lax.ppermute(a_qkv, "tp", [(i, i ^ mask) for i in range(tp)]) for mask in range(1, tp)
    ]
    a_qkv = jnp.zeros((seqs, tp, a_part, 3 * slots_a), BF16)
    for mask, value in enumerate(a_parts):
        a_qkv = lax.dynamic_update_slice(a_qkv, value[:, None], (0, tp_rank ^ mask, 0, 0))
    a_qkv = a_qkv.reshape(width, 3 * slots_a)
    b_qkv = first[:, k_rows : k_rows + rank_cols].reshape(slots_a, 3 * cols)
    owner = (
        ((head_rank - jnp.arange(heads)) % heads)[None, :] * group
        + ((group_rank + jnp.arange(group)) % group)[:, None]
    ).reshape(-1)
    held = (owner[:, None] * my_blocks + jnp.arange(my_blocks)[None, :]).reshape(-1)
    held_seq = block_sequence[held].astype(jnp.int32)
    held_place = block_position[held].astype(jnp.int32)
    prompt_count = n_seq * PROMPT_BLOCKS
    wanted = jnp.arange(prompt_count, dtype=jnp.int32)
    code = jnp.where(held_place < PROMPT_BLOCKS, held_seq * PROMPT_BLOCKS + held_place, -1)
    prompt_at = jnp.sum(
        jnp.where(
            code[None, :] == wanted[:, None], jnp.arange(held.shape[0], dtype=jnp.int32)[None, :], 0
        ),
        axis=1,
    ).astype(jnp.int32)
    own_blocks = heads * my_blocks
    tables = (held_seq[:own_blocks], held_place[:own_blocks], prompt_at)
    head_order = ((head_rank + jnp.arange(heads)) % heads).astype(jnp.int32)

    def head_shift(value, by):
        if by == 0:
            return value
        return lax.ppermute(
            value,
            "seq",
            [
                (h * group + j, ((h + by) % heads) * group + j)
                for h in range(heads)
                for j in range(group)
            ],
        )

    def group_shift(value, by):
        return lax.ppermute(
            value,
            "seq",
            [
                (h * group + j, h * group + (j + by) % group)
                for h in range(heads)
                for j in range(group)
            ],
        )

    own = lambda value, i: value[i * part : (i + 1) * part].astype(F32)
    gain = lax.dynamic_slice_in_dim(norm_gain_table[:2], tp_rank * cols, cols, 1)
    latents = (mm(x, a_qkv) * pick3).astype(BF16)
    z, squares = qkv_product(
        x, latents, first, b_qkv, k_rows, cols
    )
    squares = sum_rows(squares[:2].reshape(2, rows), tp)
    inv = lax.rsqrt(squares / width + EPS)
    inv, packed = lax.optimization_barrier((inv, packed))
    split, at = [], 0
    for piece in pieces:
        split.append(packed[:, at : at + piece.shape[0]])
        at += piece.shape[0]
    w_o = split[0].reshape(width, cols)
    a_o = split[1].reshape(slots_a, cols).T
    shared = gather_order(jnp.concatenate(split[2:4], axis=1), "tp", tp, tp_order)
    b_size = split[2].shape[1]
    b_od = (
        shared[:, :, :b_size]
        .reshape(tp, seqs, 2, rank_cols, b_part)
        .transpose(2, 1, 3, 0, 4)
        .reshape(2, slots_a, width)
    )
    a_gu = (
        shared[:, :, b_size:]
        .reshape(tp, seqs, 2, a_part, slots_a)
        .transpose(1, 0, 3, 2, 4)
        .reshape(width, 2 * slots_a)
    )
    a_down = split[4].reshape(slots_a, hidden_cols).T
    b_gu = (
        split[5]
        .reshape(seqs, 2, rank_cols, hidden_cols)
        .transpose(1, 0, 2, 3)
        .reshape(2 * slots_a, hidden_cols)
    )
    spread = spread_heads(head_order, piece_at, z, inv.T, cs, gain, heads)
    near = [head_shift(spread[k], k) for k in range(heads)]
    far = [group_shift(near[k][1:], -j) for j in range(1, group) for k in range(heads)]
    far, w_o, a_o, b_od, a_gu, a_down, b_gu = lax.optimization_barrier(
        (far, w_o, a_o, b_od, a_gu, a_down, b_gu)
    )
    attended = attend(tables, near, far, prompt_count)
    heads_out = collect_heads(
        head_order, piece_at, [head_shift(attended[k], -k) for k in range(heads)]
    )

    def norm_back(values_in, inv, scaled):
        return inv * scaled - values_in * inv**3 * jnp.mean(scaled * values_in, axis=1, keepdims=True)

    def inverse_norm(values_in):
        return lax.rsqrt(jnp.mean(values_in * values_in, axis=1, keepdims=True) + EPS)

    *far_part, o_latent1 = add_product(heads_out[1], w_o, a_o, b_od[0], selects[1], 2)
    near_part, o_latent0 = add_product(heads_out[0], w_o, a_o, b_od[0], selects[0], 1)
    attn_out = scatter_groups(near_part, far_part, tp)
    scale_o = [inverse_norm(value) for value in attn_out]
    hidden = [
        own(layer_input, i) + attn_out[i] * scale_o[i] * norm_gain_table[2] for i in groups
    ]
    h_low = gather_groups([value.astype(BF16) for value in hidden], tp)

    gates, ups, acts, gu_latents = zip(
        *[gate_up_product(h_low[g], w_gu, a_gu, b_gu, selects[g]) for g in groups]
    )
    acts, w_down = lax.optimization_barrier((acts, w_down))
    *far_part, d_latent1 = add_product(acts[1], w_down, a_down, b_od[1], selects[1], 2)
    near_part, d_latent0 = add_product(acts[0], w_down, a_down, b_od[1], selects[0], 1)
    ff_out = scatter_groups(near_part, far_part, tp)
    scale_f = [inverse_norm(value) for value in ff_out]
    output = jnp.concatenate(
        [hidden[i] + ff_out[i] * scale_f[i] * norm_gain_table[3] for i in groups], axis=0
    )

    d_ffs = gather_groups(
        [
            norm_back(ff_out[i], scale_f[i], own(cotangent, i) * norm_gain_table[3]).astype(BF16)
            for i in groups
        ],
        tp,
    )
    backs = [
        ff_back(
            d_ffs[g], b_od[1], selects[g], w_down, a_down, gates[g], ups[g], w_gu, b_gu, a_gu, 1 + g
        )
        for g in groups
    ]
    summed = scatter_groups(backs[0][0], backs[1][:2], tp)
    d_gates, d_ups, u_gus, u_downs = zip(*[back[-4:] for back in backs])
    d_hidden = [own(cotangent, i) + summed[i] for i in groups]
    d_attn = [
        norm_back(attn_out[i], scale_o[i], d_hidden[i] * norm_gain_table[2]).astype(BF16)
        for i in groups
    ]
    d_latents = (d_latent0, d_latent1)
    d_rows = gather_groups(d_attn, tp)
    o_latents = (o_latent0, o_latent1)
    u_os, grads = [], []
    for g in groups:
        u_os.append((mm_nt(d_rows[g], b_od[0]) * selects[g]).astype(BF16))
        d_heads = (mm(d_rows[g], w_o) + mm_nt(u_os[g], a_o)).astype(BF16)
        grads.append(
            [
                head_shift(
                    lax.dynamic_slice_in_dim(d_heads, head_order[k] * HEAD_DIM, HEAD_DIM, 1), k
                )
                for k in range(heads)
            ]
        )
    grads = [grads[g][k] for k in range(heads) for g in groups]
    results = list(attend_back(tables, piece_at, near, far, grads, prompt_count))
    dqs = [head_shift(results[k], -k) for k in range(heads)]
    d_kv = results[heads].reshape(2, heads, rows, HEAD_DIM)
    others = [
        group_shift(results[heads + j], j).reshape(2, heads, rows, HEAD_DIM) for j in range(1, group)
    ]
    dkvs = []
    for k in range(heads):
        total = d_kv[:, k].astype(F32)
        for other in others:
            total = total + other[:, k].astype(F32)
        dkvs.append(head_shift(total.astype(BF16), -k))
    dkvs[1], u_os, o_latents, u_downs, d_latents, u_gus, gu_latents = lax.optimization_barrier(
        (dkvs[1], u_os, o_latents, u_downs, d_latents, u_gus, gu_latents)
    )
    both_groups = lambda f: f(0) + f(1)
    grad_a_down = both_groups(lambda g: mm_tn(u_downs[g], acts[g]))
    grad_b_down = both_groups(lambda g: mm_tn(d_latents[g], d_ffs[g]))
    grad_a_gu = both_groups(lambda g: mm_tn(h_low[g], u_gus[g]))
    grad_b_gate = both_groups(lambda g: mm_tn(gu_latents[g][:, :slots_a], d_gates[g]))
    grad_b_up = both_groups(lambda g: mm_tn(gu_latents[g][:, slots_a:], d_ups[g]))
    lane = 2 * slots_a
    shards = lambda value: value.astype(BF16).reshape(seqs, -1, lane)
    early = jnp.concatenate(
        [
            shards(grad_a_gu),
            shards(grad_b_down),
            shards(grad_a_down),
            shards(grad_b_gate),
            shards(grad_b_up),
        ],
        axis=1,
    )
    grad_a_o = both_groups(lambda g: mm_tn(u_os[g], heads_out[g]))
    grad_b_o = both_groups(lambda g: mm_tn(o_latents[g], d_rows[g]))
    late_o = jnp.concatenate(
        [
            grad_b_o.astype(BF16).reshape(seqs, -1, cols),
            grad_a_o.astype(BF16).reshape(seqs, -1, cols),
        ],
        axis=1,
    )
    dqs, dkvs, early, late_o = lax.optimization_barrier((dqs, dkvs, early, late_o))
    early = lax.psum_scatter(early, "seq", scatter_dimension=0, tiled=False)
    dqs, dkvs, late_o = lax.optimization_barrier((dqs, dkvs, late_o))
    late_o = scatter_order(late_o, "seq", seqs, seq_order)
    scaled, parts = unturn_heads(head_order, piece_at, dqs, dkvs, z, cs, gain)
    parts = sum_rows(parts.T, tp) / width
    coef = jnp.concatenate([inv, inv**3 * parts], axis=0)
    dz, us = norm_back_heads(head_order, piece_at, dkvs, scaled, z, coef.T, b_qkv, select)
    grad_a_qkv = mm_tn(x, us)
    grad_b_qkv = mm_tn(latents, dz)
    lane3 = 3 * slots_a
    grad_b_qkv = jnp.concatenate(
        [
            grad_b_qkv[i * slots_a : (i + 1) * slots_a, i * cols : (i + 1) * cols]
            for i in range(3)
        ],
        axis=1,
    )
    late = jnp.concatenate(
        [
            grad_a_qkv.astype(BF16).reshape(seqs, k_rows, lane3),
            grad_b_qkv.astype(BF16).reshape(seqs, -1, lane3),
        ],
        axis=1,
    )
    dz, late = lax.optimization_barrier((dz, late))
    far_part = list(back_product(dz, 1, first, k_rows, us, a_qkv, 2))
    far_part[0], dz, early, late_o = lax.optimization_barrier((far_part[0], dz, early, late_o))
    (near_part,) = back_product(dz, 0, first, k_rows, us, a_qkv, 1)

    down_size = rank_cols * width // lane
    o_size = rank_cols * width // cols
    both = jnp.concatenate(
        [early[: k_rows + down_size], late_o[:o_size].astype(BF16).reshape(-1, lane)], axis=0
    )
    both = sum_all(both, "tp", tp).astype(F32)
    late = lax.psum_scatter(late, "seq", scatter_dimension=0, tiled=False)
    summed = scatter_groups(near_part, far_part, tp)
    summed, late = lax.optimization_barrier((summed, late))
    input_grad = jnp.concatenate([d_hidden[i] + summed[i] for i in groups], axis=0)
    grad_a_qkv = late[:k_rows].astype(F32)
    for mask in range(1, tp):
        got = lax.ppermute(late[:k_rows], "tp", [(i, i ^ mask) for i in range(tp)])
        grad_a_qkv = grad_a_qkv + got.astype(F32)
    grad_a_gu = both[:k_rows]
    grad_b_down = both[k_rows : k_rows + down_size].reshape(rank_cols, width)
    grad_b_o = both[k_rows + down_size :].reshape(rank_cols, width)
    a_size = rank_cols * hidden_cols // lane
    rest = early[k_rows + down_size :].astype(F32)
    grad_a_down = rest[:a_size].reshape(rank_cols, hidden_cols).T
    grad_b_gu = rest[a_size:].reshape(2, rank_cols, hidden_cols)
    grad_a_o = late_o[o_size:].T
    grad_b_qkv = late[k_rows:].astype(F32).reshape(rank_cols, 3, cols).transpose(1, 0, 2)
    grad_a_in = jnp.stack(
        [grad_a_qkv[:, i * slots_a : (i + 1) * slots_a] for i in range(3)]
        + [grad_a_gu[:, i * slots_a : (i + 1) * slots_a] for i in range(2)]
    )
    grad_b_out = jnp.stack([grad_b_o, grad_b_down])
    return (output, input_grad, grad_a_in, grad_a_o, grad_a_down, grad_b_qkv, grad_b_gu, grad_b_out)


def solution(mesh):
    return jax.shard_map(
        local,
        mesh=mesh,
        in_specs=(
            P(("seq", "tp"), None),
            P(("seq", "tp"), None),
            P(None, "seq", "tp"),
            P("tp", "seq"),
            P(None, "seq", "tp"),
            P("tp", "seq"),
            P(None, "seq", None),
            P("tp", "seq"),
            P("tp", "seq"),
            P(None, "seq", "tp"),
            P(None, "seq", "tp"),
            P(None, "seq", None),
            P(),
            P(),
            P(),
            P(),
        ),
        out_specs=(
            P(("seq", "tp"), None),
            P(("seq", "tp"), None),
            P(None, "seq", None),
            P("tp", "seq"),
            P("tp", "seq"),
            P(None, "seq", "tp"),
            P(None, "seq", "tp"),
            P(None, "seq", None),
        ),
        check_vma=False,
    )
```

```python
import functools

import jax
import jax.numpy as jnp
from jax import lax
from jax.experimental import pallas as pl
from jax.experimental.pallas import tpu as pltpu
from jax.sharding import PartitionSpec as P

HEAD_DIM = 128
ADAPTER_RANK = 16
BLK = 128
PROMPT_BLOCKS = 8
EPS = 1e-06
THETA = 500000.0
NEG = -1e30
LOG2E = 1.4426950408889634
F32 = jnp.float32
BF16 = jnp.bfloat16


def mm(a, b):
    return jnp.dot(a, b, preferred_element_type=F32)


def mm_nt(a, b):
    return lax.dot_general(a, b, (((1,), (1,)), ((), ())), preferred_element_type=F32)


def mm_tn(a, b):
    return lax.dot_general(a, b, (((0,), (0,)), ((), ())), preferred_element_type=F32)


def bits_of(count):
    n = count.bit_length() - 1
    assert 1 << n == count
    return n


def flip(value, axis, count, bit):
    return lax.ppermute(value, axis, [(i, i ^ (1 << bit)) for i in range(count)])


def part_orders(count):
    order = list(range(bits_of(count)))
    return (order, order[::-1])


def group_masks(count):
    groups = ([], [])
    for part, order in enumerate(part_orders(count)):
        for j in range(count):
            mask = sum(1 << bit for i, bit in enumerate(order) if (j >> i) & 1)
            groups[j >= count // 2].append((mask, part))
    return groups


def row_runs(count):
    return [run for masks in group_masks(count) for run in masks]


def gather_groups(parts, count, beside=None):
    near, far = [], []
    for value, order in zip(parts, part_orders(count)):
        for bit in order[:-1]:
            value = jnp.concatenate([value, flip(value, "tp", count, bit)], axis=0)
        near.append(value)
    if beside is not None:
        near[1], beside = lax.optimization_barrier((near[1], beside))
    for value, order in zip(near, part_orders(count)):
        far.append(flip(value, "tp", count, order[-1]))
    if beside is not None:
        return jnp.concatenate(near, axis=0), jnp.concatenate(far, axis=0), beside
    return jnp.concatenate(near, axis=0), jnp.concatenate(far, axis=0)


def scatter_groups(near, far, count):
    return scatter_rest(scatter_first(near, far, count), count)


def scatter_first(near, far, count):
    out = []
    size = near.shape[0] // 2
    for i, order in enumerate(part_orders(count)):
        got = flip(far[i], "tp", count, order[-1])
        out.append(near[i * size : (i + 1) * size].astype(F32) + got.astype(F32))
    return out


def scatter_rest(totals, count):
    out = []
    for total, order in zip(totals, part_orders(count)):
        for bit in order[-2::-1]:
            half = total.shape[0] // 2
            got = flip(total[half:].astype(BF16), "tp", count, bit)
            total = total[:half] + got.astype(F32)
        out.append(total)
    return out


def sum_rows(value, count):
    runs = row_runs(count)
    value = value.reshape(value.shape[0], len(runs), -1)
    total = value
    for mask in range(1, count):
        got = lax.ppermute(value, "tp", [(i, i ^ mask) for i in range(count)])
        order = [runs.index((other ^ mask, which)) for other, which in runs]
        total = total + jnp.concatenate([got[:, j : j + 1] for j in order], axis=1)
    return total.reshape(value.shape[0], -1)


def copy_all(pairs, sem):
    copies = [pltpu.make_async_copy(src, dst, sem.at[i]) for i, (src, dst) in enumerate(pairs)]
    for copy in copies:
        copy.start()
    for copy in copies:
        copy.wait()


def gather_prompt(prompt_at, source, target, count):
    def step(i, carry):
        start = pl.multiple_of(prompt_at[i] * BLK, BLK)
        target[pl.ds(pl.multiple_of(i * BLK, BLK), BLK), :] = source[pl.ds(start, BLK), :]
        return carry

    lax.fori_loop(0, count, step, 0)


def masked_scores(keys, own_keys, queries, place, scale):
    prompt = mm_nt(keys, queries) * scale
    block = lax.broadcasted_iota(jnp.int32, prompt.shape, 0) // BLK
    prompt = jnp.where(block < place, prompt, NEG)
    own = mm_nt(own_keys, queries) * scale
    causal = lax.broadcasted_iota(jnp.int32, own.shape, 0) <= lax.broadcasted_iota(
        jnp.int32, own.shape, 1
    )
    own = jnp.where(causal, own, NEG)
    top = jnp.maximum(jnp.max(prompt, axis=0, keepdims=True), jnp.max(own, axis=0, keepdims=True))
    prompt = jnp.exp2(prompt - top)
    own = jnp.exp2(own - top)
    total = jnp.sum(prompt, axis=0, keepdims=True) + jnp.sum(own, axis=0, keepdims=True)
    return prompt, own, 1.0 / total


def load_plan(slots, group, rows, refs, q_buf, k_buf, v_buf):
    plan = []
    for i in range(slots):
        plan.append((refs[i].at[0], q_buf.at[pl.ds(i * rows, rows)]))
    for i in range(slots * group):
        at = pl.ds(i * rows, rows)
        skip = int(i < slots)
        plan += [(refs[i].at[skip], k_buf.at[at]), (refs[i].at[skip + 1], v_buf.at[at])]
    return plan


def attend_kernel(slots, group, rows, prompt_count, q_seq, q_place, prompt_at, *refs):
    n_in = slots * group
    outs = refs[n_in : n_in + slots]
    q_buf, k_buf, v_buf, kp, vp, o_buf, sem = refs[n_in + slots :]
    copy_all(load_plan(slots, group, rows, refs, q_buf, k_buf, v_buf), sem)
    gather_prompt(prompt_at, k_buf, kp, prompt_count)
    gather_prompt(prompt_at, v_buf, vp, prompt_count)
    scale = HEAD_DIM ** (-0.5) * LOG2E
    span = PROMPT_BLOCKS * BLK

    def block(i):
        at = pl.ds(pl.multiple_of(i * BLK, BLK), BLK)
        of_seq = pl.ds(pl.multiple_of(q_seq[i] * span, span), span)
        prompt, own, inverse = masked_scores(
            kp[of_seq, :], k_buf[at, :], q_buf[at, :], q_place[i], scale
        )
        result = mm_tn(vp[of_seq, :], prompt.astype(BF16)) + mm_tn(v_buf[at, :], own.astype(BF16))
        return at, (result * inverse).T.astype(BF16)

    blocks = slots * rows // BLK
    pair = 2 if blocks % 2 == 0 else 1

    def step(i, carry):
        for at, result in [block(i * pair + j) for j in range(pair)]:
            o_buf[at, :] = result
        return carry

    lax.fori_loop(0, blocks // pair, step, 0)
    copy_all([(o_buf.at[pl.ds(i * rows, rows)], outs[i]) for i in range(slots)], sem)


def attend_back_kernel(
    slots, group, rows, pieces, prompt_count, q_seq, q_place, prompt_at, piece_at, *refs
):
    n_in = slots * group
    n_grad = slots * 2
    grads = refs[n_in : n_in + n_grad]
    outs = refs[n_in + n_grad : n_in + n_grad + slots]
    near_out = refs[n_in + n_grad + slots]
    rest = refs[n_in + n_grad + slots + 1 :]
    far_outs, rest = rest[: group - 1], rest[group - 1 :]
    q_buf, k_buf, v_buf, do_buf, kp, vp, dkp, dvp, dq_buf, dkv_buf, sem = rest
    plan = load_plan(slots, group, rows, refs, q_buf, k_buf, v_buf)
    size = rows // pieces
    for i in range(slots):
        for p in range(pieces):
            half, at = divmod(p, pieces // 2)
            to = pl.multiple_of(i * rows + piece_at[p] * size, 16)
            plan.append(
                (grads[i * 2 + half].at[pl.ds(at * size, size)], do_buf.at[pl.ds(to, size)])
            )
    copy_all(plan, sem)
    gather_prompt(prompt_at, k_buf, kp, prompt_count)
    gather_prompt(prompt_at, v_buf, vp, prompt_count)
    dkp[...] = jnp.zeros_like(dkp)
    dvp[...] = jnp.zeros_like(dvp)
    scale = HEAD_DIM ** (-0.5)
    span = PROMPT_BLOCKS * BLK
    own_rows = slots * rows
    zeros = jnp.zeros((BLK, HEAD_DIM), BF16)

    def rows_of(i):
        return pl.ds(pl.multiple_of(i * BLK, BLK), BLK)

    def clear(i, carry):
        for j in range(1, group):
            dkv_buf[j, 0, rows_of(i), :] = zeros
            dkv_buf[j, 1, rows_of(i), :] = zeros
        return carry

    lax.fori_loop(0, own_rows // BLK, clear, 0)

    def block(i):
        at = rows_of(i)
        seq, place = q_seq[i], q_place[i]
        of_seq = pl.ds(pl.multiple_of(seq * span, span), span)
        queries, grad = q_buf[at, :], do_buf[at, :]
        prompt, own, inverse = masked_scores(
            kp[of_seq, :], k_buf[at, :], queries, place, scale * LOG2E
        )
        prompt, own = prompt * inverse, own * inverse
        d_prompt = mm_nt(vp[of_seq, :], grad)
        d_own = mm_nt(v_buf[at, :], grad)
        delta = jnp.sum(prompt * d_prompt, axis=0, keepdims=True) + jnp.sum(
            own * d_own, axis=0, keepdims=True
        )
        ds_prompt = (prompt * (d_prompt - delta)).astype(BF16)
        ds_own = (own * (d_own - delta)).astype(BF16)
        dq = mm_tn(ds_prompt, kp[of_seq, :]) + mm_tn(ds_own, k_buf[at, :])
        return (
            at,
            of_seq,
            (dq * scale).astype(BF16),
            mm(prompt.astype(BF16), grad),
            mm(ds_prompt, queries) * scale,
            (mm(ds_own, queries) * scale).astype(BF16),
            mm(own.astype(BF16), grad).astype(BF16),
        )

    blocks = own_rows // BLK
    pair = 2 if blocks % 2 == 0 else 1

    def step(i, carry):
        for at, of_seq, dq, dv_prompt, dk_prompt, dk_own, dv_own in [
            block(i * pair + j) for j in range(pair)
        ]:
            dq_buf[at, :] = dq
            dvp[of_seq, :] += dv_prompt
            dkp[of_seq, :] += dk_prompt
            dkv_buf[0, 0, at, :] = dk_own
            dkv_buf[0, 1, at, :] = dv_own
        return carry

    lax.fori_loop(0, blocks // pair, step, 0)

    def spread(i, carry):
        place = prompt_at[i]
        j, to = place // blocks, rows_of(place % blocks)
        dkv_buf[j, 0, to, :] = (dkv_buf[j, 0, to, :].astype(F32) + dkp[rows_of(i), :]).astype(BF16)
        dkv_buf[j, 1, to, :] = (dkv_buf[j, 1, to, :].astype(F32) + dvp[rows_of(i), :]).astype(BF16)
        return carry

    lax.fori_loop(0, prompt_count, spread, 0)
    plan = [(dq_buf.at[pl.ds(i * rows, rows)], outs[i]) for i in range(slots)]
    plan.append((dkv_buf.at[0], near_out))
    plan += [(dkv_buf.at[j], far_outs[j - 1]) for j in range(1, group)]
    copy_all(plan, sem)


ANY = pl.BlockSpec(memory_space=pl.ANY)


def attend(tables, near, far, prompt_count):
    slots = len(near)
    rows = near[0].shape[1]
    group = 1 + len(far) // slots
    own, every = slots * rows, slots * group * rows
    pairs = own * (PROMPT_BLOCKS + 1) * BLK
    wide = lambda count, kind=BF16: pltpu.VMEM((count, HEAD_DIM), kind)
    return pl.pallas_call(
        functools.partial(attend_kernel, slots, group, rows, prompt_count),
        out_shape=[jax.ShapeDtypeStruct((rows, HEAD_DIM), BF16)] * slots,
        grid_spec=pltpu.PrefetchScalarGridSpec(
            num_scalar_prefetch=3,
            in_specs=[ANY] * (slots * group),
            out_specs=[ANY] * slots,
            scratch_shapes=[
                wide(own),
                wide(every),
                wide(every),
                wide(prompt_count * BLK),
                wide(prompt_count * BLK),
                wide(own),
                pltpu.SemaphoreType.DMA((slots + 2 * slots * group,)),
            ],
        ),
        cost_estimate=pl.CostEstimate(
            flops=4 * pairs * HEAD_DIM, bytes_accessed=6 * every * HEAD_DIM, transcendentals=pairs
        ),
        name="attend",
    )(*tables, *near, *far)


def attend_back(tables, piece_at, near, far, grads, prompt_count):
    pieces = piece_at.shape[0]
    slots = len(near)
    rows = near[0].shape[1]
    group = 1 + len(far) // slots
    own, every = slots * rows, slots * group * rows
    pairs = own * (PROMPT_BLOCKS + 1) * BLK
    wide = lambda count, kind=BF16: pltpu.VMEM((count, HEAD_DIM), kind)
    return pl.pallas_call(
        functools.partial(attend_back_kernel, slots, group, rows, pieces, prompt_count),
        out_shape=[jax.ShapeDtypeStruct((rows, HEAD_DIM), BF16)] * slots
        + [jax.ShapeDtypeStruct((2, own, HEAD_DIM), BF16)] * group,
        grid_spec=pltpu.PrefetchScalarGridSpec(
            num_scalar_prefetch=4,
            in_specs=[ANY] * (slots * group + 2 * slots),
            out_specs=[ANY] * (slots + group),
            scratch_shapes=[
                wide(own),
                wide(every),
                wide(every),
                wide(own),
                wide(prompt_count * BLK),
                wide(prompt_count * BLK),
                wide(prompt_count * BLK, F32),
                wide(prompt_count * BLK, F32),
                wide(own),
                pltpu.VMEM((group, 2, own, HEAD_DIM), BF16),
                pltpu.SemaphoreType.DMA((slots + 2 * slots * group + slots * pieces,)),
            ],
        ),
        cost_estimate=pl.CostEstimate(
            flops=10 * pairs * HEAD_DIM, bytes_accessed=12 * every * HEAD_DIM, transcendentals=pairs
        ),
        name="attend_back",
    )(*tables, piece_at, *near, *far, *grads)


def turn(values, cosine, sine):
    return values * cosine + pltpu.roll(values, HEAD_DIM // 2, 1) * sine


def lanes(head, base=0):
    return pl.ds(pl.multiple_of(base + head * HEAD_DIM, HEAD_DIM), HEAD_DIM)


def here(size, width):
    return pl.BlockSpec((size, width), lambda p, order, piece_at: (p, 0))


def there(size, at=None, count=1):
    if at is None:
        return pl.BlockSpec((size, HEAD_DIM), lambda p, order, piece_at: (piece_at[p], 0))
    return pl.BlockSpec((count, size, HEAD_DIM), lambda p, order, piece_at: (at, piece_at[p], 0))


def all_of(value):
    return pl.BlockSpec(value.shape, lambda p, order, piece_at: (0, 0))


def piece_rows(index, size):
    return pl.ds(pl.multiple_of(index * size, 16), size)


def spread_kernel(slots, order, piece_at, z, inv, cs, gain, *outs):
    cols = slots * HEAD_DIM
    cosine, sine = cs[:, :HEAD_DIM], cs[:, HEAD_DIM:]
    for which in range(2):
        factor = inv[:, which : which + 1]
        for k in range(slots):
            head = order[k]
            scaled = z[:, lanes(head, which * cols)] * factor
            scaled = scaled * gain[which : which + 1, lanes(head)]
            outs[k][which, :, :] = turn(scaled, cosine, sine).astype(BF16)
    for k in range(slots):
        outs[k][2, :, :] = z[:, lanes(order[k], 2 * cols)].astype(BF16)


WHOLE = pl.BlockSpec(memory_space=pltpu.VMEM)
BIG = pltpu.CompilerParams(vmem_limit_bytes=56 * 1024 * 1024)


def spread_heads(order, piece_at, z, inv, cs, gain, slots):
    rows = z.shape[0]
    pieces = piece_at.shape[0]
    size = rows // pieces
    return pl.pallas_call(
        functools.partial(spread_kernel, slots),
        out_shape=[jax.ShapeDtypeStruct((3, rows, HEAD_DIM), BF16)] * slots,
        grid_spec=pltpu.PrefetchScalarGridSpec(
            num_scalar_prefetch=2,
            grid=(pieces,),
            in_specs=[
                here(size, z.shape[1]),
                here(size, inv.shape[1]),
                here(size, cs.shape[1]),
                all_of(gain),
            ],
            out_specs=[there(size, 0, 3)] * slots,
        ),
        compiler_params=BIG,
        name="spread_heads",
    )(order, piece_at, z, inv, cs, gain)


def collect_kernel(slots, pieces, order, piece_at, *refs):
    outs = refs[slots:]
    size = refs[0].shape[0] // pieces
    for p in range(pieces):
        half, at = divmod(p, pieces // 2)
        for k in range(slots):
            outs[half][pl.ds(at * size, size), lanes(order[k])] = refs[k][
                piece_rows(piece_at[p], size), :
            ]


def collect_heads(order, piece_at, parts):
    slots = len(parts)
    rows = parts[0].shape[0]
    return pl.pallas_call(
        functools.partial(collect_kernel, slots, piece_at.shape[0]),
        out_shape=[jax.ShapeDtypeStruct((rows // 2, slots * HEAD_DIM), BF16)] * 2,
        grid_spec=pltpu.PrefetchScalarGridSpec(
            num_scalar_prefetch=2, in_specs=[WHOLE] * slots, out_specs=[WHOLE] * 2
        ),
        name="collect_heads",
    )(order, piece_at, *parts)


def unturn_kernel(slots, order, piece_at, *refs):
    dqs, dkvs, rest = refs[:slots], refs[slots : 2 * slots], refs[2 * slots :]
    z, cs, gain, scaled_out, part_out = rest
    cols = slots * HEAD_DIM
    cosine, sine = cs[:, :HEAD_DIM], cs[:, HEAD_DIM:]
    for which in range(2):
        total = jnp.zeros((z.shape[0], HEAD_DIM), F32)
        for k in range(slots):
            head = order[k]
            grad = dqs[k][...] if which == 0 else dkvs[k][0, :, :]
            grad = turn(grad.astype(F32), cosine, -sine) * gain[which : which + 1, lanes(head)]
            scaled_out[:, lanes(head, which * cols)] = grad
            total = total + grad * z[:, lanes(head, which * cols)]
        part_out[:, which : which + 1] = jnp.sum(total, axis=1, keepdims=True)


def unturn_heads(order, piece_at, dqs, dkvs, z, cs, gain):
    slots = len(dqs)
    rows = z.shape[0]
    cols = slots * HEAD_DIM
    pieces = piece_at.shape[0]
    size = rows // pieces
    return pl.pallas_call(
        functools.partial(unturn_kernel, slots),
        out_shape=[
            jax.ShapeDtypeStruct((rows, 2 * cols), F32),
            jax.ShapeDtypeStruct((rows, 2), F32),
        ],
        grid_spec=pltpu.PrefetchScalarGridSpec(
            num_scalar_prefetch=2,
            grid=(pieces,),
            in_specs=[there(size)] * slots
            + [there(size, 0)] * slots
            + [here(size, 2 * cols), here(size, cs.shape[1]), all_of(gain)],
            out_specs=[here(size, 2 * cols), here(size, 2)],
        ),
        compiler_params=BIG,
        name="unturn_heads",
    )(order, piece_at, *dqs, *dkvs, z, cs, gain)


def norm_back_kernel(slots, order, piece_at, *refs):
    dkvs, (scaled, z, coef, second, pick, out, latent_out) = refs[:slots], refs[slots:]
    cols = slots * HEAD_DIM
    low = second.shape[0]
    for which in range(2):
        to = slice(which * cols, (which + 1) * cols)
        out[:, to] = (
            scaled[:, to] * coef[:, which : which + 1] - z[:, to] * coef[:, 2 + which : 3 + which]
        ).astype(BF16)
    for k in range(slots):
        out[:, lanes(order[k], 2 * cols)] = dkvs[k][0, :, :]
    for which in range(3):
        to = slice(which * cols, (which + 1) * cols)
        at = slice(which * low, (which + 1) * low)
        latent_out[:, at] = (mm_nt(out[:, to], second[:, to]) * pick[...]).astype(BF16)


def norm_back_heads(order, piece_at, dkvs, scaled, z, coef, second, pick):
    slots = len(dkvs)
    rows = z.shape[0]
    cols = slots * HEAD_DIM
    low = second.shape[0]
    pieces = piece_at.shape[0]
    size = rows // pieces
    return pl.pallas_call(
        functools.partial(norm_back_kernel, slots),
        out_shape=[
            jax.ShapeDtypeStruct((rows, 3 * cols), BF16),
            jax.ShapeDtypeStruct((rows, 3 * low), BF16),
        ],
        grid_spec=pltpu.PrefetchScalarGridSpec(
            num_scalar_prefetch=2,
            grid=(pieces,),
            in_specs=[there(size, 1)] * slots
            + [
                here(size, 2 * cols),
                here(size, 2 * cols),
                here(size, 4),
                all_of(second),
                here(size, low),
            ],
            out_specs=[here(size, 3 * cols), here(size, 3 * low)],
        ),
        compiler_params=BIG,
        name="norm_back_heads",
    )(order, piece_at, *dkvs, scaled, z, coef, second, pick)


def fixed(*shape, at=None):
    place = at or (0,) * len(shape)
    return pl.BlockSpec(shape, lambda i: place)


def flat(value):
    return value.reshape(-1, value.shape[-1])


def qkv_kernel(x, latent, weight, second, z, squares):
    i = pl.program_id(0)
    result = mm(x[...], flat(weight[...])) + mm(latent[...], flat(second[...]))
    z[...] = result
    squares[0, :, :] = jnp.sum(result * result, axis=1, keepdims=True)


def qkv_product(x, latents, first, second, k_rows, cols):
    rows, width = x.shape
    shards, _, total = first.shape
    low = latents.shape[1] // 3
    return pl.pallas_call(
        qkv_kernel,
        grid=(3,),
        out_shape=[
            jax.ShapeDtypeStruct((rows, total), F32),
            jax.ShapeDtypeStruct((3, rows, 1), F32),
        ],
        in_specs=[
            fixed(rows, width),
            pl.BlockSpec((rows, low), lambda i: (0, i)),
            pl.BlockSpec((shards, k_rows, cols), lambda i: (0, 0, i)),
            pl.BlockSpec((low, cols), lambda i: (0, i)),
        ],
        out_specs=[
            pl.BlockSpec((rows, cols), lambda i: (0, i)),
            pl.BlockSpec((1, rows, 1), lambda i: (i, 0, 0)),
        ],
        compiler_params=BIG,
        cost_estimate=pl.CostEstimate(
            flops=2 * rows * width * total, bytes_accessed=2 * first.size, transcendentals=0
        ),
        name="qkv_product",
    )(x, latents, first, second)


def add_kernel(parts, a, weight, first, second, pick, *refs):
    outs, (latent_out, latent) = refs[:parts], refs[parts:]

    @pl.when(pl.program_id(0) == 0)
    def _():
        latent[...] = (mm(a[...], first[...]) * pick[...]).astype(BF16)
        latent_out[...] = latent[...]

    result = mm_nt(a[...], weight[...]) + mm(latent[...], second[...])
    size = result.shape[0] // parts
    for i in range(parts):
        outs[i][...] = result[i * size : (i + 1) * size].astype(BF16)


def add_product(a, weight, first, second, pick, parts, tile=512):
    rows, depth = a.shape
    width, low = weight.shape[0], first.shape[1]
    size = rows // parts
    return pl.pallas_call(
        functools.partial(add_kernel, parts),
        grid=(width // tile,),
        out_shape=[jax.ShapeDtypeStruct((size, width), BF16)] * parts
        + [jax.ShapeDtypeStruct((rows, low), BF16)],
        in_specs=[
            fixed(rows, depth),
            pl.BlockSpec((tile, depth), lambda i: (i, 0)),
            fixed(depth, low),
            pl.BlockSpec((low, tile), lambda i: (0, i)),
            fixed(rows, low),
        ],
        out_specs=[pl.BlockSpec((size, tile), lambda i: (0, i))] * parts + [fixed(rows, low)],
        scratch_shapes=[pltpu.VMEM((rows, low), BF16)],
        compiler_params=BIG,
        cost_estimate=pl.CostEstimate(
            flops=2 * rows * width * depth, bytes_accessed=2 * weight.size, transcendentals=0
        ),
        name="add_product",
    )(a, weight, first, second, pick)


def back_kernel(parts, a, weight, u, first, *outs):
    result = mm_nt(a[...], flat(weight[...])) + mm_nt(u[...], first[...])
    size = result.shape[0] // parts
    for i in range(parts):
        outs[i][...] = result[i * size : (i + 1) * size].astype(BF16)


def back_product(a, group, weight, k_rows, u, first, parts):
    rows, depth = a.shape
    rows //= 2
    shards = weight.shape[0]
    width, low = first.shape
    per = max(1, 512 // k_rows)
    size = rows // parts
    return pl.pallas_call(
        functools.partial(back_kernel, parts),
        grid=(shards // per,),
        out_shape=[jax.ShapeDtypeStruct((size, width), BF16)] * parts,
        in_specs=[
            fixed(rows, depth, at=(group, 0)),
            pl.BlockSpec((per, k_rows, depth), lambda i: (i, 0, 0)),
            fixed(rows, low, at=(group, 0)),
            pl.BlockSpec((per * k_rows, low), lambda i: (i, 0)),
        ],
        out_specs=[pl.BlockSpec((size, per * k_rows), lambda i: (0, i))] * parts,
        compiler_params=BIG,
        cost_estimate=pl.CostEstimate(
            flops=2 * rows * width * depth, bytes_accessed=2 * width * depth, transcendentals=0
        ),
        name="back_product",
    )(a, weight, u, first)


def gate_up_kernel(h, first, pick, w_g, w_u, b_g, b_u, gate_out, up_out, act, latent_out, latent):
    low = pick.shape[1]

    @pl.when(pl.program_id(0) == 0)
    def _():
        both = mm(h[...], first[...])
        latent[:, :low] = (both[:, :low] * pick[...]).astype(BF16)
        latent[:, low:] = (both[:, low:] * pick[...]).astype(BF16)
        latent_out[...] = latent[...]

    gate = mm(h[...], w_g[...]) + mm(latent[:, :low], b_g[...])
    up = mm(h[...], w_u[...]) + mm(latent[:, low:], b_u[...])
    gate_out[...] = gate
    up_out[...] = up
    act[...] = (gate / (1.0 + jnp.exp(-gate)) * up).astype(BF16)


def gate_up_product(h, w_gu, a_gu, b_gu, pick, tile=512):
    rows, width = h.shape
    units, low = w_gu.shape[1] // 2, pick.shape[1]
    n = units // tile
    left = lambda depth: pl.BlockSpec((depth, tile), lambda i: (0, i))
    out = pl.BlockSpec((rows, tile), lambda i: (0, i))
    return pl.pallas_call(
        gate_up_kernel,
        grid=(n,),
        out_shape=[jax.ShapeDtypeStruct((rows, units), F32)] * 2
        + [
            jax.ShapeDtypeStruct((rows, units), BF16),
            jax.ShapeDtypeStruct((rows, 2 * low), BF16),
        ],
        in_specs=[
            fixed(rows, width),
            fixed(width, 2 * low),
            fixed(rows, low),
            left(width),
            pl.BlockSpec((width, tile), lambda i: (0, i + n)),
            left(low),
            pl.BlockSpec((low, tile), lambda i: (1, i)),
        ],
        out_specs=[out, out, out, fixed(rows, 2 * low)],
        scratch_shapes=[pltpu.VMEM((rows, 2 * low), BF16)],
        compiler_params=BIG,
        cost_estimate=pl.CostEstimate(
            flops=4 * rows * width * units, bytes_accessed=4 * width * units, transcendentals=0
        ),
        name="gate_up_product",
    )(h, a_gu, pick, w_gu, w_gu, b_gu, b_gu)


def ff_back_kernel(
    parts, steps, d_ff, b_down, pick, w_down, a_down, gate, up, w_g, w_u, b_g, b_u, a_gu, *refs
):
    outs, (d_gate_out, d_up_out, u_out, u_down_out, acc, u_g, u_u, u_down) = refs[:parts], refs[parts:]
    i = pl.program_id(0)

    @pl.when(i == 0)
    def _():
        u_down[...] = (mm_nt(d_ff[...], b_down[...]) * pick[...]).astype(BF16)
        u_down_out[...] = u_down[...]

    d_act = mm(d_ff[...], w_down[...]) + mm_nt(u_down[...], a_down[...])
    g = gate[...]
    sigmoid = 1.0 / (1.0 + jnp.exp(-g))
    silu = g * sigmoid
    d_gate = (d_act * up[...] * (sigmoid + silu * (1.0 - sigmoid))).astype(BF16)
    d_up = (d_act * silu).astype(BF16)
    d_gate_out[...] = d_gate
    d_up_out[...] = d_up
    part = mm_nt(d_gate, w_g[...]) + mm_nt(d_up, w_u[...])
    part_g, part_u = mm_nt(d_gate, b_g[...]), mm_nt(d_up, b_u[...])

    @pl.when(i == 0)
    def _():
        acc[...] = part
        u_g[...] = part_g
        u_u[...] = part_u

    @pl.when(i > 0)
    def _():
        acc[...] += part
        u_g[...] += part_g
        u_u[...] += part_u

    @pl.when(i == steps - 1)
    def _():
        low = pick.shape[1]
        last_g = (u_g[...] * pick[...]).astype(BF16)
        last_u = (u_u[...] * pick[...]).astype(BF16)
        u_out[:, :low] = last_g
        u_out[:, low:] = last_u
        size = acc.shape[0] // parts
        for p in range(parts):
            at = slice(p * size, (p + 1) * size)
            outs[p][...] = (
                acc[at, :]
                + mm_nt(last_g[at], a_gu[:, :low])
                + mm_nt(last_u[at], a_gu[:, low:])
            ).astype(BF16)


def ff_back(d_ff, b_down, pick, w_down, a_down, gate, up, w_gu, b_gu, a_gu, parts, tile=512):
    rows, width = d_ff.shape
    units, low = gate.shape[1], pick.shape[1]
    n = units // tile
    size = rows // parts
    column = lambda depth: pl.BlockSpec((depth, tile), lambda i: (0, i))
    return pl.pallas_call(
        functools.partial(ff_back_kernel, parts, n),
        grid=(n,),
        out_shape=[jax.ShapeDtypeStruct((size, width), BF16)] * parts
        + [jax.ShapeDtypeStruct((rows, units), BF16)] * 2
        + [
            jax.ShapeDtypeStruct((rows, 2 * low), BF16),
            jax.ShapeDtypeStruct((rows, low), BF16),
        ],
        in_specs=[
            fixed(rows, width),
            fixed(low, width),
            fixed(rows, low),
            column(width),
            pl.BlockSpec((tile, low), lambda i: (i, 0)),
            column(rows),
            column(rows),
            column(width),
            pl.BlockSpec((width, tile), lambda i: (0, i + n)),
            column(low),
            pl.BlockSpec((low, tile), lambda i: (1, i)),
            fixed(width, 2 * low),
        ],
        out_specs=[fixed(size, width)] * parts
        + [column(rows), column(rows), fixed(rows, 2 * low), fixed(rows, low)],
        scratch_shapes=[
            pltpu.VMEM((rows, width), F32),
            pltpu.VMEM((rows, low), F32),
            pltpu.VMEM((rows, low), F32),
            pltpu.VMEM((rows, low), BF16),
        ],
        compiler_params=BIG,
        cost_estimate=pl.CostEstimate(
            flops=6 * rows * width * units, bytes_accessed=6 * width * units, transcendentals=0
        ),
        name="ff_back",
    )(d_ff, b_down, pick, w_down, a_down, gate, up, w_gu, w_gu, b_gu, b_gu, a_gu)


def local(
    layer_input,
    cotangent,
    query_key_value_weight,
    output_weight,
    gate_up_weight,
    down_weight,
    input_first_factor,
    output_first_factor,
    down_first_factor,
    query_key_value_second,
    gate_up_second_factor,
    output_down_second_factor,
    norm_gain_table,
    sequence_adapter,
    block_sequence,
    block_position,
):
    tp, tp_rank = lax.axis_size("tp"), lax.axis_index("tp")
    seqs, seq_rank = lax.axis_size("seq"), lax.axis_index("seq")
    own_rows, width = layer_input.shape
    rows = own_rows * tp
    part = own_rows // 2
    my_blocks = rows // BLK
    cols = query_key_value_weight.shape[2]
    heads = cols // HEAD_DIM
    hidden_cols = gate_up_weight.shape[2]
    k_rows = query_key_value_weight.shape[1]
    slots_a = input_first_factor.shape[2]
    rank_cols = output_first_factor.shape[1]
    group = seqs // heads
    head_rank, group_rank = seq_rank // group, seq_rank % group
    n_seq = sequence_adapter.shape[0]
    groups = (0, 1)

    runs = row_runs(tp)
    piece_at = jnp.stack([2 * (tp_rank ^ mask) + which for mask, which in runs]).astype(jnp.int32)
    token = (piece_at[:, None] * part + jnp.arange(part, dtype=jnp.int32)[None, :]).reshape(-1)
    token_block, offset = token // BLK, token % BLK
    block_ids = seq_rank * my_blocks + jnp.arange(my_blocks, dtype=jnp.int32)
    place_blocks = block_position[block_ids]
    adapter_blocks = sequence_adapter[block_sequence[block_ids]]
    in_block = token_block[:, None] == jnp.arange(my_blocks, dtype=jnp.int32)[None, :]
    pick = lambda per_block: jnp.sum(jnp.where(in_block, per_block[None, :], 0), axis=1)
    select = (
        jnp.arange(slots_a, dtype=jnp.int32)[None, :] // ADAPTER_RANK
        == pick(adapter_blocks)[:, None]
    ).astype(F32) * 2.0
    half = rows // 2
    selects = [select[:half], select[half:]]
    start = jnp.where(place_blocks < PROMPT_BLOCKS, place_blocks, PROMPT_BLOCKS) * BLK
    position = pick(start) + offset
    frequency = THETA ** (-(jnp.arange(HEAD_DIM // 2, dtype=F32) * 2.0) / HEAD_DIM)
    angles = position.astype(F32)[:, None] * frequency[None, :]
    cosine, sine = jnp.cos(angles), jnp.sin(angles)
    cs = jnp.concatenate([cosine, cosine, -sine, sine], axis=1)

    a_part = k_rows // tp
    b_part = width // tp
    a_mine = lax.dynamic_slice_in_dim(input_first_factor, tp_rank * a_part, a_part, 1)
    b_mine = lax.dynamic_slice_in_dim(output_down_second_factor, tp_rank * b_part, b_part, 2)
    first = jnp.concatenate(
        [
            query_key_value_weight.transpose(1, 0, 2).reshape(k_rows, 3 * cols),
            query_key_value_second.transpose(1, 0, 2).reshape(rank_cols, 3 * cols),
            a_mine[:3].reshape(-1, 3 * cols),
        ],
        axis=0,
    )
    x_parts = [layer_input] + [
        lax.ppermute(layer_input, "tp", [(i, i ^ mask) for i in range(tp)]) for mask in range(1, tp)
    ]
    x = jnp.concatenate(
        [x_parts[mask][which * part : (which + 1) * part] for mask, which in runs], axis=0
    )
    pick3 = jnp.tile(select, (1, 3))
    first = lax.all_gather(first, "seq", axis=0)
    pieces = [
        output_weight.T,
        output_first_factor.T,
        b_mine.reshape(-1, cols),
        a_mine[3:].reshape(-1, cols),
        down_first_factor.T.reshape(-1, cols),
        gate_up_second_factor.reshape(-1, cols),
    ]
    packed = jnp.concatenate(pieces, axis=0)
    first, x, cs, pick3, packed, w_gu, w_down = lax.optimization_barrier(
        (
            first,
            x,
            cs,
            pick3,
            packed,
            gate_up_weight.transpose(1, 0, 2).reshape(k_rows, 2 * hidden_cols),
            down_weight.T,
        )
    )
    packed = lax.all_gather(packed, "seq", axis=0)
    w_gu = lax.all_gather(w_gu, "seq", axis=0, tiled=True)
    w_down = lax.all_gather(w_down, "seq", axis=0, tiled=True)

    a_qkv = first[:, k_rows + rank_cols :].reshape(seqs, 3, a_part, slots_a)
    a_qkv = a_qkv.transpose(0, 2, 1, 3).reshape(seqs, a_part, 3 * slots_a)
    a_parts = [a_qkv] + [
        lax.ppermute(a_qkv, "tp", [(i, i ^ mask) for i in range(tp)]) for mask in range(1, tp)
    ]
    a_qkv = jnp.zeros((seqs, tp, a_part, 3 * slots_a), BF16)
    for mask, value in enumerate(a_parts):
        a_qkv = lax.dynamic_update_slice(a_qkv, value[:, None], (0, tp_rank ^ mask, 0, 0))
    a_qkv = a_qkv.reshape(width, 3 * slots_a)
    b_qkv = first[:, k_rows : k_rows + rank_cols].reshape(slots_a, 3 * cols)
    owner = (
        ((head_rank - jnp.arange(heads)) % heads)[None, :] * group
        + ((group_rank + jnp.arange(group)) % group)[:, None]
    ).reshape(-1)
    held = (owner[:, None] * my_blocks + jnp.arange(my_blocks)[None, :]).reshape(-1)
    held_seq = block_sequence[held].astype(jnp.int32)
    held_place = block_position[held].astype(jnp.int32)
    prompt_count = n_seq * PROMPT_BLOCKS
    wanted = jnp.arange(prompt_count, dtype=jnp.int32)
    code = jnp.where(held_place < PROMPT_BLOCKS, held_seq * PROMPT_BLOCKS + held_place, -1)
    prompt_at = jnp.sum(
        jnp.where(
            code[None, :] == wanted[:, None], jnp.arange(held.shape[0], dtype=jnp.int32)[None, :], 0
        ),
        axis=1,
    ).astype(jnp.int32)
    own_blocks = heads * my_blocks
    tables = (held_seq[:own_blocks], held_place[:own_blocks], prompt_at)
    head_order = ((head_rank + jnp.arange(heads)) % heads).astype(jnp.int32)

    def head_shift(value, by):
        if by == 0:
            return value
        return lax.ppermute(
            value,
            "seq",
            [
                (h * group + j, ((h + by) % heads) * group + j)
                for h in range(heads)
                for j in range(group)
            ],
        )

    def group_shift(value, by):
        return lax.ppermute(
            value,
            "seq",
            [
                (h * group + j, h * group + (j + by) % group)
                for h in range(heads)
                for j in range(group)
            ],
        )

    own = lambda value, i: value[i * part : (i + 1) * part].astype(F32)
    gain = lax.dynamic_slice_in_dim(norm_gain_table[:2], tp_rank * cols, cols, 1)
    latents = (mm(x, a_qkv) * pick3).astype(BF16)
    z, squares = qkv_product(
        x, latents, first, b_qkv, k_rows, cols
    )
    squares = sum_rows(squares[:2].reshape(2, rows), tp)
    inv = lax.rsqrt(squares / width + EPS)
    inv, packed = lax.optimization_barrier((inv, packed))
    split, at = [], 0
    for piece in pieces:
        split.append(packed[:, at : at + piece.shape[0]])
        at += piece.shape[0]
    w_o = split[0].reshape(width, cols)
    a_o = split[1].reshape(slots_a, cols).T
    mine = jnp.concatenate(split[2:4], axis=1)
    shared = jnp.zeros((tp, *mine.shape), BF16)
    for mask in range(tp):
        got = lax.ppermute(mine, "tp", [(i, i ^ mask) for i in range(tp)]) if mask else mine
        shared = lax.dynamic_update_slice(shared, got[None], (tp_rank ^ mask, 0, 0, 0))
    b_size = split[2].shape[1]
    b_od = (
        shared[:, :, :b_size]
        .reshape(tp, seqs, 2, rank_cols, b_part)
        .transpose(2, 1, 3, 0, 4)
        .reshape(2, slots_a, width)
    )
    a_gu = (
        shared[:, :, b_size:]
        .reshape(tp, seqs, 2, a_part, slots_a)
        .transpose(1, 0, 3, 2, 4)
        .reshape(width, 2 * slots_a)
    )
    a_down = split[4].reshape(slots_a, hidden_cols).T
    b_gu = (
        split[5]
        .reshape(seqs, 2, rank_cols, hidden_cols)
        .transpose(1, 0, 2, 3)
        .reshape(2 * slots_a, hidden_cols)
    )
    spread = spread_heads(head_order, piece_at, z, inv.T, cs, gain, heads)
    near = [head_shift(spread[k], k) for k in range(heads)]
    far = [group_shift(near[k][1:], -j) for j in range(1, group) for k in range(heads)]
    far, w_o, a_o, b_od, a_gu, a_down, b_gu = lax.optimization_barrier(
        (far, w_o, a_o, b_od, a_gu, a_down, b_gu)
    )
    attended = attend(tables, near, far, prompt_count)
    heads_out = collect_heads(
        head_order, piece_at, [head_shift(attended[k], -k) for k in range(heads)]
    )

    def norm_back(values_in, inv, scaled):
        return inv * scaled - values_in * inv**3 * jnp.mean(scaled * values_in, axis=1, keepdims=True)

    def inverse_norm(values_in):
        return lax.rsqrt(jnp.mean(values_in * values_in, axis=1, keepdims=True) + EPS)

    *far_part, o_latent1 = add_product(heads_out[1], w_o, a_o, b_od[0], selects[1], 2)
    near_part, o_latent0 = add_product(heads_out[0], w_o, a_o, b_od[0], selects[0], 1)
    attn_out = scatter_groups(near_part, far_part, tp)
    scale_o = [inverse_norm(value) for value in attn_out]
    hidden = [
        own(layer_input, i) + attn_out[i] * scale_o[i] * norm_gain_table[2] for i in groups
    ]
    h_low = gather_groups([value.astype(BF16) for value in hidden], tp)

    gates, ups, acts, gu_latents = zip(
        *[gate_up_product(h_low[g], w_gu, a_gu, b_gu, selects[g]) for g in groups]
    )
    acts, w_down = lax.optimization_barrier((acts, w_down))
    *far_part, d_latent1 = add_product(acts[1], w_down, a_down, b_od[1], selects[1], 2)
    near_part, d_latent0 = add_product(acts[0], w_down, a_down, b_od[1], selects[0], 1)
    ff_out = scatter_groups(near_part, far_part, tp)
    scale_f = [inverse_norm(value) for value in ff_out]
    output = jnp.concatenate(
        [hidden[i] + ff_out[i] * scale_f[i] * norm_gain_table[3] for i in groups], axis=0
    )

    d_ffs = gather_groups(
        [
            norm_back(ff_out[i], scale_f[i], own(cotangent, i) * norm_gain_table[3]).astype(BF16)
            for i in groups
        ],
        tp,
    )
    backs = [
        ff_back(
            d_ffs[g], b_od[1], selects[g], w_down, a_down, gates[g], ups[g], w_gu, b_gu, a_gu, 1 + g
        )
        for g in groups
    ]
    summed = scatter_groups(backs[0][0], backs[1][:2], tp)
    d_gates, d_ups, u_gus, u_downs = zip(*[back[-4:] for back in backs])
    d_hidden = [own(cotangent, i) + summed[i] for i in groups]
    d_attn = [
        norm_back(attn_out[i], scale_o[i], d_hidden[i] * norm_gain_table[2]).astype(BF16)
        for i in groups
    ]
    d_latents = (d_latent0, d_latent1)
    d_rows = gather_groups(d_attn, tp)
    o_latents = (o_latent0, o_latent1)
    u_os, grads = [], []
    for g in groups:
        u_os.append((mm_nt(d_rows[g], b_od[0]) * selects[g]).astype(BF16))
        d_heads = (mm(d_rows[g], w_o) + mm_nt(u_os[g], a_o)).astype(BF16)
        grads.append(
            [
                head_shift(
                    lax.dynamic_slice_in_dim(d_heads, head_order[k] * HEAD_DIM, HEAD_DIM, 1), k
                )
                for k in range(heads)
            ]
        )
    grads = [grads[g][k] for k in range(heads) for g in groups]
    results = list(attend_back(tables, piece_at, near, far, grads, prompt_count))
    dqs = [head_shift(results[k], -k) for k in range(heads)]
    d_kv = results[heads].reshape(2, heads, rows, HEAD_DIM)
    others = [
        group_shift(results[heads + j], j).reshape(2, heads, rows, HEAD_DIM) for j in range(1, group)
    ]
    dkvs = []
    for k in range(heads):
        total = d_kv[:, k].astype(F32)
        for other in others:
            total = total + other[:, k].astype(F32)
        dkvs.append(head_shift(total.astype(BF16), -k))
    dkvs[1], u_os, o_latents, u_downs, d_latents, u_gus, gu_latents = lax.optimization_barrier(
        (dkvs[1], u_os, o_latents, u_downs, d_latents, u_gus, gu_latents)
    )
    both_groups = lambda f: f(0) + f(1)
    grad_a_down = both_groups(lambda g: mm_tn(u_downs[g], acts[g]))
    grad_b_down = both_groups(lambda g: mm_tn(d_latents[g], d_ffs[g]))
    grad_a_gu = both_groups(lambda g: mm_tn(h_low[g], u_gus[g]))
    grad_b_gate = both_groups(lambda g: mm_tn(gu_latents[g][:, :slots_a], d_gates[g]))
    grad_b_up = both_groups(lambda g: mm_tn(gu_latents[g][:, slots_a:], d_ups[g]))
    lane = 2 * slots_a
    shards = lambda value: value.astype(BF16).reshape(seqs, -1, lane)
    grad_a_o = both_groups(lambda g: mm_tn(u_os[g], heads_out[g]))
    grad_b_o = both_groups(lambda g: mm_tn(o_latents[g], d_rows[g]))
    early = jnp.concatenate(
        [
            shards(grad_a_gu),
            shards(grad_b_down),
            shards(grad_b_o),
            shards(grad_a_down),
            shards(grad_b_gate),
            shards(grad_b_up),
            shards(grad_a_o),
        ],
        axis=1,
    )
    dqs, dkvs, early = lax.optimization_barrier((dqs, dkvs, early))
    early = lax.psum_scatter(early, "seq", scatter_dimension=0, tiled=False)
    scaled, parts = unturn_heads(head_order, piece_at, dqs, dkvs, z, cs, gain)
    parts = sum_rows(parts.T, tp) / width
    coef = jnp.concatenate([inv, inv**3 * parts], axis=0)
    dz, us = norm_back_heads(head_order, piece_at, dkvs, scaled, z, coef.T, b_qkv, select)
    grad_a_qkv = mm_tn(x, us)
    grad_b_qkv = mm_tn(latents, dz)
    lane3 = 3 * slots_a
    grad_b_qkv = jnp.concatenate(
        [
            grad_b_qkv[i * slots_a : (i + 1) * slots_a, i * cols : (i + 1) * cols]
            for i in range(3)
        ],
        axis=1,
    )
    late = jnp.concatenate(
        [
            grad_a_qkv.astype(BF16).reshape(seqs, k_rows, lane3),
            grad_b_qkv.astype(BF16).reshape(seqs, -1, lane3),
        ],
        axis=1,
    )
    dz, late = lax.optimization_barrier((dz, late))
    far_part = list(back_product(dz, 1, first, k_rows, us, a_qkv, 2))
    far_part[0], dz = lax.optimization_barrier((far_part[0], dz))
    (near_part,) = back_product(dz, 0, first, k_rows, us, a_qkv, 1)

    near_part, early = lax.optimization_barrier((near_part, early))

    def sum_tp(value):
        total = value.astype(F32)
        for mask in range(1, tp):
            got = lax.ppermute(value, "tp", [(i, i ^ mask) for i in range(tp)])
            total = total + got.astype(F32)
        return total

    down_size = rank_cols * width // lane
    both = sum_tp(early[: k_rows + 2 * down_size])
    late = lax.psum_scatter(late, "seq", scatter_dimension=0, tiled=False)
    summed = scatter_groups(near_part, far_part, tp)
    summed, late = lax.optimization_barrier((summed, late))
    input_grad = jnp.concatenate([d_hidden[i] + summed[i] for i in groups], axis=0)
    grad_a_qkv = sum_tp(late[:k_rows])
    grad_a_gu = both[:k_rows]
    grad_b_down = both[k_rows : k_rows + down_size].reshape(rank_cols, width)
    grad_b_o = both[k_rows + down_size :].reshape(rank_cols, width)
    a_size = rank_cols * hidden_cols // lane
    rest = early[k_rows + 2 * down_size :].astype(F32)
    grad_a_down = rest[:a_size].reshape(rank_cols, hidden_cols).T
    grad_b_gu = rest[a_size : 3 * a_size].reshape(2, rank_cols, hidden_cols)
    grad_a_o = rest[3 * a_size :].reshape(rank_cols, cols).T
    grad_b_qkv = late[k_rows:].astype(F32).reshape(rank_cols, 3, cols).transpose(1, 0, 2)
    grad_a_in = jnp.stack(
        [grad_a_qkv[:, i * slots_a : (i + 1) * slots_a] for i in range(3)]
        + [grad_a_gu[:, i * slots_a : (i + 1) * slots_a] for i in range(2)]
    )
    grad_b_out = jnp.stack([grad_b_o, grad_b_down])
    return (output, input_grad, grad_a_in, grad_a_o, grad_a_down, grad_b_qkv, grad_b_gu, grad_b_out)


def solution(mesh):
    return jax.shard_map(
        local,
        mesh=mesh,
        in_specs=(
            P(("seq", "tp"), None),
            P(("seq", "tp"), None),
            P(None, "seq", "tp"),
            P("tp", "seq"),
            P(None, "seq", "tp"),
            P("tp", "seq"),
            P(None, "seq", None),
            P("tp", "seq"),
            P("tp", "seq"),
            P(None, "seq", "tp"),
            P(None, "seq", "tp"),
            P(None, "seq", None),
            P(),
            P(),
            P(),
            P(),
        ),
        out_specs=(
            P(("seq", "tp"), None),
            P(("seq", "tp"), None),
            P(None, "seq", None),
            P("tp", "seq"),
            P("tp", "seq"),
            P(None, "seq", "tp"),
            P(None, "seq", "tp"),
            P(None, "seq", None),
        ),
        check_vma=False,
    )
```

```python
import functools

import jax
import jax.numpy as jnp
from jax import lax
from jax.experimental import pallas as pl
from jax.experimental.pallas import tpu as pltpu
from jax.sharding import PartitionSpec as P

HEAD_DIM = 128
ADAPTER_RANK = 16
BLK = 128
PROMPT_BLOCKS = 8
EPS = 1e-06
THETA = 500000.0
NEG = -1e30
LOG2E = 1.4426950408889634
F32 = jnp.float32
BF16 = jnp.bfloat16


def mm(a, b):
    return jnp.dot(a, b, preferred_element_type=F32)


def mm_nt(a, b):
    return lax.dot_general(a, b, (((1,), (1,)), ((), ())), preferred_element_type=F32)


def mm_tn(a, b):
    return lax.dot_general(a, b, (((0,), (0,)), ((), ())), preferred_element_type=F32)


def bits_of(count):
    n = count.bit_length() - 1
    assert 1 << n == count
    return n


def flip(value, axis, count, bit):
    return lax.ppermute(value, axis, [(i, i ^ (1 << bit)) for i in range(count)])


def part_orders(count):
    order = list(range(bits_of(count)))
    return (order, order[::-1])


def group_masks(count):
    groups = ([], [])
    for part, order in enumerate(part_orders(count)):
        for j in range(count):
            mask = sum(1 << bit for i, bit in enumerate(order) if (j >> i) & 1)
            groups[j >= count // 2].append((mask, part))
    return groups


def row_runs(count):
    return [run for masks in group_masks(count) for run in masks]


def gather_groups(parts, count, beside=None):
    near, far = [], []
    for value, order in zip(parts, part_orders(count)):
        for bit in order[:-1]:
            value = jnp.concatenate([value, flip(value, "tp", count, bit)], axis=0)
        near.append(value)
    if beside is not None:
        near[1], beside = lax.optimization_barrier((near[1], beside))
    for value, order in zip(near, part_orders(count)):
        far.append(flip(value, "tp", count, order[-1]))
    if beside is not None:
        return jnp.concatenate(near, axis=0), jnp.concatenate(far, axis=0), beside
    return jnp.concatenate(near, axis=0), jnp.concatenate(far, axis=0)


def scatter_groups(near, far, count):
    return scatter_rest(scatter_first(near, far, count), count)


def scatter_first(near, far, count):
    out = []
    size = near.shape[0] // 2
    for i, order in enumerate(part_orders(count)):
        got = flip(far[i], "tp", count, order[-1])
        out.append(near[i * size : (i + 1) * size].astype(F32) + got.astype(F32))
    return out


def scatter_rest(totals, count):
    out = []
    for total, order in zip(totals, part_orders(count)):
        for bit in order[-2::-1]:
            half = total.shape[0] // 2
            got = flip(total[half:].astype(BF16), "tp", count, bit)
            total = total[:half] + got.astype(F32)
        out.append(total)
    return out


def sum_rows(value, count):
    runs = row_runs(count)
    value = value.reshape(value.shape[0], len(runs), -1)
    total = value
    for mask in range(1, count):
        got = lax.ppermute(value, "tp", [(i, i ^ mask) for i in range(count)])
        order = [runs.index((other ^ mask, which)) for other, which in runs]
        total = total + jnp.concatenate([got[:, j : j + 1] for j in order], axis=1)
    return total.reshape(value.shape[0], -1)


def copy_all(pairs, sem):
    copies = [pltpu.make_async_copy(src, dst, sem.at[i]) for i, (src, dst) in enumerate(pairs)]
    for copy in copies:
        copy.start()
    for copy in copies:
        copy.wait()


def gather_prompt(prompt_at, source, target, count):
    def step(i, carry):
        start = pl.multiple_of(prompt_at[i] * BLK, BLK)
        target[pl.ds(pl.multiple_of(i * BLK, BLK), BLK), :] = source[pl.ds(start, BLK), :]
        return carry

    lax.fori_loop(0, count, step, 0)


def masked_scores(keys, own_keys, queries, place, scale):
    prompt = mm_nt(keys, queries) * scale
    block = lax.broadcasted_iota(jnp.int32, prompt.shape, 0) // BLK
    prompt = jnp.where(block < place, prompt, NEG)
    own = mm_nt(own_keys, queries) * scale
    causal = lax.broadcasted_iota(jnp.int32, own.shape, 0) <= lax.broadcasted_iota(
        jnp.int32, own.shape, 1
    )
    own = jnp.where(causal, own, NEG)
    top = jnp.maximum(jnp.max(prompt, axis=0, keepdims=True), jnp.max(own, axis=0, keepdims=True))
    prompt = jnp.exp2(prompt - top)
    own = jnp.exp2(own - top)
    total = jnp.sum(prompt, axis=0, keepdims=True) + jnp.sum(own, axis=0, keepdims=True)
    return prompt, own, 1.0 / total


def load_plan(slots, group, rows, refs, q_buf, k_buf, v_buf):
    plan = []
    for i in range(slots):
        plan.append((refs[i].at[0], q_buf.at[pl.ds(i * rows, rows)]))
    for i in range(slots * group):
        at = pl.ds(i * rows, rows)
        skip = int(i < slots)
        plan += [(refs[i].at[skip], k_buf.at[at]), (refs[i].at[skip + 1], v_buf.at[at])]
    return plan


def attend_kernel(slots, group, rows, prompt_count, q_seq, q_place, prompt_at, *refs):
    n_in = slots * group
    outs = refs[n_in : n_in + slots]
    q_buf, k_buf, v_buf, kp, vp, o_buf, sem = refs[n_in + slots :]
    copy_all(load_plan(slots, group, rows, refs, q_buf, k_buf, v_buf), sem)
    gather_prompt(prompt_at, k_buf, kp, prompt_count)
    gather_prompt(prompt_at, v_buf, vp, prompt_count)
    scale = HEAD_DIM ** (-0.5) * LOG2E
    span = PROMPT_BLOCKS * BLK

    def block(i):
        at = pl.ds(pl.multiple_of(i * BLK, BLK), BLK)
        of_seq = pl.ds(pl.multiple_of(q_seq[i] * span, span), span)
        prompt, own, inverse = masked_scores(
            kp[of_seq, :], k_buf[at, :], q_buf[at, :], q_place[i], scale
        )
        result = mm_tn(vp[of_seq, :], prompt.astype(BF16)) + mm_tn(v_buf[at, :], own.astype(BF16))
        return at, (result * inverse).T.astype(BF16)

    blocks = slots * rows // BLK
    pair = 2 if blocks % 2 == 0 else 1

    def step(i, carry):
        for at, result in [block(i * pair + j) for j in range(pair)]:
            o_buf[at, :] = result
        return carry

    lax.fori_loop(0, blocks // pair, step, 0)
    copy_all([(o_buf.at[pl.ds(i * rows, rows)], outs[i]) for i in range(slots)], sem)


def attend_back_kernel(
    slots, group, rows, pieces, prompt_count, q_seq, q_place, prompt_at, piece_at, *refs
):
    n_in = slots * group
    n_grad = slots * 2
    grads = refs[n_in : n_in + n_grad]
    outs = refs[n_in + n_grad : n_in + n_grad + slots]
    near_out = refs[n_in + n_grad + slots]
    rest = refs[n_in + n_grad + slots + 1 :]
    far_outs, rest = rest[: group - 1], rest[group - 1 :]
    q_buf, k_buf, v_buf, do_buf, kp, vp, dkp, dvp, dq_buf, dkv_buf, sem = rest
    plan = load_plan(slots, group, rows, refs, q_buf, k_buf, v_buf)
    size = rows // pieces
    for i in range(slots):
        for p in range(pieces):
            half, at = divmod(p, pieces // 2)
            to = pl.multiple_of(i * rows + piece_at[p] * size, 16)
            plan.append(
                (grads[i * 2 + half].at[pl.ds(at * size, size)], do_buf.at[pl.ds(to, size)])
            )
    copy_all(plan, sem)
    gather_prompt(prompt_at, k_buf, kp, prompt_count)
    gather_prompt(prompt_at, v_buf, vp, prompt_count)
    dkp[...] = jnp.zeros_like(dkp)
    dvp[...] = jnp.zeros_like(dvp)
    scale = HEAD_DIM ** (-0.5)
    span = PROMPT_BLOCKS * BLK
    own_rows = slots * rows
    zeros = jnp.zeros((BLK, HEAD_DIM), BF16)

    def rows_of(i):
        return pl.ds(pl.multiple_of(i * BLK, BLK), BLK)

    def clear(i, carry):
        for j in range(1, group):
            dkv_buf[j, 0, rows_of(i), :] = zeros
            dkv_buf[j, 1, rows_of(i), :] = zeros
        return carry

    lax.fori_loop(0, own_rows // BLK, clear, 0)

    def block(i):
        at = rows_of(i)
        seq, place = q_seq[i], q_place[i]
        of_seq = pl.ds(pl.multiple_of(seq * span, span), span)
        queries, grad = q_buf[at, :], do_buf[at, :]
        prompt, own, inverse = masked_scores(
            kp[of_seq, :], k_buf[at, :], queries, place, scale * LOG2E
        )
        prompt, own = prompt * inverse, own * inverse
        d_prompt = mm_nt(vp[of_seq, :], grad)
        d_own = mm_nt(v_buf[at, :], grad)
        delta = jnp.sum(prompt * d_prompt, axis=0, keepdims=True) + jnp.sum(
            own * d_own, axis=0, keepdims=True
        )
        ds_prompt = (prompt * (d_prompt - delta)).astype(BF16)
        ds_own = (own * (d_own - delta)).astype(BF16)
        dq = mm_tn(ds_prompt, kp[of_seq, :]) + mm_tn(ds_own, k_buf[at, :])
        return (
            at,
            of_seq,
            (dq * scale).astype(BF16),
            mm(prompt.astype(BF16), grad),
            mm(ds_prompt, queries) * scale,
            (mm(ds_own, queries) * scale).astype(BF16),
            mm(own.astype(BF16), grad).astype(BF16),
        )

    blocks = own_rows // BLK
    pair = 2 if blocks % 2 == 0 else 1

    def step(i, carry):
        for at, of_seq, dq, dv_prompt, dk_prompt, dk_own, dv_own in [
            block(i * pair + j) for j in range(pair)
        ]:
            dq_buf[at, :] = dq
            dvp[of_seq, :] += dv_prompt
            dkp[of_seq, :] += dk_prompt
            dkv_buf[0, 0, at, :] = dk_own
            dkv_buf[0, 1, at, :] = dv_own
        return carry

    lax.fori_loop(0, blocks // pair, step, 0)

    def spread(i, carry):
        place = prompt_at[i]
        j, to = place // blocks, rows_of(place % blocks)
        dkv_buf[j, 0, to, :] = (dkv_buf[j, 0, to, :].astype(F32) + dkp[rows_of(i), :]).astype(BF16)
        dkv_buf[j, 1, to, :] = (dkv_buf[j, 1, to, :].astype(F32) + dvp[rows_of(i), :]).astype(BF16)
        return carry

    lax.fori_loop(0, prompt_count, spread, 0)
    plan = [(dq_buf.at[pl.ds(i * rows, rows)], outs[i]) for i in range(slots)]
    plan.append((dkv_buf.at[0], near_out))
    plan += [(dkv_buf.at[j], far_outs[j - 1]) for j in range(1, group)]
    copy_all(plan, sem)


ANY = pl.BlockSpec(memory_space=pl.ANY)


def attend(tables, near, far, prompt_count):
    slots = len(near)
    rows = near[0].shape[1]
    group = 1 + len(far) // slots
    own, every = slots * rows, slots * group * rows
    pairs = own * (PROMPT_BLOCKS + 1) * BLK
    wide = lambda count, kind=BF16: pltpu.VMEM((count, HEAD_DIM), kind)
    return pl.pallas_call(
        functools.partial(attend_kernel, slots, group, rows, prompt_count),
        out_shape=[jax.ShapeDtypeStruct((rows, HEAD_DIM), BF16)] * slots,
        grid_spec=pltpu.PrefetchScalarGridSpec(
            num_scalar_prefetch=3,
            in_specs=[ANY] * (slots * group),
            out_specs=[ANY] * slots,
            scratch_shapes=[
                wide(own),
                wide(every),
                wide(every),
                wide(prompt_count * BLK),
                wide(prompt_count * BLK),
                wide(own),
                pltpu.SemaphoreType.DMA((slots + 2 * slots * group,)),
            ],
        ),
        cost_estimate=pl.CostEstimate(
            flops=4 * pairs * HEAD_DIM, bytes_accessed=6 * every * HEAD_DIM, transcendentals=pairs
        ),
        name="attend",
    )(*tables, *near, *far)


def attend_back(tables, piece_at, near, far, grads, prompt_count):
    pieces = piece_at.shape[0]
    slots = len(near)
    rows = near[0].shape[1]
    group = 1 + len(far) // slots
    own, every = slots * rows, slots * group * rows
    pairs = own * (PROMPT_BLOCKS + 1) * BLK
    wide = lambda count, kind=BF16: pltpu.VMEM((count, HEAD_DIM), kind)
    return pl.pallas_call(
        functools.partial(attend_back_kernel, slots, group, rows, pieces, prompt_count),
        out_shape=[jax.ShapeDtypeStruct((rows, HEAD_DIM), BF16)] * slots
        + [jax.ShapeDtypeStruct((2, own, HEAD_DIM), BF16)] * group,
        grid_spec=pltpu.PrefetchScalarGridSpec(
            num_scalar_prefetch=4,
            in_specs=[ANY] * (slots * group + 2 * slots),
            out_specs=[ANY] * (slots + group),
            scratch_shapes=[
                wide(own),
                wide(every),
                wide(every),
                wide(own),
                wide(prompt_count * BLK),
                wide(prompt_count * BLK),
                wide(prompt_count * BLK, F32),
                wide(prompt_count * BLK, F32),
                wide(own),
                pltpu.VMEM((group, 2, own, HEAD_DIM), BF16),
                pltpu.SemaphoreType.DMA((slots + 2 * slots * group + slots * pieces,)),
            ],
        ),
        cost_estimate=pl.CostEstimate(
            flops=10 * pairs * HEAD_DIM, bytes_accessed=12 * every * HEAD_DIM, transcendentals=pairs
        ),
        name="attend_back",
    )(*tables, piece_at, *near, *far, *grads)


def turn(values, cosine, sine):
    return values * cosine + pltpu.roll(values, HEAD_DIM // 2, 1) * sine


def lanes(head, base=0):
    return pl.ds(pl.multiple_of(base + head * HEAD_DIM, HEAD_DIM), HEAD_DIM)


def here(size, width):
    return pl.BlockSpec((size, width), lambda p, order, piece_at: (p, 0))


def there(size, at=None, count=1):
    if at is None:
        return pl.BlockSpec((size, HEAD_DIM), lambda p, order, piece_at: (piece_at[p], 0))
    return pl.BlockSpec((count, size, HEAD_DIM), lambda p, order, piece_at: (at, piece_at[p], 0))


def all_of(value):
    return pl.BlockSpec(value.shape, lambda p, order, piece_at: (0, 0))


def piece_rows(index, size):
    return pl.ds(pl.multiple_of(index * size, 16), size)


def spread_kernel(slots, order, piece_at, z, inv, cs, gain, *outs):
    cols = slots * HEAD_DIM
    cosine, sine = cs[:, :HEAD_DIM], cs[:, HEAD_DIM:]
    for which in range(2):
        factor = inv[:, which : which + 1]
        for k in range(slots):
            head = order[k]
            scaled = z[:, lanes(head, which * cols)] * factor
            scaled = scaled * gain[which : which + 1, lanes(head)]
            outs[k][which, :, :] = turn(scaled, cosine, sine).astype(BF16)
    for k in range(slots):
        outs[k][2, :, :] = z[:, lanes(order[k], 2 * cols)].astype(BF16)


WHOLE = pl.BlockSpec(memory_space=pltpu.VMEM)
BIG = pltpu.CompilerParams(vmem_limit_bytes=56 * 1024 * 1024)


def spread_heads(order, piece_at, z, inv, cs, gain, slots):
    rows = z.shape[0]
    pieces = piece_at.shape[0]
    size = rows // pieces
    return pl.pallas_call(
        functools.partial(spread_kernel, slots),
        out_shape=[jax.ShapeDtypeStruct((3, rows, HEAD_DIM), BF16)] * slots,
        grid_spec=pltpu.PrefetchScalarGridSpec(
            num_scalar_prefetch=2,
            grid=(pieces,),
            in_specs=[
                here(size, z.shape[1]),
                here(size, inv.shape[1]),
                here(size, cs.shape[1]),
                all_of(gain),
            ],
            out_specs=[there(size, 0, 3)] * slots,
        ),
        compiler_params=BIG,
        name="spread_heads",
    )(order, piece_at, z, inv, cs, gain)


def collect_kernel(slots, pieces, order, piece_at, *refs):
    outs = refs[slots:]
    size = refs[0].shape[0] // pieces
    for p in range(pieces):
        half, at = divmod(p, pieces // 2)
        for k in range(slots):
            outs[half][pl.ds(at * size, size), lanes(order[k])] = refs[k][
                piece_rows(piece_at[p], size), :
            ]


def collect_heads(order, piece_at, parts):
    slots = len(parts)
    rows = parts[0].shape[0]
    return pl.pallas_call(
        functools.partial(collect_kernel, slots, piece_at.shape[0]),
        out_shape=[jax.ShapeDtypeStruct((rows // 2, slots * HEAD_DIM), BF16)] * 2,
        grid_spec=pltpu.PrefetchScalarGridSpec(
            num_scalar_prefetch=2, in_specs=[WHOLE] * slots, out_specs=[WHOLE] * 2
        ),
        name="collect_heads",
    )(order, piece_at, *parts)


def unturn_kernel(slots, order, piece_at, *refs):
    dqs, dkvs, rest = refs[:slots], refs[slots : 2 * slots], refs[2 * slots :]
    z, cs, gain, scaled_out, part_out = rest
    cols = slots * HEAD_DIM
    cosine, sine = cs[:, :HEAD_DIM], cs[:, HEAD_DIM:]
    for which in range(2):
        total = jnp.zeros((z.shape[0], HEAD_DIM), F32)
        for k in range(slots):
            head = order[k]
            grad = dqs[k][...] if which == 0 else dkvs[k][0, :, :]
            grad = turn(grad.astype(F32), cosine, -sine) * gain[which : which + 1, lanes(head)]
            scaled_out[:, lanes(head, which * cols)] = grad
            total = total + grad * z[:, lanes(head, which * cols)]
        part_out[:, which : which + 1] = jnp.sum(total, axis=1, keepdims=True)


def unturn_heads(order, piece_at, dqs, dkvs, z, cs, gain):
    slots = len(dqs)
    rows = z.shape[0]
    cols = slots * HEAD_DIM
    pieces = piece_at.shape[0]
    size = rows // pieces
    return pl.pallas_call(
        functools.partial(unturn_kernel, slots),
        out_shape=[
            jax.ShapeDtypeStruct((rows, 2 * cols), F32),
            jax.ShapeDtypeStruct((rows, 2), F32),
        ],
        grid_spec=pltpu.PrefetchScalarGridSpec(
            num_scalar_prefetch=2,
            grid=(pieces,),
            in_specs=[there(size)] * slots
            + [there(size, 0)] * slots
            + [here(size, 2 * cols), here(size, cs.shape[1]), all_of(gain)],
            out_specs=[here(size, 2 * cols), here(size, 2)],
        ),
        compiler_params=BIG,
        name="unturn_heads",
    )(order, piece_at, *dqs, *dkvs, z, cs, gain)


def norm_back_kernel(slots, order, piece_at, *refs):
    dkvs, (scaled, z, coef, second, pick, out, latent_out) = refs[:slots], refs[slots:]
    cols = slots * HEAD_DIM
    low = second.shape[0]
    for which in range(2):
        to = slice(which * cols, (which + 1) * cols)
        out[:, to] = (
            scaled[:, to] * coef[:, which : which + 1] - z[:, to] * coef[:, 2 + which : 3 + which]
        ).astype(BF16)
    for k in range(slots):
        out[:, lanes(order[k], 2 * cols)] = dkvs[k][0, :, :]
    for which in range(3):
        to = slice(which * cols, (which + 1) * cols)
        at = slice(which * low, (which + 1) * low)
        latent_out[:, at] = (mm_nt(out[:, to], second[:, to]) * pick[...]).astype(BF16)


def norm_back_heads(order, piece_at, dkvs, scaled, z, coef, second, pick):
    slots = len(dkvs)
    rows = z.shape[0]
    cols = slots * HEAD_DIM
    low = second.shape[0]
    pieces = piece_at.shape[0]
    size = rows // pieces
    return pl.pallas_call(
        functools.partial(norm_back_kernel, slots),
        out_shape=[
            jax.ShapeDtypeStruct((rows, 3 * cols), BF16),
            jax.ShapeDtypeStruct((rows, 3 * low), BF16),
        ],
        grid_spec=pltpu.PrefetchScalarGridSpec(
            num_scalar_prefetch=2,
            grid=(pieces,),
            in_specs=[there(size, 1)] * slots
            + [
                here(size, 2 * cols),
                here(size, 2 * cols),
                here(size, 4),
                all_of(second),
                here(size, low),
            ],
            out_specs=[here(size, 3 * cols), here(size, 3 * low)],
        ),
        compiler_params=BIG,
        name="norm_back_heads",
    )(order, piece_at, *dkvs, scaled, z, coef, second, pick)


def fixed(*shape, at=None):
    place = at or (0,) * len(shape)
    return pl.BlockSpec(shape, lambda i: place)


def flat(value):
    return value.reshape(-1, value.shape[-1])


def qkv_kernel(x, latent, weight, second, z, squares):
    i = pl.program_id(0)
    result = mm(x[...], flat(weight[...])) + mm(latent[...], flat(second[...]))
    z[...] = result
    squares[0, :, :] = jnp.sum(result * result, axis=1, keepdims=True)


def qkv_product(x, latents, first, second, k_rows, cols):
    rows, width = x.shape
    shards, _, total = first.shape
    low = latents.shape[1] // 3
    return pl.pallas_call(
        qkv_kernel,
        grid=(3,),
        out_shape=[
            jax.ShapeDtypeStruct((rows, total), F32),
            jax.ShapeDtypeStruct((3, rows, 1), F32),
        ],
        in_specs=[
            fixed(rows, width),
            pl.BlockSpec((rows, low), lambda i: (0, i)),
            pl.BlockSpec((shards, k_rows, cols), lambda i: (0, 0, i)),
            pl.BlockSpec((low, cols), lambda i: (0, i)),
        ],
        out_specs=[
            pl.BlockSpec((rows, cols), lambda i: (0, i)),
            pl.BlockSpec((1, rows, 1), lambda i: (i, 0, 0)),
        ],
        compiler_params=BIG,
        cost_estimate=pl.CostEstimate(
            flops=2 * rows * width * total, bytes_accessed=2 * first.size, transcendentals=0
        ),
        name="qkv_product",
    )(x, latents, first, second)


def add_kernel(parts, a, weight, first, second, pick, *refs):
    outs, (latent_out, latent) = refs[:parts], refs[parts:]

    @pl.when(pl.program_id(0) == 0)
    def _():
        latent[...] = (mm(a[...], first[...]) * pick[...]).astype(BF16)
        latent_out[...] = latent[...]

    result = mm_nt(a[...], weight[...]) + mm(latent[...], second[...])
    size = result.shape[0] // parts
    for i in range(parts):
        outs[i][...] = result[i * size : (i + 1) * size].astype(BF16)


def add_product(a, weight, first, second, pick, parts, tile=512):
    rows, depth = a.shape
    width, low = weight.shape[0], first.shape[1]
    size = rows // parts
    return pl.pallas_call(
        functools.partial(add_kernel, parts),
        grid=(width // tile,),
        out_shape=[jax.ShapeDtypeStruct((size, width), BF16)] * parts
        + [jax.ShapeDtypeStruct((rows, low), BF16)],
        in_specs=[
            fixed(rows, depth),
            pl.BlockSpec((tile, depth), lambda i: (i, 0)),
            fixed(depth, low),
            pl.BlockSpec((low, tile), lambda i: (0, i)),
            fixed(rows, low),
        ],
        out_specs=[pl.BlockSpec((size, tile), lambda i: (0, i))] * parts + [fixed(rows, low)],
        scratch_shapes=[pltpu.VMEM((rows, low), BF16)],
        compiler_params=BIG,
        cost_estimate=pl.CostEstimate(
            flops=2 * rows * width * depth, bytes_accessed=2 * weight.size, transcendentals=0
        ),
        name="add_product",
    )(a, weight, first, second, pick)


def back_kernel(parts, a, weight, u, first, *outs):
    result = mm_nt(a[...], flat(weight[...])) + mm_nt(u[...], first[...])
    size = result.shape[0] // parts
    for i in range(parts):
        outs[i][...] = result[i * size : (i + 1) * size].astype(BF16)


def back_product(a, group, weight, k_rows, u, first, parts):
    rows, depth = a.shape
    rows //= 2
    shards = weight.shape[0]
    width, low = first.shape
    per = max(1, 512 // k_rows)
    size = rows // parts
    return pl.pallas_call(
        functools.partial(back_kernel, parts),
        grid=(shards // per,),
        out_shape=[jax.ShapeDtypeStruct((size, width), BF16)] * parts,
        in_specs=[
            fixed(rows, depth, at=(group, 0)),
            pl.BlockSpec((per, k_rows, depth), lambda i: (i, 0, 0)),
            fixed(rows, low, at=(group, 0)),
            pl.BlockSpec((per * k_rows, low), lambda i: (i, 0)),
        ],
        out_specs=[pl.BlockSpec((size, per * k_rows), lambda i: (0, i))] * parts,
        compiler_params=BIG,
        cost_estimate=pl.CostEstimate(
            flops=2 * rows * width * depth, bytes_accessed=2 * width * depth, transcendentals=0
        ),
        name="back_product",
    )(a, weight, u, first)


def gate_up_kernel(h, first, pick, w_g, w_u, b_g, b_u, gate_out, up_out, act, latent_out, latent):
    low = pick.shape[1]

    @pl.when(pl.program_id(0) == 0)
    def _():
        both = mm(h[...], first[...])
        latent[:, :low] = (both[:, :low] * pick[...]).astype(BF16)
        latent[:, low:] = (both[:, low:] * pick[...]).astype(BF16)
        latent_out[...] = latent[...]

    gate = mm(h[...], w_g[...]) + mm(latent[:, :low], b_g[...])
    up = mm(h[...], w_u[...]) + mm(latent[:, low:], b_u[...])
    gate_out[...] = gate
    up_out[...] = up
    act[...] = (gate / (1.0 + jnp.exp(-gate)) * up).astype(BF16)


def gate_up_product(h, w_gu, a_gu, b_gu, pick, tile=512):
    rows, width = h.shape
    units, low = w_gu.shape[1] // 2, pick.shape[1]
    n = units // tile
    left = lambda depth: pl.BlockSpec((depth, tile), lambda i: (0, i))
    out = pl.BlockSpec((rows, tile), lambda i: (0, i))
    return pl.pallas_call(
        gate_up_kernel,
        grid=(n,),
        out_shape=[jax.ShapeDtypeStruct((rows, units), F32)] * 2
        + [
            jax.ShapeDtypeStruct((rows, units), BF16),
            jax.ShapeDtypeStruct((rows, 2 * low), BF16),
        ],
        in_specs=[
            fixed(rows, width),
            fixed(width, 2 * low),
            fixed(rows, low),
            left(width),
            pl.BlockSpec((width, tile), lambda i: (0, i + n)),
            left(low),
            pl.BlockSpec((low, tile), lambda i: (1, i)),
        ],
        out_specs=[out, out, out, fixed(rows, 2 * low)],
        scratch_shapes=[pltpu.VMEM((rows, 2 * low), BF16)],
        compiler_params=BIG,
        cost_estimate=pl.CostEstimate(
            flops=4 * rows * width * units, bytes_accessed=4 * width * units, transcendentals=0
        ),
        name="gate_up_product",
    )(h, a_gu, pick, w_gu, w_gu, b_gu, b_gu)


def ff_back_kernel(
    parts, steps, d_ff, b_down, pick, w_down, a_down, gate, up, w_g, w_u, b_g, b_u, a_gu, *refs
):
    outs, (d_gate_out, d_up_out, u_out, u_down_out, acc, u_g, u_u, u_down) = refs[:parts], refs[parts:]
    i = pl.program_id(0)

    @pl.when(i == 0)
    def _():
        u_down[...] = (mm_nt(d_ff[...], b_down[...]) * pick[...]).astype(BF16)
        u_down_out[...] = u_down[...]

    d_act = mm(d_ff[...], w_down[...]) + mm_nt(u_down[...], a_down[...])
    g = gate[...]
    sigmoid = 1.0 / (1.0 + jnp.exp(-g))
    silu = g * sigmoid
    d_gate = (d_act * up[...] * (sigmoid + silu * (1.0 - sigmoid))).astype(BF16)
    d_up = (d_act * silu).astype(BF16)
    d_gate_out[...] = d_gate
    d_up_out[...] = d_up
    part = mm_nt(d_gate, w_g[...]) + mm_nt(d_up, w_u[...])
    part_g, part_u = mm_nt(d_gate, b_g[...]), mm_nt(d_up, b_u[...])

    @pl.when(i == 0)
    def _():
        acc[...] = part
        u_g[...] = part_g
        u_u[...] = part_u

    @pl.when(i > 0)
    def _():
        acc[...] += part
        u_g[...] += part_g
        u_u[...] += part_u

    @pl.when(i == steps - 1)
    def _():
        low = pick.shape[1]
        last_g = (u_g[...] * pick[...]).astype(BF16)
        last_u = (u_u[...] * pick[...]).astype(BF16)
        u_out[:, :low] = last_g
        u_out[:, low:] = last_u
        size = acc.shape[0] // parts
        for p in range(parts):
            at = slice(p * size, (p + 1) * size)
            outs[p][...] = (
                acc[at, :]
                + mm_nt(last_g[at], a_gu[:, :low])
                + mm_nt(last_u[at], a_gu[:, low:])
            ).astype(BF16)


def ff_back(d_ff, b_down, pick, w_down, a_down, gate, up, w_gu, b_gu, a_gu, parts, tile=512):
    rows, width = d_ff.shape
    units, low = gate.shape[1], pick.shape[1]
    n = units // tile
    size = rows // parts
    column = lambda depth: pl.BlockSpec((depth, tile), lambda i: (0, i))
    return pl.pallas_call(
        functools.partial(ff_back_kernel, parts, n),
        grid=(n,),
        out_shape=[jax.ShapeDtypeStruct((size, width), BF16)] * parts
        + [jax.ShapeDtypeStruct((rows, units), BF16)] * 2
        + [
            jax.ShapeDtypeStruct((rows, 2 * low), BF16),
            jax.ShapeDtypeStruct((rows, low), BF16),
        ],
        in_specs=[
            fixed(rows, width),
            fixed(low, width),
            fixed(rows, low),
            column(width),
            pl.BlockSpec((tile, low), lambda i: (i, 0)),
            column(rows),
            column(rows),
            column(width),
            pl.BlockSpec((width, tile), lambda i: (0, i + n)),
            column(low),
            pl.BlockSpec((low, tile), lambda i: (1, i)),
            fixed(width, 2 * low),
        ],
        out_specs=[fixed(size, width)] * parts
        + [column(rows), column(rows), fixed(rows, 2 * low), fixed(rows, low)],
        scratch_shapes=[
            pltpu.VMEM((rows, width), F32),
            pltpu.VMEM((rows, low), F32),
            pltpu.VMEM((rows, low), F32),
            pltpu.VMEM((rows, low), BF16),
        ],
        compiler_params=BIG,
        cost_estimate=pl.CostEstimate(
            flops=6 * rows * width * units, bytes_accessed=6 * width * units, transcendentals=0
        ),
        name="ff_back",
    )(d_ff, b_down, pick, w_down, a_down, gate, up, w_gu, w_gu, b_gu, b_gu, a_gu)


def local(
    layer_input,
    cotangent,
    query_key_value_weight,
    output_weight,
    gate_up_weight,
    down_weight,
    input_first_factor,
    output_first_factor,
    down_first_factor,
    query_key_value_second,
    gate_up_second_factor,
    output_down_second_factor,
    norm_gain_table,
    sequence_adapter,
    block_sequence,
    block_position,
):
    tp, tp_rank = lax.axis_size("tp"), lax.axis_index("tp")
    seqs, seq_rank = lax.axis_size("seq"), lax.axis_index("seq")
    own_rows, width = layer_input.shape
    rows = own_rows * tp
    part = own_rows // 2
    my_blocks = rows // BLK
    cols = query_key_value_weight.shape[2]
    heads = cols // HEAD_DIM
    hidden_cols = gate_up_weight.shape[2]
    k_rows = query_key_value_weight.shape[1]
    slots_a = input_first_factor.shape[2]
    rank_cols = output_first_factor.shape[1]
    group = seqs // heads
    head_rank, group_rank = seq_rank // group, seq_rank % group
    n_seq = sequence_adapter.shape[0]
    groups = (0, 1)

    runs = row_runs(tp)
    piece_at = jnp.stack([2 * (tp_rank ^ mask) + which for mask, which in runs]).astype(jnp.int32)
    token = (piece_at[:, None] * part + jnp.arange(part, dtype=jnp.int32)[None, :]).reshape(-1)
    token_block, offset = token // BLK, token % BLK
    block_ids = seq_rank * my_blocks + jnp.arange(my_blocks, dtype=jnp.int32)
    place_blocks = block_position[block_ids]
    adapter_blocks = sequence_adapter[block_sequence[block_ids]]
    in_block = token_block[:, None] == jnp.arange(my_blocks, dtype=jnp.int32)[None, :]
    pick = lambda per_block: jnp.sum(jnp.where(in_block, per_block[None, :], 0), axis=1)
    select = (
        jnp.arange(slots_a, dtype=jnp.int32)[None, :] // ADAPTER_RANK
        == pick(adapter_blocks)[:, None]
    ).astype(F32) * 2.0
    half = rows // 2
    selects = [select[:half], select[half:]]
    start = jnp.where(place_blocks < PROMPT_BLOCKS, place_blocks, PROMPT_BLOCKS) * BLK
    position = pick(start) + offset
    frequency = THETA ** (-(jnp.arange(HEAD_DIM // 2, dtype=F32) * 2.0) / HEAD_DIM)
    angles = position.astype(F32)[:, None] * frequency[None, :]
    cosine, sine = jnp.cos(angles), jnp.sin(angles)
    cs = jnp.concatenate([cosine, cosine, -sine, sine], axis=1)

    a_part = k_rows // tp
    b_part = width // tp
    a_mine = lax.dynamic_slice_in_dim(input_first_factor, tp_rank * a_part, a_part, 1)
    b_mine = lax.dynamic_slice_in_dim(output_down_second_factor, tp_rank * b_part, b_part, 2)
    first = jnp.concatenate(
        [
            query_key_value_weight.transpose(1, 0, 2).reshape(k_rows, 3 * cols),
            query_key_value_second.transpose(1, 0, 2).reshape(rank_cols, 3 * cols),
            a_mine[:3].reshape(-1, 3 * cols),
        ],
        axis=0,
    )
    x_parts = [layer_input] + [
        lax.ppermute(layer_input, "tp", [(i, i ^ mask) for i in range(tp)]) for mask in range(1, tp)
    ]
    x = jnp.concatenate(
        [x_parts[mask][which * part : (which + 1) * part] for mask, which in runs], axis=0
    )
    pick3 = jnp.tile(select, (1, 3))
    first = lax.all_gather(first, "seq", axis=0)
    pieces = [
        output_weight.T,
        output_first_factor.T,
        b_mine.reshape(-1, cols),
        a_mine[3:].reshape(-1, cols),
        down_first_factor.T.reshape(-1, cols),
        gate_up_second_factor.reshape(-1, cols),
    ]
    packed = jnp.concatenate(pieces, axis=0)
    first, x, cs, pick3, packed, w_gu, w_down = lax.optimization_barrier(
        (
            first,
            x,
            cs,
            pick3,
            packed,
            gate_up_weight.transpose(1, 0, 2).reshape(k_rows, 2 * hidden_cols),
            down_weight.T,
        )
    )
    packed = lax.all_gather(packed, "seq", axis=0)
    w_gu = lax.all_gather(w_gu, "seq", axis=0, tiled=True)
    w_down = lax.all_gather(w_down, "seq", axis=0, tiled=True)

    a_qkv = first[:, k_rows + rank_cols :].reshape(seqs, 3, a_part, slots_a)
    a_qkv = a_qkv.transpose(0, 2, 1, 3).reshape(seqs, a_part, 3 * slots_a)
    a_parts = [a_qkv] + [
        lax.ppermute(a_qkv, "tp", [(i, i ^ mask) for i in range(tp)]) for mask in range(1, tp)
    ]
    a_qkv = jnp.zeros((seqs, tp, a_part, 3 * slots_a), BF16)
    for mask, value in enumerate(a_parts):
        a_qkv = lax.dynamic_update_slice(a_qkv, value[:, None], (0, tp_rank ^ mask, 0, 0))
    a_qkv = a_qkv.reshape(width, 3 * slots_a)
    b_qkv = first[:, k_rows : k_rows + rank_cols].reshape(slots_a, 3 * cols)
    owner = (
        ((head_rank - jnp.arange(heads)) % heads)[None, :] * group
        + ((group_rank + jnp.arange(group)) % group)[:, None]
    ).reshape(-1)
    held = (owner[:, None] * my_blocks + jnp.arange(my_blocks)[None, :]).reshape(-1)
    held_seq = block_sequence[held].astype(jnp.int32)
    held_place = block_position[held].astype(jnp.int32)
    prompt_count = n_seq * PROMPT_BLOCKS
    wanted = jnp.arange(prompt_count, dtype=jnp.int32)
    code = jnp.where(held_place < PROMPT_BLOCKS, held_seq * PROMPT_BLOCKS + held_place, -1)
    prompt_at = jnp.sum(
        jnp.where(
            code[None, :] == wanted[:, None], jnp.arange(held.shape[0], dtype=jnp.int32)[None, :], 0
        ),
        axis=1,
    ).astype(jnp.int32)
    own_blocks = heads * my_blocks
    tables = (held_seq[:own_blocks], held_place[:own_blocks], prompt_at)
    head_order = ((head_rank + jnp.arange(heads)) % heads).astype(jnp.int32)

    def head_shift(value, by):
        if by == 0:
            return value
        return lax.ppermute(
            value,
            "seq",
            [
                (h * group + j, ((h + by) % heads) * group + j)
                for h in range(heads)
                for j in range(group)
            ],
        )

    def group_shift(value, by):
        return lax.ppermute(
            value,
            "seq",
            [
                (h * group + j, h * group + (j + by) % group)
                for h in range(heads)
                for j in range(group)
            ],
        )

    own = lambda value, i: value[i * part : (i + 1) * part].astype(F32)
    gain = lax.dynamic_slice_in_dim(norm_gain_table[:2], tp_rank * cols, cols, 1)
    latents = (mm(x, a_qkv) * pick3).astype(BF16)
    z, squares = qkv_product(
        x, latents, first, b_qkv, k_rows, cols
    )
    squares = sum_rows(squares[:2].reshape(2, rows), tp)
    inv = lax.rsqrt(squares / width + EPS)
    inv, packed = lax.optimization_barrier((inv, packed))
    split, at = [], 0
    for piece in pieces:
        split.append(packed[:, at : at + piece.shape[0]])
        at += piece.shape[0]
    w_o = split[0].reshape(width, cols)
    a_o = split[1].reshape(slots_a, cols).T
    mine = jnp.concatenate(split[2:4], axis=1)
    shared = jnp.zeros((tp, *mine.shape), BF16)
    for mask in range(tp):
        got = lax.ppermute(mine, "tp", [(i, i ^ mask) for i in range(tp)]) if mask else mine
        shared = lax.dynamic_update_slice(shared, got[None], (tp_rank ^ mask, 0, 0, 0))
    b_size = split[2].shape[1]
    b_od = (
        shared[:, :, :b_size]
        .reshape(tp, seqs, 2, rank_cols, b_part)
        .transpose(2, 1, 3, 0, 4)
        .reshape(2, slots_a, width)
    )
    a_gu = (
        shared[:, :, b_size:]
        .reshape(tp, seqs, 2, a_part, slots_a)
        .transpose(1, 0, 3, 2, 4)
        .reshape(width, 2 * slots_a)
    )
    a_down = split[4].reshape(slots_a, hidden_cols).T
    b_gu = (
        split[5]
        .reshape(seqs, 2, rank_cols, hidden_cols)
        .transpose(1, 0, 2, 3)
        .reshape(2 * slots_a, hidden_cols)
    )
    spread = spread_heads(head_order, piece_at, z, inv.T, cs, gain, heads)
    near = [head_shift(spread[k], k) for k in range(heads)]
    far = [group_shift(near[k][1:], -j) for j in range(1, group) for k in range(heads)]
    far, w_o, a_o, b_od, a_gu, a_down, b_gu = lax.optimization_barrier(
        (far, w_o, a_o, b_od, a_gu, a_down, b_gu)
    )
    attended = attend(tables, near, far, prompt_count)
    heads_out = collect_heads(
        head_order, piece_at, [head_shift(attended[k], -k) for k in range(heads)]
    )

    def norm_back(values_in, inv, scaled):
        return inv * scaled - values_in * inv**3 * jnp.mean(scaled * values_in, axis=1, keepdims=True)

    def inverse_norm(values_in):
        return lax.rsqrt(jnp.mean(values_in * values_in, axis=1, keepdims=True) + EPS)

    *far_part, o_latent1 = add_product(heads_out[1], w_o, a_o, b_od[0], selects[1], 2)
    near_part, o_latent0 = add_product(heads_out[0], w_o, a_o, b_od[0], selects[0], 1)
    attn_out = scatter_groups(near_part, far_part, tp)
    scale_o = [inverse_norm(value) for value in attn_out]
    hidden = [
        own(layer_input, i) + attn_out[i] * scale_o[i] * norm_gain_table[2] for i in groups
    ]
    h_low = gather_groups([value.astype(BF16) for value in hidden], tp)

    gates, ups, acts, gu_latents = zip(
        *[gate_up_product(h_low[g], w_gu, a_gu, b_gu, selects[g]) for g in groups]
    )
    acts, w_down = lax.optimization_barrier((acts, w_down))
    *far_part, d_latent1 = add_product(acts[1], w_down, a_down, b_od[1], selects[1], 2)
    near_part, d_latent0 = add_product(acts[0], w_down, a_down, b_od[1], selects[0], 1)
    ff_out = scatter_groups(near_part, far_part, tp)
    scale_f = [inverse_norm(value) for value in ff_out]
    output = jnp.concatenate(
        [hidden[i] + ff_out[i] * scale_f[i] * norm_gain_table[3] for i in groups], axis=0
    )

    d_ffs = gather_groups(
        [
            norm_back(ff_out[i], scale_f[i], own(cotangent, i) * norm_gain_table[3]).astype(BF16)
            for i in groups
        ],
        tp,
    )
    backs = [
        ff_back(
            d_ffs[g], b_od[1], selects[g], w_down, a_down, gates[g], ups[g], w_gu, b_gu, a_gu, 1 + g
        )
        for g in groups
    ]
    summed = scatter_groups(backs[0][0], backs[1][:2], tp)
    d_gates, d_ups, u_gus, u_downs = zip(*[back[-4:] for back in backs])
    d_hidden = [own(cotangent, i) + summed[i] for i in groups]
    d_attn = [
        norm_back(attn_out[i], scale_o[i], d_hidden[i] * norm_gain_table[2]).astype(BF16)
        for i in groups
    ]
    d_latents = (d_latent0, d_latent1)
    d_rows = gather_groups(d_attn, tp)
    o_latents = (o_latent0, o_latent1)
    u_os, grads = [], []
    for g in groups:
        u_os.append((mm_nt(d_rows[g], b_od[0]) * selects[g]).astype(BF16))
        d_heads = (mm(d_rows[g], w_o) + mm_nt(u_os[g], a_o)).astype(BF16)
        grads.append(
            [
                head_shift(
                    lax.dynamic_slice_in_dim(d_heads, head_order[k] * HEAD_DIM, HEAD_DIM, 1), k
                )
                for k in range(heads)
            ]
        )
    grads = [grads[g][k] for k in range(heads) for g in groups]
    results = list(attend_back(tables, piece_at, near, far, grads, prompt_count))
    dqs = [head_shift(results[k], -k) for k in range(heads)]
    d_kv = results[heads].reshape(2, heads, rows, HEAD_DIM)
    others = [
        group_shift(results[heads + j], j).reshape(2, heads, rows, HEAD_DIM) for j in range(1, group)
    ]
    dkvs = []
    for k in range(heads):
        total = d_kv[:, k].astype(F32)
        for other in others:
            total = total + other[:, k].astype(F32)
        dkvs.append(head_shift(total.astype(BF16), -k))
    dkvs[1], u_os, o_latents, u_downs, d_latents, u_gus, gu_latents = lax.optimization_barrier(
        (dkvs[1], u_os, o_latents, u_downs, d_latents, u_gus, gu_latents)
    )
    both_groups = lambda f: f(0) + f(1)
    grad_a_down = both_groups(lambda g: mm_tn(u_downs[g], acts[g]))
    grad_b_down = both_groups(lambda g: mm_tn(d_latents[g], d_ffs[g]))
    grad_a_gu = both_groups(lambda g: mm_tn(h_low[g], u_gus[g]))
    grad_b_gate = both_groups(lambda g: mm_tn(gu_latents[g][:, :slots_a], d_gates[g]))
    grad_b_up = both_groups(lambda g: mm_tn(gu_latents[g][:, slots_a:], d_ups[g]))
    lane = 2 * slots_a
    shards = lambda value: value.astype(BF16).reshape(seqs, -1, lane)
    grad_a_o = both_groups(lambda g: mm_tn(u_os[g], heads_out[g]))
    grad_b_o = both_groups(lambda g: mm_tn(o_latents[g], d_rows[g]))
    early = jnp.concatenate(
        [
            shards(grad_a_gu),
            shards(grad_b_down),
            shards(grad_b_o),
            shards(grad_a_down),
            shards(grad_b_gate),
            shards(grad_b_up),
            shards(grad_a_o),
        ],
        axis=1,
    )
    dqs, dkvs, early = lax.optimization_barrier((dqs, dkvs, early))
    early = lax.psum_scatter(early, "seq", scatter_dimension=0, tiled=False)
    scaled, parts = unturn_heads(head_order, piece_at, dqs, dkvs, z, cs, gain)
    parts = sum_rows(parts.T, tp) / width
    coef = jnp.concatenate([inv, inv**3 * parts], axis=0)
    dz, us = norm_back_heads(head_order, piece_at, dkvs, scaled, z, coef.T, b_qkv, select)
    grad_a_qkv = mm_tn(x, us)
    grad_b_qkv = mm_tn(latents, dz)
    lane3 = 3 * slots_a
    grad_b_qkv = jnp.concatenate(
        [
            grad_b_qkv[i * slots_a : (i + 1) * slots_a, i * cols : (i + 1) * cols]
            for i in range(3)
        ],
        axis=1,
    )
    late = jnp.concatenate(
        [
            grad_a_qkv.astype(BF16).reshape(seqs, k_rows, lane3),
            grad_b_qkv.astype(BF16).reshape(seqs, -1, lane3),
        ],
        axis=1,
    )
    dz, late = lax.optimization_barrier((dz, late))
    far_part = list(back_product(dz, 1, first, k_rows, us, a_qkv, 2))
    far_part[0], dz = lax.optimization_barrier((far_part[0], dz))
    (near_part,) = back_product(dz, 0, first, k_rows, us, a_qkv, 1)

    near_part, early = lax.optimization_barrier((near_part, early))

    def sum_tp(value):
        total = value.astype(F32)
        for mask in range(1, tp):
            got = lax.ppermute(value, "tp", [(i, i ^ mask) for i in range(tp)])
            total = total + got.astype(F32)
        return total

    down_size = rank_cols * width // lane
    both = sum_tp(early[: k_rows + 2 * down_size])
    late = lax.psum_scatter(late, "seq", scatter_dimension=0, tiled=False)
    summed = scatter_groups(near_part, far_part, tp)
    summed, late, early, both = lax.optimization_barrier((summed, late, early, both))
    input_grad = jnp.concatenate([d_hidden[i] + summed[i] for i in groups], axis=0)
    grad_a_qkv = sum_tp(late[:k_rows])
    grad_a_gu = both[:k_rows]
    grad_b_down = both[k_rows : k_rows + down_size].reshape(rank_cols, width)
    grad_b_o = both[k_rows + down_size :].reshape(rank_cols, width)
    a_size = rank_cols * hidden_cols // lane
    rest = early[k_rows + 2 * down_size :].astype(F32)
    grad_a_down = rest[:a_size].reshape(rank_cols, hidden_cols).T
    grad_b_gu = rest[a_size : 3 * a_size].reshape(2, rank_cols, hidden_cols)
    grad_a_o = rest[3 * a_size :].reshape(rank_cols, cols).T
    grad_b_qkv = late[k_rows:].astype(F32).reshape(rank_cols, 3, cols).transpose(1, 0, 2)
    grad_a_in = jnp.stack(
        [grad_a_qkv[:, i * slots_a : (i + 1) * slots_a] for i in range(3)]
        + [grad_a_gu[:, i * slots_a : (i + 1) * slots_a] for i in range(2)]
    )
    grad_b_out = jnp.stack([grad_b_o, grad_b_down])
    return (output, input_grad, grad_a_in, grad_a_o, grad_a_down, grad_b_qkv, grad_b_gu, grad_b_out)


def solution(mesh):
    return jax.shard_map(
        local,
        mesh=mesh,
        in_specs=(
            P(("seq", "tp"), None),
            P(("seq", "tp"), None),
            P(None, "seq", "tp"),
            P("tp", "seq"),
            P(None, "seq", "tp"),
            P("tp", "seq"),
            P(None, "seq", None),
            P("tp", "seq"),
            P("tp", "seq"),
            P(None, "seq", "tp"),
            P(None, "seq", "tp"),
            P(None, "seq", None),
            P(),
            P(),
            P(),
            P(),
        ),
        out_specs=(
            P(("seq", "tp"), None),
            P(("seq", "tp"), None),
            P(None, "seq", None),
            P("tp", "seq"),
            P("tp", "seq"),
            P(None, "seq", "tp"),
            P(None, "seq", "tp"),
            P(None, "seq", None),
        ),
        check_vma=False,
    )
```
